32 devices in a mesh: rows: 8 (over y, x, core), heads: 4 (over z).
Axes of the slice: x: 2, y: 2, z: 4, core: 2. Of those that a mesh axis runs over, the one named last changes fastest.
Arguments:
- inputs: bfloat16 [8192, 2048], P('rows'), may hold values from -6 to 6
- cotangent: bfloat16 [8192, 2048], P('rows'), may hold values from -6 to 6
- lengths: int32 [8], P('rows'), may hold values from 256 to 1024, as said below
- gain_attn: bfloat16 [2048], replicated, may hold values from 0.5 to 1.5
- gain_mlp: bfloat16 [2048], replicated, may hold values from 0.5 to 1.5
- w_query: bfloat16 [2048, 2048], P(None, 'heads'), may hold values from -0.125 to 0.125
- w_key: bfloat16 [2048, 2048], P(None, 'heads'), may hold values from -0.125 to 0.125
- w_value: bfloat16 [2048, 2048], P(None, 'heads'), may hold values from -0.125 to 0.125
- w_out: bfloat16 [2048, 2048], P('heads'), may hold values from -0.125 to 0.125
- w_gate: bfloat16 [2048, 5632], P(None, 'heads'), may hold values from -0.125 to 0.125
- w_up: bfloat16 [2048, 5632], P(None, 'heads'), may hold values from -0.125 to 0.125
- w_down: bfloat16 [5632, 2048], P('heads'), may hold values from -0.078125 to 0.078125
- qkv_left: float32 [3, 2048, 16], replicated, may hold values from -0.125 to 0.125
- qkv_right: float32 [3, 16, 2048], P(None, None, 'heads'), may hold values from -0.375 to 0.375
- qkv_mags: float32 [3, 2048], P(None, 'heads'), may hold values from 0.8 to 1.6
- mlp_left: float32 [2, 2048, 16], replicated, may hold values from -0.125 to 0.125
- mlp_right: float32 [2, 16, 5632], P(None, None, 'heads'), may hold values from -0.375 to 0.375
- mlp_mags: float32 [2, 5632], P(None, 'heads'), may hold values from 0.8 to 1.6
- out_left: float32 [2048, 16], P('heads'), may hold values from -0.125 to 0.125
- down_left: float32 [5632, 16], P('heads'), may hold values from -0.078125 to 0.078125
- exit_right: float32 [2, 16, 2048], replicated, may hold values from -0.375 to 0.375
- out_mags: float32 [2048], replicated, may hold values from 3 to 9
- down_mags: float32 [2048], replicated, may hold values from 0.8 to 1.6
Outputs:
- outputs: bfloat16 [8192, 2048], P(('rows', 'heads'))
- input_grad: float32 [8192, 2048], P(('rows', 'heads'))
- grad_qkv_left: float32 [3, 2048, 16], replicated
- grad_qkv_right: float32 [3, 16, 2048], P(None, None, 'heads')
- grad_qkv_mags: float32 [3, 2048], P(None, 'heads')
- grad_mlp_left: float32 [2, 2048, 16], replicated
- grad_mlp_right: float32 [2, 16, 5632], P(None, None, 'heads')
- grad_mlp_mags: float32 [2, 5632], P(None, 'heads')
- grad_out_left: float32 [2048, 16], P('heads')
- grad_down_left: float32 [5632, 16], P('heads')
- grad_exit_right: float32 [2, 16, 2048], replicated
- grad_out_mags: float32 [2048], replicated
- grad_down_mags: float32 [2048], replicated
- norm_stats: float32 [2, 21504], replicated
The draws below stay inside these ranges and needn't reach their ends.
Inputs may be any that keep to these rules, and one draw needn't show every extreme that they name: Sequence i has its first lengths[i] tokens real and the rest padding; some sequence has no padding.
All inputs are finite; a program needn't handle non-finite values.
Results may differ from the reference program's by a relative error of at most 0.028.
Values may be sent and summed in bfloat16 or wider, within the bound.
A program may use at most 320 MiB of HBM per device.

```python
import math
import jax
import jax.numpy as jnp
from jax import lax

D = 2048
H = 16
HEAD_DIM = 128
FF = 5632
RANK = 16
LEN = 1024
SEQS = 8
TOKENS = 8192
N_HEADS = 4


def draw_lengths(key, part):
    first, second = jax.random.split(jax.random.fold_in(key, 7))
    drawn = jax.random.randint(first, (SEQS,), LEN // 4, LEN + 1, dtype=jnp.int32)
    chosen = jax.random.randint(second, (), 0, SEQS, dtype=jnp.int32)
    return jnp.where(jnp.arange(SEQS, dtype=jnp.int32) == chosen, LEN, drawn).astype(jnp.int32)


def shard_levels(own_key, dims, shards, least, high):
    loudness, own = 1.0, jax.random.fold_in(own_key, 6)
    for axis_at, blocks in shards:
        heights = jnp.exp(jax.random.uniform(jax.random.fold_in(own, axis_at), (blocks,), jnp.float32, least / len(shards), high / len(shards)))
        loudness = loudness * jnp.repeat(heights, dims[axis_at] // blocks).reshape([-1 if axis == axis_at else 1 for axis in range(len(dims))])
    return loudness


def centred(key, shape, deviation, reach, shards=(), kind=jnp.bfloat16):
    level = shard_levels(key, shape, shards, -0.22, 0.18) if shards else 1.0
    array = jax.random.normal(key, shape, jnp.float32) * deviation * level
    return jnp.minimum(jnp.maximum(array, -reach), reach).astype(kind)


def setup_inputs(seed: int = 0) -> dict:
    seeds = jax.random.split(jax.random.key(seed), 24)
    inputs = centred(seeds[0], (TOKENS, D), 1.0, 6.0, ((0, 8),))
    cotangent = centred(seeds[1], (TOKENS, D), 1.0, 6.0, ((0, 8),))
    lengths = draw_lengths(jax.random.fold_in(seeds[23], 71), 0)
    gain_attn = jnp.clip(1.0 + 0.1 * jax.random.normal(seeds[3], (D,), jnp.float32), 0.5, 1.5).astype(jnp.bfloat16)
    gain_mlp = jnp.clip(1.0 + 0.1 * jax.random.normal(seeds[4], (D,), jnp.float32), 0.5, 1.5).astype(jnp.bfloat16)
    w_query = centred(seeds[5], (D, H * HEAD_DIM), D ** -0.5, 0.125, ((1, 4),))
    w_key = centred(seeds[6], (D, H * HEAD_DIM), D ** -0.5, 0.125, ((1, 4),))
    w_value = centred(seeds[7], (D, H * HEAD_DIM), D ** -0.5, 0.125, ((1, 4),))
    w_out = centred(seeds[8], (H * HEAD_DIM, D), (H * HEAD_DIM) ** -0.5, 0.125, ((0, 4),))
    w_gate = centred(seeds[9], (D, FF), D ** -0.5, 0.125, ((1, 4),))
    w_up = centred(seeds[10], (D, FF), D ** -0.5, 0.125, ((1, 4),))
    w_down = centred(seeds[11], (FF, D), FF ** -0.5, 0.078125, ((0, 4),))
    qkv_left = centred(seeds[12], (3, D, RANK), D ** -0.5, 0.125, (), jnp.float32)
    qkv_right = centred(seeds[13], (3, RANK, H * HEAD_DIM), 256 ** -0.5, 0.375, ((2, 4),), jnp.float32)
    qkv_mags = jnp.clip(0.8 + 0.8 * jax.random.uniform(seeds[14], (3, H * HEAD_DIM), jnp.float32) ** shard_levels(seeds[14], (3, H * HEAD_DIM), ((1, 4),), -0.2, 0.2), 0.8, 1.6)
    mlp_left = centred(seeds[15], (2, D, RANK), D ** -0.5, 0.125, (), jnp.float32)
    mlp_right = centred(seeds[16], (2, RANK, FF), 256 ** -0.5, 0.375, ((2, 4),), jnp.float32)
    mlp_mags = jnp.clip(0.8 + 0.8 * jax.random.uniform(seeds[17], (2, FF), jnp.float32) ** shard_levels(seeds[17], (2, FF), ((1, 4),), -0.2, 0.2), 0.8, 1.6)
    out_left = centred(seeds[18], (H * HEAD_DIM, RANK), (H * HEAD_DIM) ** -0.5, 0.125, ((0, 4),), jnp.float32)
    down_left = centred(seeds[19], (FF, RANK), FF ** -0.5, 0.078125, ((0, 4),), jnp.float32)
    exit_right = centred(seeds[20], (2, RANK, D), 256 ** -0.5, 0.375, (), jnp.float32)
    out_mags = jnp.clip(jax.random.uniform(seeds[21], (D,), jnp.float32, 3.0, 9.0), 3.0, 9.0)
    down_mags = jnp.clip(jax.random.uniform(seeds[22], (D,), jnp.float32, 0.8, 1.6), 0.8, 1.6)
    return dict(inputs=inputs, cotangent=cotangent, lengths=lengths, gain_attn=gain_attn, gain_mlp=gain_mlp, w_query=w_query, w_key=w_key, w_value=w_value, w_out=w_out, w_gate=w_gate, w_up=w_up, w_down=w_down, qkv_left=qkv_left, qkv_right=qkv_right, qkv_mags=qkv_mags, mlp_left=mlp_left, mlp_right=mlp_right, mlp_mags=mlp_mags, out_left=out_left, down_left=down_left, exit_right=exit_right, out_mags=out_mags, down_mags=down_mags)


@jax.custom_vjp
def low(v):
    return lax.optimization_barrier(v.astype(jnp.bfloat16)).astype(jnp.float32)

@jax.custom_vjp
def low_back(v):
    return v

def low_keep(v):
    return (low(v), None)

def low_pass(kept, grad):
    return (grad,)

def back_keep(v):
    return (v, None)

def back_low(kept, grad):
    return (low(grad),)
low.defvjp(low_keep, low_pass)
low_back.defvjp(back_keep, back_low)
highest = lax.Precision.HIGHEST
norm_eps = 1e-05
adapter_alpha = 32.0
rope_base = 10000.0
mask_fill = -1e+30

def exact(left, right):
    return jnp.dot(left, right, precision=highest)

def norm_rows(rows, gain):
    return rows * lax.rsqrt(lax.optimization_barrier(jnp.mean(rows * rows, axis=-1, keepdims=True)) + norm_eps) * gain

def rope_tables(length, width):
    half = width // 2
    freqs = rope_base ** (-(jnp.arange(half, dtype=jnp.float32) * 2.0) / width)
    angles = jnp.arange(length, dtype=jnp.float32)[:, None] * freqs[None, :]
    angles = jnp.concatenate([angles, angles], axis=1)
    return (jnp.cos(angles), jnp.sin(angles))

def turn(field, cosines, sines):
    half = field.shape[-1] // 2
    swapped = jnp.concatenate([-field[..., half:], field[..., :half]], axis=-1)
    return field * cosines[:, None, :] + swapped * sines[:, None, :]

def column_norms(weight, left, right, scale):
    full = weight + scale * exact(left, right)
    return jnp.sqrt(lax.optimization_barrier(jnp.sum(full * full, axis=0)))

def column_proj(normed, weight, left, right, mags, scale):
    norms = column_norms(weight, left, right, scale)
    length = normed.shape[0]
    width = weight.shape[1] // N_HEADS
    inner = low(exact(normed, low(left)))
    copies = low_back(jnp.broadcast_to(inner[None], (N_HEADS,) + inner.shape))
    right_blocks = low(right).reshape(right.shape[0], N_HEADS, width)
    adapted = jnp.einsum('gtr,rgc->tgc', copies, right_blocks, precision=highest).reshape(length, -1)
    summed = low_back(exact(normed, weight) + scale * adapted)
    return summed * (mags / norms)

def row_proj(hidden, weight, left, right, mags, scale):
    norms = column_norms(weight, left, right, scale)
    length = hidden.shape[0]
    width = weight.shape[0] // N_HEADS
    pieces = hidden.reshape(length, N_HEADS, width)
    inner = low_back(jnp.einsum('tgw,gwr->gtr', pieces, low(left).reshape(N_HEADS, width, -1), precision=highest))
    parts = jnp.einsum('tgw,gwd->gtd', pieces, weight.reshape(N_HEADS, width, -1), precision=highest)
    parts = parts + scale * jnp.einsum('gtr,rd->gtd', inner, low(right), precision=highest)
    summed = low_back(lax.optimization_barrier(jnp.sum(low(parts), axis=0)))
    return summed * (mags / norms)

def masked_scores(rows, keys, start, length, factor):
    raw = low_back(jnp.einsum('qhd,khd->hqk', rows, keys, precision=highest))
    places = jnp.arange(keys.shape[0], dtype=jnp.int32)
    queries_at = start + jnp.arange(rows.shape[0], dtype=jnp.int32)
    allowed = (places[None, :] <= queries_at[:, None]) & (places[None, :] < length)
    return jnp.where(allowed[None], raw * factor, mask_fill)

def attend(query, keys, values, length):
    total = query.shape[0]
    block = min(512, total)
    factor = 1.0 / math.sqrt(HEAD_DIM)

    def one_block(start):
        rows = lax.dynamic_slice_in_dim(query, start, block, 0)
        scores = masked_scores(rows, keys, start, length, factor)
        peak = lax.optimization_barrier(jnp.max(scores, axis=-1, keepdims=True))
        weights = jnp.exp(scores - peak)
        probs = weights / lax.optimization_barrier(jnp.sum(weights, axis=-1, keepdims=True))
        return jnp.einsum('hqk,khd->qhd', low(probs), values, precision=highest)
    starts = (jnp.arange(total // block) * block).astype(jnp.int32)
    mixed = lax.map(jax.checkpoint(one_block), starts)
    return mixed.reshape(query.shape)

def reference(inputs, cotangent, lengths, gain_attn, gain_mlp, w_query, w_key, w_value, w_out, w_gate, w_up, w_down, qkv_left, qkv_right, qkv_mags, mlp_left, mlp_right, mlp_mags, out_left, down_left, exit_right, out_mags, down_mags):
    scale = adapter_alpha / RANK
    column_weights = [weight.astype(jnp.float32) for weight in (w_query, w_key, w_value)]
    mlp_weights = [weight.astype(jnp.float32) for weight in (w_gate, w_up)]
    out_weight = w_out.astype(jnp.float32)
    down_weight = w_down.astype(jnp.float32)
    first_gain = gain_attn.astype(jnp.float32)
    second_gain = gain_mlp.astype(jnp.float32)
    cosines, sines = rope_tables(LEN, HEAD_DIM)
    params = (qkv_left, qkv_right, qkv_mags, mlp_left, mlp_right, mlp_mags, out_left, down_left, exit_right, out_mags, down_mags)

    def forward(rows, weights, length):
        first = low(norm_rows(rows, first_gain))
        projected = [column_proj(first, column_weights[index], weights[0][index], weights[1][index], weights[2][index], scale) for index in range(3)]
        shape = (LEN, H, HEAD_DIM)
        query = low(turn(projected[0].reshape(shape), cosines, sines))
        keys = low(turn(projected[1].reshape(shape), cosines, sines))
        values = low(projected[2].reshape(shape))
        attended = low(low_back(attend(query, keys, values, length).reshape(LEN, H * HEAD_DIM)))
        middle = rows + row_proj(attended, out_weight, weights[6], weights[8][0], weights[9], scale)
        second = low(norm_rows(middle, second_gain))
        gate = column_proj(second, mlp_weights[0], weights[3][0], weights[4][0], weights[5][0], scale)
        upper = column_proj(second, mlp_weights[1], weights[3][1], weights[4][1], weights[5][1], scale)
        hidden = low(gate / (1.0 + jnp.exp(-gate)) * upper)
        return middle + row_proj(hidden, down_weight, weights[7], weights[8][1], weights[10], scale)

    def per_sequence(carry, items):
        rows, back, length = items
        result, pull = jax.vjp(lambda field, weights: forward(field, weights, length), rows, params)
        grad_field, grad_weights = pull(back)
        return (jax.tree.map(jnp.add, carry, grad_weights), (result.astype(jnp.bfloat16), grad_field))
    start_sums = jax.tree.map(jnp.zeros_like, params)
    sums, (results, grads) = lax.scan(per_sequence, start_sums, (inputs.astype(jnp.float32).reshape(SEQS, LEN, D), cotangent.astype(jnp.float32).reshape(SEQS, LEN, D), lengths))
    norms = [column_norms(column_weights[index], qkv_left[index], qkv_right[index], scale) for index in range(3)]
    norms = norms + [column_norms(mlp_weights[index], mlp_left[index], mlp_right[index], scale) for index in range(2)]
    norms = norms + [column_norms(out_weight, out_left, exit_right[0], scale), column_norms(down_weight, down_left, exit_right[1], scale)]
    every_norm = jnp.concatenate(norms)
    every_mag = jnp.concatenate([qkv_mags[0], qkv_mags[1], qkv_mags[2], mlp_mags[0], mlp_mags[1], out_mags, down_mags])
    norm_stats = jnp.stack([every_norm, every_mag - every_norm])
    return (results.reshape(TOKENS, D), grads.reshape(TOKENS, D), sums[0], sums[1], sums[2], sums[3], sums[4], sums[5], sums[6], sums[7], sums[8], sums[9], sums[10], norm_stats)
```

```python
import functools
import math

import jax
import jax.numpy as jnp
from jax import lax
from jax.experimental import pallas as pl
from jax.experimental.pallas import tpu as pltpu
from jax.sharding import PartitionSpec as P

HEAD_DIM = 128
RANK = 16
norm_eps = 1e-05
rope_base = 10000.0
mask_fill = -1e30
SCALE = 32.0 / RANK

f32 = jnp.float32
bf16 = jnp.bfloat16
MESH = pl.DeviceIdType.MESH
VMEM = pl.BlockSpec(memory_space=pltpu.VMEM)
SMEM = pl.BlockSpec(memory_space=pltpu.SMEM)
ANY = pl.BlockSpec(memory_space=pl.ANY)
LIMIT = 60 << 20


def nn(left, right):
    return jnp.dot(left, right, preferred_element_type=f32)


def nt(left, right):
    return lax.dot_general(left, right, (((1,), (1,)), ((), ())), preferred_element_type=f32)


def nn_exact(left, right):
    return jnp.dot(left, right, precision=lax.Precision.HIGHEST, preferred_element_type=f32)


def nt_exact(left, right):
    return lax.dot_general(
        left,
        right,
        (((1,), (1,)), ((), ())),
        precision=lax.Precision.HIGHEST,
        preferred_element_type=f32,
    )


def split_rows(field):
    high = field.astype(bf16)
    return jnp.concatenate([high, (field - high.astype(f32)).astype(bf16)], axis=0)


def square_sums(ref, columns, chunk=128):
    depth = ref.shape[0]
    width = columns.size if isinstance(columns, pl.Slice) else columns.stop - columns.start

    def step(index, total):
        piece = ref[pl.ds(pl.multiple_of(index * chunk, chunk), chunk), columns].astype(f32)
        return total + jnp.sum((piece * piece).reshape(chunk // 8, 8, width), axis=0)

    total = lax.fori_loop(0, depth // chunk, step, jnp.zeros((8, width), f32))
    return jnp.sum(total, axis=0, keepdims=True)


def direction(squares, pieces, gram, right):
    plain = pieces[:RANK] + pieces[RANK:]
    turned = nn_exact(gram, jnp.concatenate([right, right], axis=0))
    full = plain + SCALE * (turned[:RANK] + turned[RANK:])
    return squares + SCALE * jnp.sum(right * (plain + full), axis=0, keepdims=True), full


def padded_right(right, at, count, factor):
    low = factor * right.astype(bf16).astype(f32)
    zero = jnp.zeros_like(low)
    return jnp.concatenate([low if slot == at else zero for slot in range(count)], axis=0).astype(bf16)


def norm_value(rows, gain):
    inverse = lax.rsqrt(jnp.mean(rows * rows, axis=-1, keepdims=True) + norm_eps)
    return rows * inverse * gain, inverse


def greet(count):
    row, me = lax.axis_index("rows"), lax.axis_index("heads")
    barrier = pltpu.get_barrier_semaphore()
    for step in range(1, count):
        pl.semaphore_signal(
            barrier, inc=1, device_id=(row, lax.rem(me + step, count)), device_id_type=MESH
        )
    pl.semaphore_wait(barrier, count - 1)


def exit_stats_kernel(w_out, w_down, lt_out, lt_down, right, part):
    for index, (weight, lt) in enumerate(((w_out, lt_out), (w_down, lt_down))):
        for start in range(0, weight.shape[1], 512):
            columns = slice(start, start + 512)
            squares, full = direction(
                square_sums(weight, columns),
                nn(lt[...], weight[:, columns]),
                nt(lt[...], lt[...]),
                right[index, :, columns],
            )
            part[index * RANK : (index + 1) * RANK, columns] = full
            part[2 * RANK + index : 2 * RANK + index + 1, columns] = squares
    part[2 * RANK + 2 :, :] = jnp.zeros((6, part.shape[1]), f32)


def attention_forward_kernel(
    count,
    length_ref,
    x_ref,
    gain_ref,
    lth,
    ltl,
    right,
    mags,
    cosines,
    sines,
    w_query,
    w_key,
    w_value,
    first,
    query,
    keys,
    values,
    att,
    lse,
    summed,
    inner_ref,
    norms_ref,
    full_ref,
    gathered,
    ext,
    weights,
    wsem,
    fsem,
    send_sem,
    recv_sem,
):
    me = lax.axis_index("heads")
    row = lax.axis_index("rows")
    total = x_ref.shape[0]
    share = total // count
    loads = [
        pltpu.make_async_copy(source, weights.at[index], wsem.at[index])
        for index, source in enumerate((w_query, w_key, w_value))
    ]
    for load in loads:
        load.start()
    greet(count)
    gain = gain_ref[...].astype(f32)

    @pl.loop(0, total // 128)
    def _(index):
        rows = pl.ds(pl.multiple_of(index * 128, 128), 128)
        normed, _ = norm_value(x_ref[rows, :].astype(f32), gain)
        ext[rows, :] = normed.astype(bf16)

    store_first = pltpu.make_async_copy(ext.at[:total], first, fsem)
    store_first.start()
    inner = nt(ext[:total, :], lth[...]).astype(bf16)
    inner_ref[...] = inner
    heads = query.shape[1] // HEAD_DIM
    for index in range(3):
        block = slice(index * RANK, (index + 1) * RANK)
        ext[total : total + RANK, :] = lth[block, :]
        ext[total + RANK :, :] = ltl[block, :]
        adapters = ext[total:, :]
        gram = nt(adapters, adapters)
        loads[index].wait()
        for start in range(0, query.shape[1], 256):
            columns = slice(start, start + 256)
            weight = weights[index, :, columns]
            product = nn(ext[...], weight)
            local_right = right[index, :, columns]
            squares, full = direction(
                square_sums(weights.at[index], columns), product[total:], gram, local_right
            )
            norms = jnp.sqrt(squares)
            norms_ref[index : index + 1, columns] = norms
            full_ref[index, :, columns] = full
            z = product[:total] + nn(inner, padded_right(local_right, index, 3, SCALE))
            summed[index, :, columns] = z.astype(bf16)
            y = z * (mags[index : index + 1, columns] / norms)
            if index == 2:
                values[:, columns] = y.astype(bf16)
            else:
                for head in range(2):
                    part = y[:, head * HEAD_DIM : (head + 1) * HEAD_DIM]
                    turned = part * cosines[...] + pltpu.roll(part, HEAD_DIM // 2, 1) * sines[...]
                    place = slice(start + head * HEAD_DIM, start + (head + 1) * HEAD_DIM)
                    (query if index == 0 else keys)[:, place] = turned.astype(bf16)

    length = length_ref[0]
    factor = 1.0 / math.sqrt(HEAD_DIM)
    copies = []
    for head in range(heads):
        place = slice(head * HEAD_DIM, (head + 1) * HEAD_DIM)
        turned_values = values[:, place].astype(f32).T.astype(bf16)
        for block in range(total // 256):
            reach = (block + 1) * 256
            at = slice(block * 256, reach)
            scores = nt(keys[:reach, place], query[at, place])
            spots = lax.broadcasted_iota(jnp.int32, (reach, 256), 0)
            asking = lax.broadcasted_iota(jnp.int32, (reach, 256), 1) + block * 256
            allowed = (spots <= asking) & (spots < length)
            scores = jnp.where(allowed, scores * factor, mask_fill)
            peak = jnp.max(scores, axis=0, keepdims=True)
            exps = jnp.exp(scores - peak)
            totals = jnp.sum(exps, axis=0, keepdims=True)
            probs = (exps * (1.0 / totals)).astype(bf16)
            mixed = nn(turned_values[:, :reach], probs)
            att[at, place] = mixed.T.astype(bf16)
            lse[head : head + 1, at] = peak + jnp.log(totals)
        for step in range(1, count):
            peer = lax.rem(me + step, count)
            copy = pltpu.make_async_remote_copy(
                src_ref=att.at[pl.ds(pl.multiple_of(peer * share, share), share), place],
                dst_ref=gathered.at[me, :, place],
                send_sem=send_sem.at[head, step],
                recv_sem=recv_sem.at[head, step],
                device_id=(row, peer),
                device_id_type=MESH,
            )
            copy.start()
            copies.append(copy)
    gathered[me] = att[pl.ds(pl.multiple_of(me * share, share), share), :]
    store_first.wait()
    for copy in copies:
        copy.wait()


def out_forward_kernel(
    gathered, w_full, lth, right, norms, mags, x_ref, gain_ref, middle, second, summed, inner_ref, att
):
    group = gathered.shape[2]
    for index in range(gathered.shape[0]):
        att[:, index * group : (index + 1) * group] = gathered[index]
    x = att[...]
    inner = nt(x, lth[...])
    inner_ref[...] = inner
    low = inner.astype(bf16)
    width = w_full.shape[2]
    for index in range(w_full.shape[0]):
        columns = slice(index * width, (index + 1) * width)
        z = nn(x, w_full[index]) + nn(low, padded_right(right[:, columns], 0, 1, SCALE))
        summed[:, columns] = z
        middle[:, columns] = x_ref[:, columns].astype(f32) + z * (
            mags[:, columns] / norms[:, columns]
        )
    normed, _ = norm_value(middle[...], gain_ref[...].astype(f32))
    second[...] = normed.astype(bf16)


def feed_forward_kernel(
    sec,
    cot,
    w_gate,
    w_up,
    w_down,
    lth,
    ltl,
    lt_down,
    right,
    mags,
    right_down,
    mags_down,
    norms_down,
    part,
    grad_second,
    grad_left,
    grad_right,
    grad_mags,
    norms_ref,
    grad_left_down,
    grad_right_down,
    factors,
):
    weights = (w_gate, w_up)
    fulls, lows, backs = [], [], []
    for index in range(2):
        block = slice(index * RANK, (index + 1) * RANK)
        adapters = jnp.concatenate([lth[block, :], ltl[block, :]], axis=0)
        squares, full = direction(
            square_sums(weights[index], slice(0, w_gate.shape[1])),
            nn(adapters, weights[index][...]),
            nt(adapters, adapters),
            right[index],
        )
        norms = jnp.sqrt(squares)
        norms_ref[index : index + 1, :] = norms
        factors[index : index + 1, :] = mags[index : index + 1, :] / norms
        fulls.append(full)
    factor_down = mags_down[...] / norms_down[...]
    grad_left[...] = jnp.zeros_like(grad_left)
    grad_right[...] = jnp.zeros_like(grad_right)
    grad_mags[...] = jnp.zeros_like(grad_mags)
    grad_left_down[...] = jnp.zeros_like(grad_left_down)
    grad_right_down[...] = jnp.zeros_like(grad_right_down)

    @pl.loop(0, sec.shape[0] // 256)
    def _(step):
        rows = pl.ds(pl.multiple_of(step * 256, 256), 256)
        x = sec[rows, :]
        inner = nt(x, lth[...])
        inner_low = inner.astype(bf16)
        zs = [
            nn(x, weights[index][...])
            + nn(inner_low, padded_right(right[index], index, 2, SCALE))
            for index in range(2)
        ]
        gate = zs[0] * factors[0:1, :]
        upper = zs[1] * factors[1:2, :]
        sigmoid = 1.0 / (1.0 + jnp.exp(-gate))
        activated = gate * sigmoid
        hidden = (activated * upper).astype(bf16)
        right_low = right_down[...].astype(bf16)
        inner_down = nt(hidden, lt_down[:RANK, :])
        part[rows, :] = (
            nn(hidden, w_down[...]) + SCALE * nn(inner_down.astype(bf16), right_low)
        ).astype(bf16)
        gz_down = (cot[rows, :].astype(f32) * factor_down).astype(bf16)
        gin_down = SCALE * nt(gz_down, right_low)
        grad_hidden = nt(gz_down, w_down[...]) + nn(gin_down.astype(bf16), lt_down[:RANK, :])
        grad_left_down[...] += nn(gin_down.T.astype(bf16), hidden)
        grad_right_down[...] += SCALE * nn(inner_down.T.astype(bf16), gz_down)
        grads = (
            grad_hidden * upper * sigmoid * (1.0 + gate * (1.0 - sigmoid)),
            grad_hidden * activated,
        )
        gin = jnp.zeros((256, 2 * RANK), f32)
        gzs = []
        for index in range(2):
            grad_mags[index : index + 1, :] += jnp.sum(grads[index] * zs[index], axis=0, keepdims=True)
            gz = (grads[index] * factors[index : index + 1, :]).astype(bf16)
            gin = gin + nt(gz, padded_right(right[index], index, 2, SCALE))
            gzs.append(gz)
        gin_low = gin.astype(bf16)
        grad_second[rows, :] = (
            nt(gzs[0], w_gate[...]) + nt(gzs[1], w_up[...]) + nn(gin_low, lth[...])
        ).astype(bf16)
        grad_left[...] += nn(gin.T.astype(bf16), x)
        inner_turned = inner.T.astype(bf16)
        for index in range(2):
            grad_right[index] += (
                SCALE * nn(inner_turned, gzs[index])[index * RANK : (index + 1) * RANK]
            )

    for index in range(2):
        block = slice(index * RANK, (index + 1) * RANK)
        norms = norms_ref[index : index + 1, :]
        factor_grad = grad_mags[index : index + 1, :]
        shape = -factor_grad * mags[index : index + 1, :] / (norms * norms * norms)
        shaped = right[index] * shape
        pieces = nt(split_rows(shaped), weights[index][...])
        lt = lth[block, :].astype(f32) + ltl[block, :].astype(f32)
        grad_left[block, :] += SCALE * (
            pieces[:RANK]
            + pieces[RANK:]
            + SCALE * nn_exact(nt_exact(shaped, right[index]), lt)
        )
        grad_right[index] += SCALE * fulls[index] * shape
        grad_mags[index : index + 1, :] = factor_grad / norms


def out_back_kernel(
    count,
    grad_second,
    middle,
    cot,
    gain_ref,
    summed,
    gathered,
    inner,
    w_full,
    lth,
    ltl,
    right,
    norms,
    mags,
    full,
    grad_middle,
    mixed,
    grad_left,
    grad_right,
    grad_mags,
    ext,
    back,
    send_sem,
    recv_sem,
):
    me = lax.axis_index("heads")
    row = lax.axis_index("rows")
    greet(count)
    share, depth = middle.shape
    rows = middle[...]
    gain = gain_ref[...].astype(f32)
    inverse = lax.rsqrt(jnp.mean(rows * rows, axis=-1, keepdims=True) + norm_eps)
    scaled = grad_second[...].astype(f32) * gain
    grad = (
        cot[...].astype(f32)
        + inverse * scaled
        - rows * (inverse * inverse * inverse) * jnp.mean(rows * scaled, axis=-1, keepdims=True)
    )
    grad_middle[...] = grad
    norm = norms[...]
    factor_grad = jnp.sum(grad * summed[...], axis=0, keepdims=True)
    shape = -factor_grad * mags[...] / (norm * norm * norm)
    shaped = right[...] * shape
    ext[:share, :] = (grad * (mags[...] / norm)).astype(bf16)
    ext[share:, :] = split_rows(shaped)
    gz = ext[:share, :]
    gin = SCALE * nt(gz, right[...].astype(bf16))
    gin_low = gin.astype(bf16)
    width = w_full.shape[2]
    grad_mags[...] = factor_grad / norm
    grad_right[...] = SCALE * (nn(inner[...].T.astype(bf16), gz) + full[...] * shape)
    gin_turned = gin.T.astype(bf16)
    mixing = nt_exact(shaped, right[...])
    group = depth // count
    copies = []
    for step in range(1, count + 1):
        peer = lax.rem(me + step, count)
        columns = pl.ds(pl.multiple_of(peer * group, group), group)
        total = jnp.zeros((share + 2 * RANK, group), f32)
        for index in range(w_full.shape[0]):
            total = total + nt(
                ext[:, index * width : (index + 1) * width], w_full[index, columns, :]
            )
        result = (total[:share] + nn(gin_low, lth[:, columns])).astype(bf16)
        lt = lth[:, columns].astype(f32) + ltl[:, columns].astype(f32)
        grad_left[:, columns] = nn(gin_turned, gathered[peer]) + SCALE * (
            total[share : share + RANK] + total[share + RANK :] + SCALE * nn_exact(mixing, lt)
        )
        if step == count:
            mixed[me] = result
        else:
            back[peer] = result
            copy = pltpu.make_async_remote_copy(
                src_ref=back.at[peer],
                dst_ref=mixed.at[me],
                send_sem=send_sem.at[step],
                recv_sem=recv_sem.at[step],
                device_id=(row, peer),
                device_id_type=MESH,
            )
            copy.start()
            copies.append(copy)
    for copy in copies:
        copy.wait()


def attention_back_kernel(
    length_ref,
    query,
    keys,
    values,
    att,
    lse,
    mixed,
    first,
    summed,
    norms_ref,
    mags,
    fulls,
    inner,
    lth,
    ltl,
    right,
    cosines,
    sines,
    w_query,
    w_key,
    w_value,
    grad_first,
    grad_left,
    grad_right,
    grad_mags,
    gz,
    key_sums,
    value_sums,
    query_turned,
    factors,
):
    total = query.shape[0]
    heads = query.shape[1] // HEAD_DIM
    length = length_ref[0]
    factor = 1.0 / math.sqrt(HEAD_DIM)
    factors[...] = mags[...] / norms_ref[...]

    def finish(index, head, grad):
        place = slice(head * HEAD_DIM, (head + 1) * HEAD_DIM)
        if index < 2:
            grad = grad * cosines[...] - pltpu.roll(grad, HEAD_DIM // 2, 1) * sines[...]
        grad_mags[index : index + 1, place] = jnp.sum(
            grad * summed[index, :, place].astype(f32), axis=0, keepdims=True
        )
        gz[index, :, place] = (grad * factors[index : index + 1, place]).astype(bf16)

    for head in range(heads):
        place = slice(head * HEAD_DIM, (head + 1) * HEAD_DIM)
        turned_keys = keys[:, place].astype(f32).T.astype(bf16)
        key_sums[...] = jnp.zeros_like(key_sums)
        value_sums[...] = jnp.zeros_like(value_sums)
        for block in range(total // 256):
            reach = (block + 1) * 256
            at = slice(block * 256, reach)
            grad_rows = mixed[at, place]
            rows = query[at, place]
            scores = nt(keys[:reach, place], rows)
            spots = lax.broadcasted_iota(jnp.int32, (reach, 256), 0)
            asking = lax.broadcasted_iota(jnp.int32, (reach, 256), 1) + block * 256
            allowed = (spots <= asking) & (spots < length)
            scores = jnp.where(allowed, scores * factor, mask_fill)
            probs = jnp.exp(scores - lse[head : head + 1, at])
            grad_probs = nt(values[:reach, place], grad_rows)
            centre = jnp.sum(
                (grad_rows.astype(f32) * att[at, place].astype(f32)).T, axis=0, keepdims=True
            )
            raw = (probs * (grad_probs - centre) * factor).astype(bf16)
            value_sums[:reach, :] += nn(probs.astype(bf16), grad_rows)
            key_sums[:reach, :] += nn(raw, rows)
            query_turned[:, at] = nn(turned_keys[:, :reach], raw)
        finish(0, head, query_turned[...].T)
        finish(1, head, key_sums[...])
        finish(2, head, value_sums[...])

    weights = (w_query, w_key, w_value)
    gin = jnp.zeros((total, 3 * RANK), f32)
    for index in range(3):
        gin = gin + nt(gz[index], padded_right(right[index], index, 3, SCALE))
    gin_low = gin.astype(bf16)
    grad_left[...] = nn(gin.T.astype(bf16), first[...])
    inner_turned = inner[...].astype(f32).T.astype(bf16)
    for index in range(3):
        block = slice(index * RANK, (index + 1) * RANK)
        norms = norms_ref[index : index + 1, :]
        factor_grad = grad_mags[index : index + 1, :]
        shape = -factor_grad * mags[index : index + 1, :] / (norms * norms * norms)
        shaped = right[index] * shape
        pieces = nt(split_rows(shaped), weights[index][...])
        lt = lth[block, :].astype(f32) + ltl[block, :].astype(f32)
        grad_left[block, :] += SCALE * (
            pieces[:RANK]
            + pieces[RANK:]
            + SCALE * nn_exact(nt_exact(shaped, right[index]), lt)
        )
        grad_right[index] = SCALE * (nn(inner_turned, gz[index])[block] + fulls[index] * shape)
        grad_mags[index : index + 1, :] = factor_grad / norms
    for block in range(total // 256):
        at = slice(block * 256, (block + 1) * 256)
        grad_first[at, :] = (
            nt(gz[0, at, :], w_query[...])
            + nt(gz[1, at, :], w_key[...])
            + nt(gz[2, at, :], w_value[...])
            + nn(gin_low[at, :], lth[...])
        ).astype(bf16)


def call(kernel, outs, ins, specs=None, out_specs=None, scratch=(), flops=0, moved=0, collective=None):
    extra = {} if collective is None else {"collective_id": collective, "has_side_effects": True}
    return pl.pallas_call(
        kernel,
        out_shape=[jax.ShapeDtypeStruct(shape, kind) for shape, kind in outs],
        in_specs=specs or [VMEM] * len(ins),
        out_specs=out_specs or [VMEM] * len(outs),
        scratch_shapes=list(scratch),
        cost_estimate=pl.CostEstimate(flops=flops, bytes_accessed=moved, transcendentals=0),
        compiler_params=pltpu.CompilerParams(vmem_limit_bytes=LIMIT, **extra),
    )(*ins)


def rope_tables(length, width):
    half = width // 2
    freqs = rope_base ** (-(jnp.arange(half, dtype=f32) * 2.0) / width)
    angles = jnp.arange(length, dtype=f32)[:, None] * freqs[None, :]
    sines = jnp.sin(angles)
    return jnp.tile(jnp.cos(angles), (1, 2)), jnp.concatenate([-sines, sines], axis=1)


def pieces_of(turned):
    high = lax.reduce_precision(turned, 8, 7)
    return high.astype(bf16), (turned - high).astype(bf16)


def local(
    inputs,
    cotangent,
    lengths,
    gain_attn,
    gain_mlp,
    w_query,
    w_key,
    w_value,
    w_out,
    w_gate,
    w_up,
    w_down,
    qkv_left,
    qkv_right,
    qkv_mags,
    mlp_left,
    mlp_right,
    mlp_mags,
    out_left,
    down_left,
    exit_right,
    out_mags,
    down_mags,
):
    count = lax.axis_size("heads")
    teams = lax.axis_size("rows")
    total, depth = inputs.shape
    share = total // count
    group = w_query.shape[1]
    units = w_gate.shape[1]
    heads = group // HEAD_DIM
    me = lax.axis_index("heads")
    offset = me * share
    both = ("rows", "heads")

    width = depth // teams
    piece = lax.dynamic_slice_in_dim(w_out, lax.axis_index("rows") * width, width, 1)
    piece = lax.all_gather(piece, "heads", axis=0, tiled=True)
    w_full = lax.all_gather(piece, "rows", axis=0)
    if width < 256:
        merge = 256 // width
        w_full = (
            w_full.reshape(teams // merge, merge, depth, width)
            .transpose(0, 2, 1, 3)
            .reshape(teams // merge, depth, 256)
        )
    lt_qkv, ltl_qkv = pieces_of(jnp.transpose(qkv_left, (0, 2, 1)).reshape(3 * RANK, depth))
    lt_mlp, ltl_mlp = pieces_of(jnp.transpose(mlp_left, (0, 2, 1)).reshape(2 * RANK, depth))
    lt_down = jnp.concatenate(pieces_of(down_left.T), axis=0)
    turned_out = out_left.T
    lt_out_local = jnp.concatenate(pieces_of(turned_out), axis=0)
    lt_out, ltl_out = pieces_of(lax.all_gather(turned_out, "heads", axis=1, tiled=True))
    cosines, sines = rope_tables(total, HEAD_DIM)
    gain_first = gain_attn.reshape(1, depth)
    gain_second = gain_mlp.reshape(1, depth)
    out_mag, down_mag = out_mags.reshape(1, depth), down_mags.reshape(1, depth)

    (stats,) = call(
        exit_stats_kernel,
        [((2 * RANK + 8, depth), f32)],
        (w_out, w_down, lt_out_local, lt_down, exit_right),
        flops=2 * 256 * (group + units) * depth,
        moved=2 * (group + units) * depth,
    )
    stats = lax.psum(stats, "heads")
    full_out, full_down = stats[:RANK], stats[RANK : 2 * RANK]
    exit_norms = jnp.sqrt(stats[2 * RANK : 2 * RANK + 2])
    out_norms, down_norms = exit_norms[0:1], exit_norms[1:2]

    (
        first,
        query,
        keys,
        values,
        att,
        lse,
        qkv_summed,
        qkv_inner,
        qkv_norms,
        qkv_full,
        gathered,
    ) = call(
        functools.partial(attention_forward_kernel, count),
        [
            ((total, depth), bf16),
            ((total, group), bf16),
            ((total, group), bf16),
            ((total, group), bf16),
            ((total, group), bf16),
            ((heads, total), f32),
            ((3, total, group), bf16),
            ((total, 3 * RANK), bf16),
            ((3, group), f32),
            ((3, RANK, group), f32),
            ((count, share, group), bf16),
        ],
        (
            lengths,
            inputs,
            gain_first,
            lt_qkv,
            ltl_qkv,
            qkv_right,
            qkv_mags,
            cosines,
            sines,
            w_query,
            w_key,
            w_value,
        ),
        specs=[SMEM] + [VMEM] * 8 + [ANY] * 3,
        out_specs=[ANY] + [VMEM] * 10,
        scratch=(
            pltpu.VMEM((total + 2 * RANK, depth), bf16),
            pltpu.VMEM((3, depth, group), bf16),
            pltpu.SemaphoreType.DMA((3,)),
            pltpu.SemaphoreType.DMA,
            pltpu.SemaphoreType.DMA((heads, count)),
            pltpu.SemaphoreType.DMA((heads, count)),
        ),
        flops=6 * total * depth * group + 4 * total * total * group,
        moved=2 * (2 * total * depth + 3 * depth * group + 8 * total * group),
        collective=0,
    )

    x_own = lax.dynamic_slice_in_dim(inputs, offset, share, 0)
    cot_own = lax.dynamic_slice_in_dim(cotangent, offset, share, 0)
    middle, second, out_summed, out_inner = call(
        out_forward_kernel,
        [
            ((share, depth), f32),
            ((share, depth), bf16),
            ((share, depth), f32),
            ((share, RANK), f32),
        ],
        (gathered, w_full, lt_out, exit_right[0], out_norms, out_mag, x_own, gain_second),
        scratch=(pltpu.VMEM((share, depth), bf16),),
        flops=2 * share * depth * depth,
        moved=2 * depth * depth,
    )
    sec = lax.all_gather(second, "heads", axis=0, tiled=True)
    (
        part,
        grad_second,
        grad_mlp_left,
        grad_mlp_right,
        grad_mlp_mags,
        mlp_norms,
        grad_down_left,
        grad_down_right,
    ) = call(
        feed_forward_kernel,
        [
            ((total, depth), bf16),
            ((total, depth), bf16),
            ((2 * RANK, depth), f32),
            ((2, RANK, units), f32),
            ((2, units), f32),
            ((2, units), f32),
            ((RANK, units), f32),
            ((RANK, depth), f32),
        ],
        (
            sec,
            cotangent,
            w_gate,
            w_up,
            w_down,
            lt_mlp,
            ltl_mlp,
            lt_down,
            mlp_right,
            mlp_mags,
            exit_right[1],
            down_mag,
            down_norms,
        ),
        scratch=(pltpu.VMEM((2, units), f32),),
        flops=12 * total * depth * units,
        moved=2 * (3 * depth * units + 4 * total * depth),
    )
    grad_second_own = lax.psum_scatter(grad_second, "heads", scatter_dimension=0, tiled=True)
    down_own = lax.psum_scatter(part, "heads", scatter_dimension=0, tiled=True).astype(f32)

    grad_middle, mixed, grad_out_left, grad_out_right, grad_out_mags = call(
        functools.partial(out_back_kernel, count),
        [
            ((share, depth), f32),
            ((count, share, group), bf16),
            ((RANK, depth), f32),
            ((RANK, depth), f32),
            ((1, depth), f32),
        ],
        (
            grad_second_own,
            middle,
            cot_own,
            gain_second,
            out_summed,
            gathered,
            out_inner,
            w_full,
            lt_out,
            ltl_out,
            exit_right[0],
            out_norms,
            out_mag,
            full_out,
        ),
        scratch=(
            pltpu.VMEM((share + 2 * RANK, depth), bf16),
            pltpu.VMEM((count, share, group), bf16),
            pltpu.SemaphoreType.DMA((count,)),
            pltpu.SemaphoreType.DMA((count,)),
        ),
        flops=2 * share * depth * depth,
        moved=2 * depth * depth,
        collective=1,
    )

    grad_first, grad_qkv_left, grad_qkv_right, grad_qkv_mags = call(
        attention_back_kernel,
        [
            ((total, depth), bf16),
            ((3 * RANK, depth), f32),
            ((3, RANK, group), f32),
            ((3, group), f32),
        ],
        (
            lengths,
            query,
            keys,
            values,
            att,
            lse,
            mixed.reshape(total, group),
            first,
            qkv_summed,
            qkv_norms,
            qkv_mags,
            qkv_full,
            qkv_inner,
            lt_qkv,
            ltl_qkv,
            qkv_right,
            cosines,
            sines,
            w_query,
            w_key,
            w_value,
        ),
        specs=[SMEM] + [VMEM] * 20,
        scratch=(
            pltpu.VMEM((3, total, group), bf16),
            pltpu.VMEM((total, HEAD_DIM), f32),
            pltpu.VMEM((total, HEAD_DIM), f32),
            pltpu.VMEM((HEAD_DIM, total), f32),
            pltpu.VMEM((3, group), f32),
        ),
        flops=6 * total * depth * group + 10 * total * total * group,
        moved=2 * (2 * total * depth + 3 * depth * group + 8 * total * group),
    )
    grad_first_own = lax.psum_scatter(grad_first, "heads", scatter_dimension=0, tiled=True)

    x = x_own.astype(f32)
    scaled = grad_first_own.astype(f32) * gain_attn.astype(f32)
    inverse = lax.rsqrt(jnp.mean(x * x, axis=-1, keepdims=True) + norm_eps)
    input_grad = (
        grad_middle
        + inverse * scaled
        - x * (inverse * inverse * inverse) * jnp.mean(x * scaled, axis=-1, keepdims=True)
    )

    outputs = (middle + down_own * (down_mag / down_norms)).astype(bf16)
    down_factor_grad = lax.psum(
        jnp.sum(cot_own.astype(f32) * down_own, axis=0, keepdims=True), both
    )
    shape = -down_factor_grad * down_mag / (down_norms * down_norms * down_norms)
    shaped = exit_right[1] * shape
    high, low = pieces_of(shaped)
    extra_left = SCALE * (
        jnp.dot(high, w_down.T, preferred_element_type=f32)
        + jnp.dot(low, w_down.T, preferred_element_type=f32)
        + SCALE
        * jnp.dot(
            jnp.dot(shaped, exit_right[1].T, precision=lax.Precision.HIGHEST),
            down_left.T,
            precision=lax.Precision.HIGHEST,
        )
    )

    sums = lax.psum(
        (
            jnp.concatenate([grad_qkv_left, grad_mlp_left, grad_out_right, grad_down_right, grad_out_left]),
            grad_out_mags,
        ),
        both,
    )
    whole, grad_out_mags = sums
    grad_qkv_left = jnp.transpose(whole[: 3 * RANK].reshape(3, RANK, depth), (0, 2, 1))
    grad_mlp_left = jnp.transpose(
        whole[3 * RANK : 5 * RANK].reshape(2, RANK, depth), (0, 2, 1)
    )
    grad_exit_right = jnp.stack(
        [whole[5 * RANK : 6 * RANK], whole[6 * RANK : 7 * RANK] + SCALE * full_down * shape]
    )
    grad_out_left = lax.dynamic_slice_in_dim(whole[7 * RANK :], me * group, group, 1).T
    grad_qkv_right, grad_qkv_mags, grad_mlp_right, grad_mlp_mags, grad_down_left = [
        lax.psum(item.astype(bf16), "rows").astype(f32)
        for item in (grad_qkv_right, grad_qkv_mags, grad_mlp_right, grad_mlp_mags, grad_down_left)
    ]
    grad_down_left = (grad_down_left + extra_left).T

    qkv_stats = jnp.stack([qkv_norms, qkv_mags - qkv_norms]).astype(bf16)
    mlp_stats = jnp.stack([mlp_norms, mlp_mags - mlp_norms]).astype(bf16)
    qkv_table = lax.all_gather(qkv_stats, "heads", axis=2, tiled=True).astype(f32)
    mlp_table = lax.all_gather(mlp_stats, "heads", axis=2, tiled=True).astype(f32)
    exit_stats = jnp.stack([exit_norms, jnp.stack([out_mags, down_mags]) - exit_norms])
    norm_stats = jnp.concatenate(
        [qkv_table.reshape(2, -1), mlp_table.reshape(2, -1), exit_stats.reshape(2, -1)], axis=1
    )
    return (
        outputs,
        input_grad,
        grad_qkv_left,
        grad_qkv_right,
        grad_qkv_mags,
        grad_mlp_left,
        grad_mlp_right,
        grad_mlp_mags,
        grad_out_left,
        grad_down_left,
        grad_exit_right,
        grad_out_mags.reshape(depth),
        (down_factor_grad / down_norms).reshape(depth),
        norm_stats,
    )


def solution(mesh):
    placed = (
        P("rows", None),
        P("rows", None),
        P("rows"),
        P(),
        P(),
        P(None, "heads"),
        P(None, "heads"),
        P(None, "heads"),
        P("heads", None),
        P(None, "heads"),
        P(None, "heads"),
        P("heads", None),
        P(),
        P(None, None, "heads"),
        P(None, "heads"),
        P(),
        P(None, None, "heads"),
        P(None, "heads"),
        P("heads", None),
        P("heads", None),
        P(),
        P(),
        P(),
    )
    return jax.shard_map(
        local,
        mesh=mesh,
        in_specs=placed,
        out_specs=(
            P(("rows", "heads"), None),
            P(("rows", "heads"), None),
            P(),
            P(None, None, "heads"),
            P(None, "heads"),
            P(),
            P(None, None, "heads"),
            P(None, "heads"),
            P("heads", None),
            P("heads", None),
            P(),
            P(),
            P(),
            P(),
        ),
        check_vma=False,
    )
```

```python
import functools
import math

import jax
import jax.numpy as jnp
from jax import lax
from jax.experimental import pallas as pl
from jax.experimental.pallas import tpu as pltpu
from jax.sharding import PartitionSpec as P

HEAD_DIM = 128
RANK = 16
norm_eps = 1e-05
rope_base = 10000.0
mask_fill = -1e30
SCALE = 32.0 / RANK

f32 = jnp.float32
bf16 = jnp.bfloat16
MESH = pl.DeviceIdType.MESH
VMEM = pl.BlockSpec(memory_space=pltpu.VMEM)
SMEM = pl.BlockSpec(memory_space=pltpu.SMEM)
ANY = pl.BlockSpec(memory_space=pl.ANY)
LIMIT = 60 << 20


def nn(left, right):
    return jnp.dot(left, right, preferred_element_type=f32)


def nt(left, right):
    return lax.dot_general(left, right, (((1,), (1,)), ((), ())), preferred_element_type=f32)


def nn_exact(left, right):
    return jnp.dot(left, right, precision=lax.Precision.HIGHEST, preferred_element_type=f32)


def nt_exact(left, right):
    return lax.dot_general(
        left,
        right,
        (((1,), (1,)), ((), ())),
        precision=lax.Precision.HIGHEST,
        preferred_element_type=f32,
    )


def split_rows(field):
    high = field.astype(bf16)
    return jnp.concatenate([high, (field - high.astype(f32)).astype(bf16)], axis=0)


def square_sums(ref, columns, chunk=128):
    depth = ref.shape[0]
    width = columns.size if isinstance(columns, pl.Slice) else columns.stop - columns.start

    def step(index, total):
        piece = ref[pl.ds(pl.multiple_of(index * chunk, chunk), chunk), columns].astype(f32)
        return total + jnp.sum((piece * piece).reshape(chunk // 8, 8, width), axis=0)

    total = lax.fori_loop(0, depth // chunk, step, jnp.zeros((8, width), f32))
    return jnp.sum(total, axis=0, keepdims=True)


def direction(squares, pieces, gram, right):
    plain = pieces[:RANK] + pieces[RANK:]
    turned = nn_exact(gram, jnp.concatenate([right, right], axis=0))
    full = plain + SCALE * (turned[:RANK] + turned[RANK:])
    return squares + SCALE * jnp.sum(right * (plain + full), axis=0, keepdims=True), full


def padded_right(right, at, count, factor):
    low = factor * right.astype(bf16).astype(f32)
    zero = jnp.zeros_like(low)
    return jnp.concatenate([low if slot == at else zero for slot in range(count)], axis=0).astype(bf16)


def norm_value(rows, gain):
    inverse = lax.rsqrt(jnp.mean(rows * rows, axis=-1, keepdims=True) + norm_eps)
    return rows * inverse * gain, inverse


def greet(count):
    row, me = lax.axis_index("rows"), lax.axis_index("heads")
    barrier = pltpu.get_barrier_semaphore()
    for step in range(1, count):
        pl.semaphore_signal(
            barrier, inc=1, device_id=(row, lax.rem(me + step, count)), device_id_type=MESH
        )
    pl.semaphore_wait(barrier, count - 1)


def exit_stats_kernel(w_out, w_down, lt_out, lt_down, right, part):
    for index, (weight, lt) in enumerate(((w_out, lt_out), (w_down, lt_down))):
        for start in range(0, weight.shape[1], 512):
            columns = slice(start, start + 512)
            squares, full = direction(
                square_sums(weight, columns),
                nn(lt[...], weight[:, columns]),
                nt(lt[...], lt[...]),
                right[index, :, columns],
            )
            part[index * RANK : (index + 1) * RANK, columns] = full
            part[2 * RANK + index : 2 * RANK + index + 1, columns] = squares
    part[2 * RANK + 2 :, :] = jnp.zeros((6, part.shape[1]), f32)


def attention_forward_kernel(
    count,
    length_ref,
    x_ref,
    gain_ref,
    lth,
    ltl,
    right,
    mags,
    cosines,
    sines,
    w_query,
    w_key,
    w_value,
    first,
    query,
    keys,
    values,
    att,
    lse,
    summed,
    inner_ref,
    norms_ref,
    full_ref,
    gathered,
    ext,
    weights,
    wsem,
    fsem,
    send_sem,
    recv_sem,
):
    me = lax.axis_index("heads")
    row = lax.axis_index("rows")
    total = x_ref.shape[0]
    share = total // count
    loads = [
        pltpu.make_async_copy(source, weights.at[index], wsem.at[index])
        for index, source in enumerate((w_query, w_key, w_value))
    ]
    for load in loads:
        load.start()
    greet(count)
    gain = gain_ref[...].astype(f32)

    @pl.loop(0, total // 128)
    def _(index):
        rows = pl.ds(pl.multiple_of(index * 128, 128), 128)
        normed, _ = norm_value(x_ref[rows, :].astype(f32), gain)
        ext[rows, :] = normed.astype(bf16)

    store_first = pltpu.make_async_copy(ext.at[:total], first, fsem)
    store_first.start()
    inner = nt(ext[:total, :], lth[...]).astype(bf16)
    inner_ref[...] = inner
    heads = query.shape[1] // HEAD_DIM
    for index in range(3):
        block = slice(index * RANK, (index + 1) * RANK)
        ext[total : total + RANK, :] = lth[block, :]
        ext[total + RANK :, :] = ltl[block, :]
        adapters = ext[total:, :]
        gram = nt(adapters, adapters)
        loads[index].wait()
        for start in range(0, query.shape[1], 256):
            columns = slice(start, start + 256)
            weight = weights[index, :, columns]
            product = nn(ext[...], weight)
            local_right = right[index, :, columns]
            squares, full = direction(
                square_sums(weights.at[index], columns), product[total:], gram, local_right
            )
            norms = jnp.sqrt(squares)
            norms_ref[index : index + 1, columns] = norms
            full_ref[index, :, columns] = full
            z = product[:total] + nn(inner, padded_right(local_right, index, 3, SCALE))
            summed[index, :, columns] = z.astype(bf16)
            y = z * (mags[index : index + 1, columns] / norms)
            if index == 2:
                values[:, columns] = y.astype(bf16)
            else:
                for head in range(2):
                    part = y[:, head * HEAD_DIM : (head + 1) * HEAD_DIM]
                    turned = part * cosines[...] + pltpu.roll(part, HEAD_DIM // 2, 1) * sines[...]
                    place = slice(start + head * HEAD_DIM, start + (head + 1) * HEAD_DIM)
                    (query if index == 0 else keys)[:, place] = turned.astype(bf16)

    length = length_ref[0]
    factor = 1.0 / math.sqrt(HEAD_DIM)
    copies = []
    for head in range(heads):
        place = slice(head * HEAD_DIM, (head + 1) * HEAD_DIM)
        turned_values = values[:, place].astype(f32).T.astype(bf16)
        for block in range(total // 256):
            reach = (block + 1) * 256
            at = slice(block * 256, reach)
            scores = nt(keys[:reach, place], query[at, place])
            spots = lax.broadcasted_iota(jnp.int32, (reach, 256), 0)
            asking = lax.broadcasted_iota(jnp.int32, (reach, 256), 1) + block * 256
            allowed = (spots <= asking) & (spots < length)
            scores = jnp.where(allowed, scores * factor, mask_fill)
            peak = jnp.max(scores, axis=0, keepdims=True)
            exps = jnp.exp(scores - peak)
            totals = jnp.sum(exps, axis=0, keepdims=True)
            probs = (exps * (1.0 / totals)).astype(bf16)
            mixed = nn(turned_values[:, :reach], probs)
            att[at, place] = mixed.T.astype(bf16)
            lse[head : head + 1, at] = peak + jnp.log(totals)
        for step in range(1, count):
            peer = lax.rem(me + step, count)
            copy = pltpu.make_async_remote_copy(
                src_ref=att.at[pl.ds(pl.multiple_of(peer * share, share), share), place],
                dst_ref=gathered.at[me, :, place],
                send_sem=send_sem.at[head, step],
                recv_sem=recv_sem.at[head, step],
                device_id=(row, peer),
                device_id_type=MESH,
            )
            copy.start()
            copies.append(copy)
    gathered[me] = att[pl.ds(pl.multiple_of(me * share, share), share), :]
    store_first.wait()
    for copy in copies:
        copy.wait()


def out_forward_kernel(
    gathered, w_full, lth, right, norms, mags, x_ref, gain_ref, middle, second, summed, inner_ref, att
):
    group = gathered.shape[2]
    for index in range(gathered.shape[0]):
        att[:, index * group : (index + 1) * group] = gathered[index]
    x = att[...]
    inner = nt(x, lth[...])
    inner_ref[...] = inner
    low = inner.astype(bf16)
    width = w_full.shape[2]
    for index in range(w_full.shape[0]):
        columns = slice(index * width, (index + 1) * width)
        z = nn(x, w_full[index]) + nn(low, padded_right(right[:, columns], 0, 1, SCALE))
        summed[:, columns] = z
        middle[:, columns] = x_ref[:, columns].astype(f32) + z * (
            mags[:, columns] / norms[:, columns]
        )
    normed, _ = norm_value(middle[...], gain_ref[...].astype(f32))
    second[...] = normed.astype(bf16)


def feed_forward_kernel(
    own,
    cot,
    w_gate_any,
    w_up_any,
    w_down_any,
    lth,
    ltl,
    lt_down,
    right,
    mags,
    right_down,
    mags_down,
    norms_down,
    part,
    grad_second,
    grad_left,
    grad_right,
    grad_mags,
    norms_ref,
    grad_left_down,
    grad_right_down,
    factors,
    w_gate,
    w_up,
    w_down,
    sec,
    cots,
    parts,
    mine,
    outer,
    inner_sums,
    load_sem,
    cot_sem,
    part_sem,
    gather_send,
    gather_recv,
    sum_send,
    outer_recv,
    inner_recv,
):
    row, me = lax.axis_index("rows"), lax.axis_index("heads")
    size, depth = own.shape
    half = size // 2
    inward = jnp.where(me < 2, 1, -1)
    is_end = (me == 0) | (me == 3)
    ahead, behind = me + inward, me - inward

    def move(source, target, send, recv, peer):
        return pltpu.make_async_remote_copy(
            src_ref=source,
            dst_ref=target,
            send_sem=send,
            recv_sem=recv,
            device_id=(row, peer),
            device_id_type=MESH,
        )

    def rows_of(piece):
        return pl.ds(piece * half, half)

    def gather_copy(slot, block, piece, peer):
        place = sec.at[block, rows_of(piece), :]
        return move(place, place, gather_send.at[slot, piece], gather_recv.at[block, piece], peer)

    def gather_start(slot, block, peer):
        for piece in range(2):
            gather_copy(slot, block, piece, peer).start()

    def gather_wait(block, forward=None):
        for piece in range(2):
            gather_copy(0, block, piece, ahead).wait_recv()
            if forward is not None:
                slot, peer = forward
                gather_copy(slot, block, piece, peer).start()

    greet(4)
    loads = [
        pltpu.make_async_copy(source, target, load_sem.at[index])
        for index, (source, target) in enumerate(
            ((w_gate_any, w_gate), (w_up_any, w_up), (w_down_any, w_down))
        )
    ]
    sec[me] = own[...]
    gather_start(0, me, ahead)

    @pl.when(jnp.logical_not(is_end))
    def _():
        gather_start(1, me, behind)

    for load in loads:
        load.start()

    def block_at(step):
        middle = jnp.where(step == 0, me, jnp.where(step == 1, behind, me + inward * (step - 1)))
        return jnp.where(is_end, me + inward * step, middle)

    def cot_load(step):
        at = pl.ds(pl.multiple_of(block_at(step) * size, size), size)
        slot = lax.rem(step, 2)
        return pltpu.make_async_copy(cot.at[at, :], cots.at[slot], cot_sem.at[slot])

    def part_store(step):
        at = pl.ds(pl.multiple_of(block_at(step) * size, size), size)
        slot = lax.rem(step, 2)
        return pltpu.make_async_copy(parts.at[slot], part.at[at, :], part_sem.at[slot])

    cot_load(0).start()
    weights = (w_gate, w_up)
    fulls = []
    for index in range(2):
        loads[index].wait()
        block = slice(index * RANK, (index + 1) * RANK)
        adapters = jnp.concatenate([lth[block, :], ltl[block, :]], axis=0)
        squares, full = direction(
            square_sums(weights[index], slice(0, w_gate.shape[1])),
            nn(adapters, weights[index][...]),
            nt(adapters, adapters),
            right[index],
        )
        norms = jnp.sqrt(squares)
        norms_ref[index : index + 1, :] = norms
        factors[index : index + 1, :] = mags[index : index + 1, :] / norms
        fulls.append(full)
    factor_down = mags_down[...] / norms_down[...]
    grad_left[...] = jnp.zeros_like(grad_left)
    grad_right[...] = jnp.zeros_like(grad_right)
    grad_mags[...] = jnp.zeros_like(grad_mags)
    grad_left_down[...] = jnp.zeros_like(grad_left_down)
    grad_right_down[...] = jnp.zeros_like(grad_right_down)
    loads[2].wait()

    @pl.loop(0, 4)
    def _(step):
        block = block_at(step)
        slot = lax.rem(step, 2)

        @pl.when(step < 3)
        def _():
            cot_load(step + 1).start()

        @pl.when(is_end & (step > 0))
        def _():
            gather_wait(block)

        @pl.when(jnp.logical_not(is_end) & (step == 1))
        def _():
            gather_wait(behind, (2, ahead))
            gather_wait(ahead, (3, behind))

        x = sec[block]
        inner = nt(x, lth[...])
        inner_low = inner.astype(bf16)
        zs = [
            nn(x, weights[index][...])
            + nn(inner_low, padded_right(right[index], index, 2, SCALE))
            for index in range(2)
        ]
        gate = zs[0] * factors[0:1, :]
        upper = zs[1] * factors[1:2, :]
        sigmoid = 1.0 / (1.0 + jnp.exp(-gate))
        activated = gate * sigmoid
        hidden = (activated * upper).astype(bf16)
        right_low = right_down[...].astype(bf16)
        inner_down = nt(hidden, lt_down[:RANK, :])

        @pl.when(step > 1)
        def _():
            part_store(step - 2).wait()

        parts[slot] = (
            nn(hidden, w_down[...]) + SCALE * nn(inner_down.astype(bf16), right_low)
        ).astype(bf16)
        part_store(step).start()

        @pl.when(jnp.logical_not(is_end) & (step == 2))
        def _():
            gather_wait(ahead + inward, (4, behind))

        cot_load(step).wait()
        gz_down = (cots[slot].astype(f32) * factor_down).astype(bf16)
        gin_down = SCALE * nt(gz_down, right_low)
        grad_hidden = nt(gz_down, w_down[...]) + nn(gin_down.astype(bf16), lt_down[:RANK, :])
        grad_left_down[...] += nn(gin_down.T.astype(bf16), hidden)
        grad_right_down[...] += SCALE * nn(inner_down.T.astype(bf16), gz_down)
        grads = (
            grad_hidden * upper * sigmoid * (1.0 + gate * (1.0 - sigmoid)),
            grad_hidden * activated,
        )
        gin = jnp.zeros((size, 2 * RANK), f32)
        gzs = []
        for index in range(2):
            grad_mags[index : index + 1, :] += jnp.sum(grads[index] * zs[index], axis=0, keepdims=True)
            gz = (grads[index] * factors[index : index + 1, :]).astype(bf16)
            gin = gin + nt(gz, padded_right(right[index], index, 2, SCALE))
            gzs.append(gz)
        gin_low = gin.astype(bf16)
        mine[block] = (
            nt(gzs[0], w_gate[...]) + nt(gzs[1], w_up[...]) + nn(gin_low, lth[...])
        ).astype(bf16)

        @pl.when(is_end & (step > 0))
        def _():
            for piece in range(2):
                move(
                    mine.at[block, rows_of(piece), :],
                    outer.at[step - 1, rows_of(piece), :],
                    sum_send.at[step - 1, piece],
                    outer_recv.at[step - 1, piece],
                    ahead,
                ).start()

        grad_left[...] += nn(gin.T.astype(bf16), x)
        inner_turned = inner.T.astype(bf16)
        for index in range(2):
            grad_right[index] += (
                SCALE * nn(inner_turned, gzs[index])[index * RANK : (index + 1) * RANK]
            )

    for index in range(2):
        block = slice(index * RANK, (index + 1) * RANK)
        norms = norms_ref[index : index + 1, :]
        factor_grad = grad_mags[index : index + 1, :]
        shape = -factor_grad * mags[index : index + 1, :] / (norms * norms * norms)
        shaped = right[index] * shape
        pieces = nt(split_rows(shaped), weights[index][...])
        lt = lth[block, :].astype(f32) + ltl[block, :].astype(f32)
        grad_left[block, :] += SCALE * (
            pieces[:RANK]
            + pieces[RANK:]
            + SCALE * nn_exact(nt_exact(shaped, right[index]), lt)
        )
        grad_right[index] += SCALE * fulls[index] * shape
        grad_mags[index : index + 1, :] = factor_grad / norms
    part_store(2).wait()
    part_store(3).wait()

    def outer_copy(slot, piece):
        place = outer.at[slot, rows_of(piece), :]
        return move(place, place, sum_send.at[slot, piece], outer_recv.at[slot, piece], ahead)

    def inner_copy(slot, piece, source, send, peer):
        return move(
            source.at[rows_of(piece), :],
            inner_sums.at[slot, rows_of(piece), :],
            sum_send.at[send, piece],
            inner_recv.at[slot, piece],
            peer,
        )

    def add_into(block, piece, ref):
        at = rows_of(piece)
        mine[block, at, :] = (
            mine[block, at, :].astype(f32) + ref[at, :].astype(f32)
        ).astype(bf16)

    @pl.when(jnp.logical_not(is_end))
    def _():
        for distance in range(1, 3):
            block = me + inward * distance
            for piece in range(2):
                outer_copy(distance, piece).wait_recv()
                add_into(block, piece, outer.at[distance])
                inner_copy(distance - 1, piece, mine.at[block], distance - 1, ahead).start()
        for piece in range(2):
            inner_copy(1, piece, mine.at[behind], 2, behind).wait_recv()
            add_into(behind, piece, inner_sums.at[1])
            inner_copy(0, piece, mine.at[behind], 2, behind).start()
        for piece in range(2):
            outer_copy(0, piece).wait_recv()
            inner_copy(0, piece, mine.at[me], 0, ahead).wait_recv()
        grad_second[...] = (
            mine[me].astype(f32) + outer[0].astype(f32) + inner_sums[0].astype(f32)
        ).astype(f32)
        for piece in range(2):
            inner_copy(0, piece, mine.at[ahead], 0, ahead).wait_send()
            inner_copy(1, piece, mine.at[ahead], 1, ahead).wait_send()
            inner_copy(0, piece, mine.at[behind], 2, behind).wait_send()
            gather_copy(1, me, piece, behind).wait_send()
            gather_copy(2, behind, piece, ahead).wait_send()
            gather_copy(3, ahead, piece, behind).wait_send()
            gather_copy(4, ahead, piece, behind).wait_send()

    @pl.when(is_end)
    def _():
        for piece in range(2):
            inner_copy(0, piece, mine.at[me], 0, ahead).wait_recv()
        grad_second[...] = mine[me].astype(f32) + inner_sums[0].astype(f32)
        for slot in range(3):
            for piece in range(2):
                outer_copy(slot, piece).wait_send()

    for piece in range(2):
        gather_copy(0, me, piece, ahead).wait_send()


def out_back_kernel(
    count,
    grad_second,
    middle,
    cot,
    gain_ref,
    summed,
    gathered,
    inner,
    w_full,
    lth,
    ltl,
    right,
    norms,
    mags,
    full,
    grad_middle,
    mixed,
    grad_left,
    grad_right,
    grad_mags,
    ext,
    back,
    send_sem,
    recv_sem,
):
    me = lax.axis_index("heads")
    row = lax.axis_index("rows")
    greet(count)
    share, depth = middle.shape
    rows = middle[...]
    gain = gain_ref[...].astype(f32)
    inverse = lax.rsqrt(jnp.mean(rows * rows, axis=-1, keepdims=True) + norm_eps)
    scaled = grad_second[...].astype(f32) * gain
    grad = (
        cot[...].astype(f32)
        + inverse * scaled
        - rows * (inverse * inverse * inverse) * jnp.mean(rows * scaled, axis=-1, keepdims=True)
    )
    grad_middle[...] = grad
    norm = norms[...]
    factor_grad = jnp.sum(grad * summed[...], axis=0, keepdims=True)
    shape = -factor_grad * mags[...] / (norm * norm * norm)
    shaped = right[...] * shape
    ext[:share, :] = (grad * (mags[...] / norm)).astype(bf16)
    ext[share:, :] = split_rows(shaped)
    gz = ext[:share, :]
    gin = SCALE * nt(gz, right[...].astype(bf16))
    gin_low = gin.astype(bf16)
    width = w_full.shape[2]
    grad_mags[...] = factor_grad / norm
    grad_right[...] = SCALE * (nn(inner[...].T.astype(bf16), gz) + full[...] * shape)
    gin_turned = gin.T.astype(bf16)
    mixing = nt_exact(shaped, right[...])
    group = depth // count
    copies = []
    for step in range(1, count + 1):
        peer = lax.rem(me + step, count)
        columns = pl.ds(pl.multiple_of(peer * group, group), group)
        total = jnp.zeros((share + 2 * RANK, group), f32)
        for index in range(w_full.shape[0]):
            total = total + nt(
                ext[:, index * width : (index + 1) * width], w_full[index, columns, :]
            )
        result = (total[:share] + nn(gin_low, lth[:, columns])).astype(bf16)
        lt = lth[:, columns].astype(f32) + ltl[:, columns].astype(f32)
        grad_left[:, columns] = nn(gin_turned, gathered[peer]) + SCALE * (
            total[share : share + RANK] + total[share + RANK :] + SCALE * nn_exact(mixing, lt)
        )
        if step == count:
            mixed[me] = result
        else:
            back[peer] = result
            copy = pltpu.make_async_remote_copy(
                src_ref=back.at[peer],
                dst_ref=mixed.at[me],
                send_sem=send_sem.at[step],
                recv_sem=recv_sem.at[step],
                device_id=(row, peer),
                device_id_type=MESH,
            )
            copy.start()
            copies.append(copy)
    for copy in copies:
        copy.wait()


def attention_back_kernel(
    length_ref,
    query,
    keys,
    values,
    att,
    lse,
    mixed,
    first,
    summed,
    norms_ref,
    mags,
    fulls,
    inner,
    lth,
    ltl,
    right,
    cosines,
    sines,
    w_query,
    w_key,
    w_value,
    grad_first,
    grad_left,
    grad_right,
    grad_mags,
    gz,
    key_sums,
    value_sums,
    query_turned,
    factors,
):
    total = query.shape[0]
    heads = query.shape[1] // HEAD_DIM
    length = length_ref[0]
    factor = 1.0 / math.sqrt(HEAD_DIM)
    factors[...] = mags[...] / norms_ref[...]

    def finish(index, head, grad):
        place = slice(head * HEAD_DIM, (head + 1) * HEAD_DIM)
        if index < 2:
            grad = grad * cosines[...] - pltpu.roll(grad, HEAD_DIM // 2, 1) * sines[...]
        grad_mags[index : index + 1, place] = jnp.sum(
            grad * summed[index, :, place].astype(f32), axis=0, keepdims=True
        )
        gz[index, :, place] = (grad * factors[index : index + 1, place]).astype(bf16)

    for head in range(heads):
        place = slice(head * HEAD_DIM, (head + 1) * HEAD_DIM)
        turned_keys = keys[:, place].astype(f32).T.astype(bf16)
        key_sums[...] = jnp.zeros_like(key_sums)
        value_sums[...] = jnp.zeros_like(value_sums)
        for block in range(total // 256):
            reach = (block + 1) * 256
            at = slice(block * 256, reach)
            grad_rows = mixed[at, place]
            rows = query[at, place]
            scores = nt(keys[:reach, place], rows)
            spots = lax.broadcasted_iota(jnp.int32, (reach, 256), 0)
            asking = lax.broadcasted_iota(jnp.int32, (reach, 256), 1) + block * 256
            allowed = (spots <= asking) & (spots < length)
            scores = jnp.where(allowed, scores * factor, mask_fill)
            probs = jnp.exp(scores - lse[head : head + 1, at])
            grad_probs = nt(values[:reach, place], grad_rows)
            centre = jnp.sum(
                (grad_rows.astype(f32) * att[at, place].astype(f32)).T, axis=0, keepdims=True
            )
            raw = (probs * (grad_probs - centre) * factor).astype(bf16)
            value_sums[:reach, :] += nn(probs.astype(bf16), grad_rows)
            key_sums[:reach, :] += nn(raw, rows)
            query_turned[:, at] = nn(turned_keys[:, :reach], raw)
        finish(0, head, query_turned[...].T)
        finish(1, head, key_sums[...])
        finish(2, head, value_sums[...])

    weights = (w_query, w_key, w_value)
    gin = jnp.zeros((total, 3 * RANK), f32)
    for index in range(3):
        gin = gin + nt(gz[index], padded_right(right[index], index, 3, SCALE))
    gin_low = gin.astype(bf16)
    grad_left[...] = nn(gin.T.astype(bf16), first[...])
    inner_turned = inner[...].astype(f32).T.astype(bf16)
    for index in range(3):
        block = slice(index * RANK, (index + 1) * RANK)
        norms = norms_ref[index : index + 1, :]
        factor_grad = grad_mags[index : index + 1, :]
        shape = -factor_grad * mags[index : index + 1, :] / (norms * norms * norms)
        shaped = right[index] * shape
        pieces = nt(split_rows(shaped), weights[index][...])
        lt = lth[block, :].astype(f32) + ltl[block, :].astype(f32)
        grad_left[block, :] += SCALE * (
            pieces[:RANK]
            + pieces[RANK:]
            + SCALE * nn_exact(nt_exact(shaped, right[index]), lt)
        )
        grad_right[index] = SCALE * (nn(inner_turned, gz[index])[block] + fulls[index] * shape)
        grad_mags[index : index + 1, :] = factor_grad / norms
    for block in range(total // 256):
        at = slice(block * 256, (block + 1) * 256)
        grad_first[at, :] = (
            nt(gz[0, at, :], w_query[...])
            + nt(gz[1, at, :], w_key[...])
            + nt(gz[2, at, :], w_value[...])
            + nn(gin_low[at, :], lth[...])
        ).astype(bf16)


def call(kernel, outs, ins, specs=None, out_specs=None, scratch=(), flops=0, moved=0, collective=None):
    extra = {} if collective is None else {"collective_id": collective, "has_side_effects": True}
    return pl.pallas_call(
        kernel,
        out_shape=[jax.ShapeDtypeStruct(shape, kind) for shape, kind in outs],
        in_specs=specs or [VMEM] * len(ins),
        out_specs=out_specs or [VMEM] * len(outs),
        scratch_shapes=list(scratch),
        cost_estimate=pl.CostEstimate(flops=flops, bytes_accessed=moved, transcendentals=0),
        compiler_params=pltpu.CompilerParams(vmem_limit_bytes=LIMIT, **extra),
    )(*ins)


def rope_tables(length, width):
    half = width // 2
    freqs = rope_base ** (-(jnp.arange(half, dtype=f32) * 2.0) / width)
    angles = jnp.arange(length, dtype=f32)[:, None] * freqs[None, :]
    sines = jnp.sin(angles)
    return jnp.tile(jnp.cos(angles), (1, 2)), jnp.concatenate([-sines, sines], axis=1)


def pieces_of(turned):
    high = lax.reduce_precision(turned, 8, 7)
    return high.astype(bf16), (turned - high).astype(bf16)


def local(
    inputs,
    cotangent,
    lengths,
    gain_attn,
    gain_mlp,
    w_query,
    w_key,
    w_value,
    w_out,
    w_gate,
    w_up,
    w_down,
    qkv_left,
    qkv_right,
    qkv_mags,
    mlp_left,
    mlp_right,
    mlp_mags,
    out_left,
    down_left,
    exit_right,
    out_mags,
    down_mags,
):
    count = lax.axis_size("heads")
    teams = lax.axis_size("rows")
    total, depth = inputs.shape
    share = total // count
    group = w_query.shape[1]
    units = w_gate.shape[1]
    heads = group // HEAD_DIM
    me = lax.axis_index("heads")
    offset = me * share
    both = ("rows", "heads")

    width = depth // teams
    piece = lax.dynamic_slice_in_dim(w_out, lax.axis_index("rows") * width, width, 1)
    piece = lax.all_gather(piece, "heads", axis=0, tiled=True)
    w_full = lax.all_gather(piece, "rows", axis=0)
    if width < 256:
        merge = 256 // width
        w_full = (
            w_full.reshape(teams // merge, merge, depth, width)
            .transpose(0, 2, 1, 3)
            .reshape(teams // merge, depth, 256)
        )
    lt_qkv, ltl_qkv = pieces_of(jnp.transpose(qkv_left, (0, 2, 1)).reshape(3 * RANK, depth))
    lt_mlp, ltl_mlp = pieces_of(jnp.transpose(mlp_left, (0, 2, 1)).reshape(2 * RANK, depth))
    lt_down = jnp.concatenate(pieces_of(down_left.T), axis=0)
    turned_out = out_left.T
    lt_out_local = jnp.concatenate(pieces_of(turned_out), axis=0)
    lt_out, ltl_out = pieces_of(lax.all_gather(turned_out, "heads", axis=1, tiled=True))
    cosines, sines = rope_tables(total, HEAD_DIM)
    gain_first = gain_attn.reshape(1, depth)
    gain_second = gain_mlp.reshape(1, depth)
    out_mag, down_mag = out_mags.reshape(1, depth), down_mags.reshape(1, depth)

    (stats,) = call(
        exit_stats_kernel,
        [((2 * RANK + 8, depth), f32)],
        (w_out, w_down, lt_out_local, lt_down, exit_right),
        flops=2 * 256 * (group + units) * depth,
        moved=2 * (group + units) * depth,
    )
    stats = lax.psum(stats, "heads")
    full_out, full_down = stats[:RANK], stats[RANK : 2 * RANK]
    exit_norms = jnp.sqrt(stats[2 * RANK : 2 * RANK + 2])
    out_norms, down_norms = exit_norms[0:1], exit_norms[1:2]

    (
        first,
        query,
        keys,
        values,
        att,
        lse,
        qkv_summed,
        qkv_inner,
        qkv_norms,
        qkv_full,
        gathered,
    ) = call(
        functools.partial(attention_forward_kernel, count),
        [
            ((total, depth), bf16),
            ((total, group), bf16),
            ((total, group), bf16),
            ((total, group), bf16),
            ((total, group), bf16),
            ((heads, total), f32),
            ((3, total, group), bf16),
            ((total, 3 * RANK), bf16),
            ((3, group), f32),
            ((3, RANK, group), f32),
            ((count, share, group), bf16),
        ],
        (
            lengths,
            inputs,
            gain_first,
            lt_qkv,
            ltl_qkv,
            qkv_right,
            qkv_mags,
            cosines,
            sines,
            w_query,
            w_key,
            w_value,
        ),
        specs=[SMEM] + [VMEM] * 8 + [ANY] * 3,
        out_specs=[ANY] + [VMEM] * 10,
        scratch=(
            pltpu.VMEM((total + 2 * RANK, depth), bf16),
            pltpu.VMEM((3, depth, group), bf16),
            pltpu.SemaphoreType.DMA((3,)),
            pltpu.SemaphoreType.DMA,
            pltpu.SemaphoreType.DMA((heads, count)),
            pltpu.SemaphoreType.DMA((heads, count)),
        ),
        flops=6 * total * depth * group + 4 * total * total * group,
        moved=2 * (2 * total * depth + 3 * depth * group + 8 * total * group),
        collective=0,
    )

    x_own = lax.dynamic_slice_in_dim(inputs, offset, share, 0)
    cot_own = lax.dynamic_slice_in_dim(cotangent, offset, share, 0)
    middle, second, out_summed, out_inner = call(
        out_forward_kernel,
        [
            ((share, depth), f32),
            ((share, depth), bf16),
            ((share, depth), f32),
            ((share, RANK), f32),
        ],
        (gathered, w_full, lt_out, exit_right[0], out_norms, out_mag, x_own, gain_second),
        scratch=(pltpu.VMEM((share, depth), bf16),),
        flops=2 * share * depth * depth,
        moved=2 * depth * depth,
    )
    assert count == 4
    (
        part,
        grad_second_own,
        grad_mlp_left,
        grad_mlp_right,
        grad_mlp_mags,
        mlp_norms,
        grad_down_left,
        grad_down_right,
    ) = call(
        feed_forward_kernel,
        [
            ((total, depth), bf16),
            ((share, depth), f32),
            ((2 * RANK, depth), f32),
            ((2, RANK, units), f32),
            ((2, units), f32),
            ((2, units), f32),
            ((RANK, units), f32),
            ((RANK, depth), f32),
        ],
        (
            second,
            cotangent,
            w_gate,
            w_up,
            w_down,
            lt_mlp,
            ltl_mlp,
            lt_down,
            mlp_right,
            mlp_mags,
            exit_right[1],
            down_mag,
            down_norms,
        ),
        specs=[VMEM] + [ANY] * 4 + [VMEM] * 8,
        out_specs=[ANY] + [VMEM] * 7,
        scratch=(
            pltpu.VMEM((2, units), f32),
            pltpu.VMEM((depth, units), bf16),
            pltpu.VMEM((depth, units), bf16),
            pltpu.VMEM((units, depth), bf16),
            pltpu.VMEM((count, share, depth), bf16),
            pltpu.VMEM((2, share, depth), bf16),
            pltpu.VMEM((2, share, depth), bf16),
            pltpu.VMEM((count, share, depth), bf16),
            pltpu.VMEM((3, share, depth), bf16),
            pltpu.VMEM((2, share, depth), bf16),
            pltpu.SemaphoreType.DMA((3,)),
            pltpu.SemaphoreType.DMA((2,)),
            pltpu.SemaphoreType.DMA((2,)),
            pltpu.SemaphoreType.DMA((5, 2)),
            pltpu.SemaphoreType.DMA((4, 2)),
            pltpu.SemaphoreType.DMA((3, 2)),
            pltpu.SemaphoreType.DMA((3, 2)),
            pltpu.SemaphoreType.DMA((2, 2)),
        ),
        flops=12 * total * depth * units,
        moved=2 * (3 * depth * units + 4 * total * depth),
        collective=2,
    )
    down_own = lax.psum_scatter(part, "heads", scatter_dimension=0, tiled=True).astype(f32)

    grad_middle, mixed, grad_out_left, grad_out_right, grad_out_mags = call(
        functools.partial(out_back_kernel, count),
        [
            ((share, depth), f32),
            ((count, share, group), bf16),
            ((RANK, depth), f32),
            ((RANK, depth), f32),
            ((1, depth), f32),
        ],
        (
            grad_second_own,
            middle,
            cot_own,
            gain_second,
            out_summed,
            gathered,
            out_inner,
            w_full,
            lt_out,
            ltl_out,
            exit_right[0],
            out_norms,
            out_mag,
            full_out,
        ),
        scratch=(
            pltpu.VMEM((share + 2 * RANK, depth), bf16),
            pltpu.VMEM((count, share, group), bf16),
            pltpu.SemaphoreType.DMA((count,)),
            pltpu.SemaphoreType.DMA((count,)),
        ),
        flops=2 * share * depth * depth,
        moved=2 * depth * depth,
        collective=1,
    )

    grad_first, grad_qkv_left, grad_qkv_right, grad_qkv_mags = call(
        attention_back_kernel,
        [
            ((total, depth), bf16),
            ((3 * RANK, depth), f32),
            ((3, RANK, group), f32),
            ((3, group), f32),
        ],
        (
            lengths,
            query,
            keys,
            values,
            att,
            lse,
            mixed.reshape(total, group),
            first,
            qkv_summed,
            qkv_norms,
            qkv_mags,
            qkv_full,
            qkv_inner,
            lt_qkv,
            ltl_qkv,
            qkv_right,
            cosines,
            sines,
            w_query,
            w_key,
            w_value,
        ),
        specs=[SMEM] + [VMEM] * 20,
        scratch=(
            pltpu.VMEM((3, total, group), bf16),
            pltpu.VMEM((total, HEAD_DIM), f32),
            pltpu.VMEM((total, HEAD_DIM), f32),
            pltpu.VMEM((HEAD_DIM, total), f32),
            pltpu.VMEM((3, group), f32),
        ),
        flops=6 * total * depth * group + 10 * total * total * group,
        moved=2 * (2 * total * depth + 3 * depth * group + 8 * total * group),
    )
    grad_first_own = lax.psum_scatter(grad_first, "heads", scatter_dimension=0, tiled=True)

    x = x_own.astype(f32)
    scaled = grad_first_own.astype(f32) * gain_attn.astype(f32)
    inverse = lax.rsqrt(jnp.mean(x * x, axis=-1, keepdims=True) + norm_eps)
    input_grad = (
        grad_middle
        + inverse * scaled
        - x * (inverse * inverse * inverse) * jnp.mean(x * scaled, axis=-1, keepdims=True)
    )

    outputs = (middle + down_own * (down_mag / down_norms)).astype(bf16)
    down_factor_grad = lax.psum(
        jnp.sum(cot_own.astype(f32) * down_own, axis=0, keepdims=True), both
    )
    shape = -down_factor_grad * down_mag / (down_norms * down_norms * down_norms)
    shaped = exit_right[1] * shape
    high, low = pieces_of(shaped)
    extra_left = SCALE * (
        jnp.dot(high, w_down.T, preferred_element_type=f32)
        + jnp.dot(low, w_down.T, preferred_element_type=f32)
        + SCALE
        * jnp.dot(
            jnp.dot(shaped, exit_right[1].T, precision=lax.Precision.HIGHEST),
            down_left.T,
            precision=lax.Precision.HIGHEST,
        )
    )

    sums = lax.psum(
        (
            jnp.concatenate([grad_qkv_left, grad_mlp_left, grad_out_right, grad_down_right, grad_out_left]),
            grad_out_mags,
        ),
        both,
    )
    whole, grad_out_mags = sums
    grad_qkv_left = jnp.transpose(whole[: 3 * RANK].reshape(3, RANK, depth), (0, 2, 1))
    grad_mlp_left = jnp.transpose(
        whole[3 * RANK : 5 * RANK].reshape(2, RANK, depth), (0, 2, 1)
    )
    grad_exit_right = jnp.stack(
        [whole[5 * RANK : 6 * RANK], whole[6 * RANK : 7 * RANK] + SCALE * full_down * shape]
    )
    grad_out_left = lax.dynamic_slice_in_dim(whole[7 * RANK :], me * group, group, 1).T
    grad_qkv_right, grad_qkv_mags, grad_mlp_right, grad_mlp_mags, grad_down_left = [
        lax.psum(item.astype(bf16), "rows").astype(f32)
        for item in (grad_qkv_right, grad_qkv_mags, grad_mlp_right, grad_mlp_mags, grad_down_left)
    ]
    grad_down_left = (grad_down_left + extra_left).T

    qkv_stats = jnp.stack([qkv_norms, qkv_mags - qkv_norms]).astype(bf16)
    mlp_stats = jnp.stack([mlp_norms, mlp_mags - mlp_norms]).astype(bf16)
    qkv_table = lax.all_gather(qkv_stats, "heads", axis=2, tiled=True).astype(f32)
    mlp_table = lax.all_gather(mlp_stats, "heads", axis=2, tiled=True).astype(f32)
    exit_stats = jnp.stack([exit_norms, jnp.stack([out_mags, down_mags]) - exit_norms])
    norm_stats = jnp.concatenate(
        [qkv_table.reshape(2, -1), mlp_table.reshape(2, -1), exit_stats.reshape(2, -1)], axis=1
    )
    return (
        outputs,
        input_grad,
        grad_qkv_left,
        grad_qkv_right,
        grad_qkv_mags,
        grad_mlp_left,
        grad_mlp_right,
        grad_mlp_mags,
        grad_out_left,
        grad_down_left,
        grad_exit_right,
        grad_out_mags.reshape(depth),
        (down_factor_grad / down_norms).reshape(depth),
        norm_stats,
    )


def solution(mesh):
    placed = (
        P("rows", None),
        P("rows", None),
        P("rows"),
        P(),
        P(),
        P(None, "heads"),
        P(None, "heads"),
        P(None, "heads"),
        P("heads", None),
        P(None, "heads"),
        P(None, "heads"),
        P("heads", None),
        P(),
        P(None, None, "heads"),
        P(None, "heads"),
        P(),
        P(None, None, "heads"),
        P(None, "heads"),
        P("heads", None),
        P("heads", None),
        P(),
        P(),
        P(),
    )
    return jax.shard_map(
        local,
        mesh=mesh,
        in_specs=placed,
        out_specs=(
            P(("rows", "heads"), None),
            P(("rows", "heads"), None),
            P(),
            P(None, None, "heads"),
            P(None, "heads"),
            P(),
            P(None, None, "heads"),
            P(None, "heads"),
            P("heads", None),
            P("heads", None),
            P(),
            P(),
            P(),
            P(),
        ),
        check_vma=False,
    )
```

```python
import functools
import math

import jax
import jax.numpy as jnp
import numpy as np
from jax import lax
from jax.experimental import pallas as pl
from jax.experimental.pallas import tpu as pltpu
from jax.sharding import PartitionSpec as P

HEAD_DIM = 128
RANK = 16
norm_eps = 1e-05
rope_base = 10000.0
mask_fill = -1e30
SCALE = 32.0 / RANK

f32 = jnp.float32
bf16 = jnp.bfloat16
MESH = pl.DeviceIdType.MESH
VMEM = pl.BlockSpec(memory_space=pltpu.VMEM)
SMEM = pl.BlockSpec(memory_space=pltpu.SMEM)
ANY = pl.BlockSpec(memory_space=pl.ANY)
LIMIT = 63 << 20
PIECES = 4


def nn(left, right):
    return jnp.dot(left, right, preferred_element_type=f32)


def nt(left, right):
    return lax.dot_general(left, right, (((1,), (1,)), ((), ())), preferred_element_type=f32)


def nn_exact(left, right):
    return jnp.dot(left, right, precision=lax.Precision.HIGHEST, preferred_element_type=f32)


def nt_exact(left, right):
    return lax.dot_general(
        left,
        right,
        (((1,), (1,)), ((), ())),
        precision=lax.Precision.HIGHEST,
        preferred_element_type=f32,
    )


def split_rows(field):
    high = field.astype(bf16)
    return jnp.concatenate([high, (field - high.astype(f32)).astype(bf16)], axis=0)


def square_sums(ref, columns, chunk=128):
    depth = ref.shape[0]
    width = columns.size if isinstance(columns, pl.Slice) else columns.stop - columns.start

    def step(index, total):
        piece = ref[pl.ds(pl.multiple_of(index * chunk, chunk), chunk), columns].astype(f32)
        return total + jnp.sum((piece * piece).reshape(chunk // 8, 8, width), axis=0)

    total = lax.fori_loop(0, depth // chunk, step, jnp.zeros((8, width), f32))
    return jnp.sum(total, axis=0, keepdims=True)


def direction(squares, pieces, gram, right):
    plain = pieces[:RANK] + pieces[RANK:]
    turned = nn_exact(gram, jnp.concatenate([right, right], axis=0))
    full = plain + SCALE * (turned[:RANK] + turned[RANK:])
    return squares + SCALE * jnp.sum(right * (plain + full), axis=0, keepdims=True), full


def padded_right(right, at, count, factor):
    low = factor * right.astype(bf16).astype(f32)
    zero = jnp.zeros_like(low)
    return jnp.concatenate([low if slot == at else zero for slot in range(count)], axis=0).astype(bf16)


def norm_value(rows, gain):
    inverse = lax.rsqrt(jnp.mean(rows * rows, axis=-1, keepdims=True) + norm_eps)
    return rows * inverse * gain, inverse


def turning(angles):
    swapped = pltpu.roll(angles, HEAD_DIM // 2, 1)
    first = lax.broadcasted_iota(jnp.int32, angles.shape, 1) < HEAD_DIM // 2
    return jnp.where(first, angles, swapped), jnp.where(first, -swapped, angles)


def greet(count):
    row, me = lax.axis_index("rows"), lax.axis_index("heads")
    barrier = pltpu.get_barrier_semaphore()
    for step in range(1, count):
        pl.semaphore_signal(
            barrier, inc=1, device_id=(row, lax.rem(me + step, count)), device_id_type=MESH
        )
    pl.semaphore_wait(barrier, count - 1)


def attention_forward_kernel(
    count,
    teams,
    length_ref,
    gain_ref,
    lt,
    right,
    mags,
    angles,
    lt_out,
    lt_down,
    right_exit,
    mags_out,
    gain_second,
    x_any,
    w_query,
    w_key,
    w_value,
    w_out,
    w_down_any,
    first,
    query_any,
    keys_any,
    values_any,
    att_any,
    summed_any,
    w_full,
    lse,
    inner_ref,
    norms_ref,
    full_ref,
    gathered,
    middle,
    second,
    summed_out,
    inner_out,
    full_out,
    lt_full,
    exit_norms,
    full_down,
    ext,
    weights,
    query,
    keys,
    values,
    att,
    summed,
    wf,
    w_down,
    x_own,
    ext_out,
    lt_in,
    squares_in,
    down_in,
    load_sem,
    store_sem,
    send_sem,
    recv_sem,
    line_send,
    line_recv,
    team_send,
    team_recv,
    small_send,
    small_recv,
):
    team, me = lax.axis_index("rows"), lax.axis_index("heads")
    total, depth = x_any.shape
    share = total // count
    group = query.shape[1]
    heads = group // HEAD_DIM
    deep = wf.shape[2]
    bits = teams.bit_length() - 1

    def move(source, target, send, recv, peer_team, peer):
        return pltpu.make_async_remote_copy(
            src_ref=source,
            dst_ref=target,
            send_sem=send,
            recv_sem=recv,
            device_id=(peer_team, peer),
            device_id_type=MESH,
        )

    def flip(index, bit):
        weight = 1 << bit
        return index + weight - 2 * weight * lax.rem(index // weight, 2)

    x_load = pltpu.make_async_copy(x_any, ext.at[:total], load_sem.at[0])
    own_load = pltpu.make_async_copy(
        x_any.at[pl.ds(pl.multiple_of(me * share, share), share), :], x_own, load_sem.at[1]
    )
    loads = [
        pltpu.make_async_copy(source, weights.at[index], load_sem.at[2 + index])
        for index, source in enumerate((w_query, w_key, w_value))
    ]
    shard_loads = [
        pltpu.make_async_copy(
            w_out.at[index * deep : (index + 1) * deep, :], wf.at[me, index], load_sem.at[6 + index]
        )
        for index in range(teams)
    ]
    down_load = pltpu.make_async_copy(w_down_any, w_down, load_sem.at[5])
    x_load.start()
    for load in loads:
        load.start()
    own_load.start()

    barrier = pltpu.get_barrier_semaphore()
    for step in range(1, count):
        pl.semaphore_signal(
            barrier, inc=1, device_id=(team, lax.rem(me + step, count)), device_id_type=MESH
        )
    for bit in range(bits):
        pl.semaphore_signal(barrier, inc=1, device_id=(flip(team, bit), me), device_id_type=MESH)
    pl.semaphore_wait(barrier, count - 1 + bits)

    def line_copy(step):
        peer = lax.rem(me + step, count)
        return move(
            w_out.at[pl.ds(pl.multiple_of(team * deep, deep), deep), :],
            wf.at[me, team],
            line_send.at[step],
            line_recv.at[step],
            team,
            peer,
        )

    for step in range(1, count):
        line_copy(step).start()

    half = depth // 2
    outer_bits = list(range(1, bits))
    rounds = []
    slot = 0
    for stage in range(bits - 1):
        copies = []
        for side, order in enumerate((outer_bits, outer_bits[::-1])):
            held = [team]
            for bit in order[:stage]:
                held = held + [flip(index, bit) for index in held]
            for index in held:
                for step in range(1, count):
                    copies.append((slot, index, side, step, order[stage]))
                    slot += 1
        rounds.append(copies)
    held = [team]
    for bit in outer_bits:
        held = held + [flip(index, bit) for index in held]
    copies = []
    for index in held:
        for step in range(1, count):
            copies.append((slot, index, None, step, 0))
            slot += 1
    rounds.append(copies)

    def team_copy(entry):
        slot, index, side, step, bit = entry
        block = lax.rem(me + step, count)
        if side is None:
            place = wf.at[block, index]
        else:
            place = wf.at[block, index, :, side * half : (side + 1) * half]
        return move(place, place, team_send.at[slot], team_recv.at[slot], flip(team, bit), me)

    def advance(stage, distance):
        if stage == 0:
            line_copy(distance).wait_recv()
        else:
            for entry in rounds[stage - 1]:
                if entry[3] == count - distance:
                    team_copy(entry).wait_recv()
        if stage < len(rounds):
            for entry in rounds[stage]:
                if entry[3] == count - distance:
                    team_copy(entry).start()

    order = sorted(
        ((stage, distance) for stage in range(len(rounds) + 1) for distance in range(1, count)),
        key=lambda item: (2 * item[0] + 3 * item[1], item[0]),
    )

    def progress(steps):
        for _ in range(steps):
            if order:
                advance(*order.pop(0))

    def small_copy(kind, step):
        ref = (lt_in, squares_in, down_in)[kind]
        return move(
            ref.at[me],
            ref.at[me],
            small_send.at[kind, step],
            small_recv.at[kind, step],
            team,
            lax.rem(me + step, count),
        )

    lt_in[me] = lt_out[...]
    for step in range(1, count):
        small_copy(0, step).start()

    gain = gain_ref[...].astype(f32)
    x_load.wait()

    @pl.loop(0, total // 128)
    def _(index):
        rows = pl.ds(pl.multiple_of(index * 128, 128), 128)
        normed, _ = norm_value(ext[rows, :].astype(f32), gain)
        ext[rows, :] = normed.astype(bf16)

    stores = [pltpu.make_async_copy(ext.at[:total], first, store_sem.at[0])]
    stores[0].start()
    for load in shard_loads:
        load.start()
    down_load.start()
    inner = nt(ext[:total, :], lt[...].astype(bf16)).astype(bf16)
    inner_ref[...] = inner
    for index in range(3):
        block = slice(index * RANK, (index + 1) * RANK)
        adapters = split_rows(lt[block, :])
        ext[total:, :] = adapters
        gram = nt(adapters, adapters)
        loads[index].wait()
        for start in range(0, group, 256):
            columns = slice(start, start + 256)
            product = nn(ext[...], weights[index, :, columns])
            local_right = right[index, :, columns]
            squares, full = direction(
                square_sums(weights.at[index], columns), product[total:], gram, local_right
            )
            norms = jnp.sqrt(squares)
            norms_ref[index : index + 1, columns] = norms
            full_ref[index, :, columns] = full
            z = product[:total] + nn(inner, padded_right(local_right, index, 3, SCALE))
            summed[index, :, columns] = z.astype(bf16)
            y = z * (mags[index : index + 1, columns] / norms)
            if index > 0:
                progress(1)
            if index == 2:
                values[:, columns] = y.astype(bf16)
            else:
                for head in range(2):
                    part = y[:, head * HEAD_DIM : (head + 1) * HEAD_DIM]
                    cosines, sines = turning(angles[...])
                    turned = part * cosines + pltpu.roll(part, HEAD_DIM // 2, 1) * sines
                    place = slice(start + head * HEAD_DIM, start + (head + 1) * HEAD_DIM)
                    (query if index == 0 else keys)[:, place] = turned.astype(bf16)
    for source, target in (
        (summed, summed_any),
        (query, query_any),
        (keys, keys_any),
        (values, values_any),
    ):
        stores.append(pltpu.make_async_copy(source, target, store_sem.at[len(stores)]))
        stores[-1].start()
    length = length_ref[0]
    factor = 1.0 / math.sqrt(HEAD_DIM)
    copies = []
    for head in range(heads):
        place = slice(head * HEAD_DIM, (head + 1) * HEAD_DIM)
        turned_values = values[:, place].astype(f32).T.astype(bf16)
        for block in range(total // 256):
            reach = (block + 1) * 256
            at = slice(block * 256, reach)
            scores = nt(keys[:reach, place], query[at, place])
            spots = lax.broadcasted_iota(jnp.int32, (reach, 256), 0)
            asking = lax.broadcasted_iota(jnp.int32, (reach, 256), 1) + block * 256
            allowed = (spots <= asking) & (spots < length)
            scores = jnp.where(allowed, scores * factor, mask_fill)
            peak = jnp.max(scores, axis=0, keepdims=True)
            exps = jnp.exp(scores - peak)
            totals = jnp.sum(exps, axis=0, keepdims=True)
            probs = (exps * (1.0 / totals)).astype(bf16)
            mixed = nn(turned_values[:, :reach], probs)
            att[at, place] = mixed.T.astype(bf16)
            lse[head : head + 1, at] = peak + jnp.log(totals)
        for step in range(1, count):
            peer = lax.rem(me + step, count)
            copy = move(
                att.at[pl.ds(pl.multiple_of(peer * share, share), share), place],
                gathered.at[me, :, place],
                send_sem.at[head, step],
                recv_sem.at[head, step],
                team,
                peer,
            )
            copy.start()
            copies.append(copy)
        progress(2)
    gathered[me] = att[pl.ds(pl.multiple_of(me * share, share), share), :]
    stores.append(pltpu.make_async_copy(att, att_any, store_sem.at[5]))
    stores[-1].start()

    for load in shard_loads:
        load.wait()
    down_load.wait()
    squares_in[me] = jnp.zeros((8, depth), f32)
    for index, (pieces, chunk) in enumerate(((lt_out[...], 64), (lt_down[...], 128))):
        adapters = split_rows(pieces)
        gram = nt(adapters, adapters)
        for start in range(0, depth, 512):
            columns = slice(start, start + 512)
            if index == 0:
                weight = wf[me, :, :, columns].reshape(group, 512)
                low = weight.astype(f32)
                sums = jnp.sum(low * low, axis=0, keepdims=True)
            else:
                weight = w_down[:, columns]
                sums = square_sums(w_down, columns)
            squares, full = direction(
                sums, nn(adapters, weight), gram, right_exit[index, :, columns]
            )
            squares_in[me, index : index + 1, columns] = squares
            if index == 1:
                down_in[me, :, columns] = full.astype(bf16)
    for step in range(1, count):
        small_copy(1, step).start()
        small_copy(2, step).start()
    for step in range(1, count):
        small_copy(0, step).wait()
    for index in range(count):
        lt_full[:, index * group : (index + 1) * group] = lt_in[index]
    for copy in copies:
        copy.wait()
    for index in range(count):
        ext_out[:share, index * group : (index + 1) * group] = gathered[index]
    adapters = split_rows(lt_full[...])
    ext_out[share:, :] = adapters
    gram = nt(adapters, adapters)
    inner_low = adapters[:RANK]
    inner = nt(ext_out[:share, :], inner_low)
    inner_out[...] = inner
    low = inner.astype(bf16)
    own_load.wait()
    for step in range(1, count):
        small_copy(1, step).wait()
        small_copy(2, step).wait()
    squares = squares_in[0]
    full = down_in[0].astype(f32)
    for index in range(1, count):
        squares = squares + squares_in[index]
        full = full + down_in[index].astype(f32)
    exit_norms[...] = jnp.sqrt(squares[0:2])
    full_down[...] = full
    progress(len(order))
    store_full = [
        pltpu.make_async_copy(
            wf.at[index // teams, index % teams],
            w_full.at[index * deep : (index + 1) * deep, :],
            store_sem.at[6 + index],
        )
        for index in range(count * teams)
    ]
    for store in store_full:
        store.start()
    for start in range(0, depth, 512):
        columns = slice(start, start + 512)
        weight = wf[:, :, :, columns].reshape(depth, 512)
        local_right = right_exit[0, :, columns]
        product = nn(ext_out[...], weight)
        _, full = direction(0.0, product[share:], gram, local_right)
        full_out[:, columns] = full
        z = product[:share] + nn(low, padded_right(local_right, 0, 1, SCALE))
        summed_out[:, columns] = z.astype(bf16)
        middle[:, columns] = x_own[:, columns].astype(f32) + z * (
            mags_out[:, columns] / exit_norms[0:1, columns]
        )
    normed, _ = norm_value(middle[...], gain_second[...].astype(f32))
    second[...] = normed.astype(bf16)
    for store in stores + store_full:
        store.wait()
    for step in range(1, count):
        line_copy(step).wait_send()
    for copies in rounds:
        for entry in copies:
            team_copy(entry).wait_send()


def feed_forward_kernel(
    own,
    cot,
    w_gate_any,
    w_up_any,
    w_down_any,
    lt_pair,
    lt_down_pair,
    right,
    mags,
    right_down,
    mags_down,
    norms_down,
    norms_qkv,
    mags_qkv,
    norms_out,
    mags_out,
    gain_ref,
    inner_out,
    lt_out,
    right_out,
    full_out,
    middle_any,
    summed_any,
    gathered_any,
    w_full_any,
    part,
    early,
    early_rows,
    norm_table,
    grad_middle,
    mixed,
    early_out,
    early_mags,
    grad_second,
    adapted,
    lth,
    lt_down,
    norms_ref,
    factors,
    w_gate,
    w_up,
    w_down,
    sec,
    cots,
    cot_own,
    parts,
    mine,
    outer,
    inner_sums,
    near,
    tables,
    load_sem,
    cot_sem,
    part_sem,
    gather_send,
    gather_recv,
    sum_send,
    outer_recv,
    inner_recv,
    near_send,
    near_recv,
    table_send,
    table_recv,
    exit_sem,
    own_sem,
    mixed_send,
    mixed_recv,
):
    row, me = lax.axis_index("rows"), lax.axis_index("heads")
    size, depth = own.shape
    half = size // PIECES
    inward = jnp.where(me < 2, 1, -1)
    is_end = (me == 0) | (me == 3)
    in_middle = jnp.logical_not(is_end)
    ahead, behind = me + inward, me - inward

    def move(source, target, send, recv, peer):
        return pltpu.make_async_remote_copy(
            src_ref=source,
            dst_ref=target,
            send_sem=send,
            recv_sem=recv,
            device_id=(row, peer),
            device_id_type=MESH,
        )

    def rows_of(piece):
        return pl.ds(piece * half, half)

    def gather_copy(slot, block, piece, peer):
        place = sec.at[block, rows_of(piece), :]
        return move(place, place, gather_send.at[slot, piece], gather_recv.at[block, piece], peer)

    def gather_start(slot, block, peer):
        for piece in range(PIECES):
            gather_copy(slot, block, piece, peer).start()

    def gather_wait(block, pieces, forward=None):
        for piece in pieces:
            gather_copy(0, block, piece, ahead).wait_recv()
            if forward is not None:
                slot, peer = forward
                gather_copy(slot, block, piece, peer).start()

    greet(4)
    lth[...] = lt_pair[...].astype(bf16)
    lt_down[...] = lt_down_pair[...].astype(bf16)
    loads = [
        pltpu.make_async_copy(source, target, load_sem.at[index])
        for index, (source, target) in enumerate(
            ((w_gate_any, w_gate), (w_up_any, w_up), (w_down_any, w_down))
        )
    ]
    load_own = pltpu.make_async_copy(own, sec.at[me], own_sem)
    load_own.start()
    load_own.wait()
    gather_start(0, me, ahead)

    @pl.when(jnp.logical_not(is_end))
    def _():
        gather_start(1, me, behind)

    for load in loads:
        load.start()

    def block_at(step):
        middle = jnp.where(
            step == 0, me, jnp.where(step == 1, ahead, jnp.where(step == 2, behind, ahead + inward))
        )
        return jnp.where(is_end, me + inward * step, middle)

    def token_rows(step):
        return pl.ds(pl.multiple_of(block_at(step) * size, size), size)

    def cot_load(step):
        slot = lax.rem(step, 2)
        return pltpu.make_async_copy(cot.at[token_rows(step), :], cots.at[slot], cot_sem.at[slot])

    def part_store(step):
        return pltpu.make_async_copy(
            parts.at[block_at(step)], part.at[token_rows(step), :], part_sem.at[step]
        )

    own_rows = pl.ds(pl.multiple_of(me * size, size), size)
    near_store = pltpu.make_async_copy(parts.at[me], part.at[own_rows, :], part_sem.at[0])
    early_rows_near = pl.ds(0, 3 * half)
    near_copy = move(
        parts.at[ahead, early_rows_near, :], near.at[early_rows_near, :], near_send, near_recv, ahead
    )

    def table_copy(step):
        peer = lax.rem(me + step, 4)
        return move(tables.at[me], tables.at[me], table_send.at[step], table_recv.at[step], peer)

    cot_load(0).start()
    weights = (w_gate, w_up)
    fulls = []
    for index in range(2):
        loads[index].wait()
        block = slice(index * RANK, (index + 1) * RANK)
        adapters = split_rows(lt_pair[block, :])
        squares, full = direction(
            square_sums(weights[index], slice(0, w_gate.shape[1])),
            nn(adapters, weights[index][...]),
            nt(adapters, adapters),
            right[index],
        )
        norms = jnp.sqrt(squares)
        norms_ref[index : index + 1, :] = norms
        factors[index : index + 1, :] = mags[index : index + 1, :] / norms
        fulls.append(full)
    group = norms_qkv.shape[1]
    units = mags.shape[1]
    for index in range(2):
        norm = norms_ref[index : index + 1, :]
        tables[me, index : index + 1, :units] = norm
        tables[me, index + 2 : index + 3, :units] = mags[index : index + 1, :] - norm
    for index in range(3):
        norm = norms_qkv[index : index + 1, :]
        at = slice(index * group, (index + 1) * group)
        tables[me, 4:5, at] = norm
        tables[me, 5:6, at] = mags_qkv[index : index + 1, :] - norm
    for step in range(1, 4):
        table_copy(step).start()
    factor_down = mags_down[...] / norms_down[...]
    grad_left, grad_right_down = early.at[: 2 * RANK], early.at[2 * RANK :]
    grad_right = [early_rows.at[index * RANK : (index + 1) * RANK] for index in range(2)]
    grad_left_down = early_rows.at[2 * RANK : 3 * RANK]
    grad_mags = early_rows.at[3 * RANK :]
    early[...] = jnp.zeros_like(early)
    early_rows[...] = jnp.zeros_like(early_rows)
    loads[2].wait()

    def outer_copy(slot, piece, block):
        return move(
            mine.at[block, rows_of(piece), :],
            outer.at[slot, rows_of(piece), :],
            sum_send.at[slot, piece],
            outer_recv.at[slot, piece],
            ahead,
        )

    def inner_copy(slot, piece, block, send, peer):
        return move(
            mine.at[block, rows_of(piece), :],
            inner_sums.at[slot, rows_of(piece), :],
            sum_send.at[send, piece],
            inner_recv.at[slot, piece],
            peer,
        )

    def add_into(block, piece, ref):
        at = rows_of(piece)
        mine[block, at, :] = (
            mine[block, at, :].astype(f32) + ref[at, :].astype(f32)
        ).astype(bf16)

    def pass_on(distance, piece):
        block = me + inward * distance
        outer_copy(distance, piece, me).wait_recv()
        add_into(block, piece, outer.at[distance])
        inner_copy(distance - 1, piece, block, distance - 1, ahead).start()

    def hand_out(piece):
        inner_copy(1, piece, me, 2, behind).wait_recv()
        add_into(behind, piece, inner_sums.at[1])
        inner_copy(0, piece, behind, 2, behind).start()

    @pl.loop(0, 4)
    def _(step):
        block = block_at(step)
        slot = lax.rem(step, 2)

        @pl.when(step < 3)
        def _():
            cot_load(step + 1).start()

        @pl.when(is_end & (step > 0))
        def _():
            gather_wait(block, range(PIECES))

        @pl.when(in_middle & (step == 2))
        def _():
            gather_wait(ahead + inward, range(PIECES), (4, behind))

        x = sec[block]
        inner = nt(x, lth[...])
        inner_low = inner.astype(bf16)
        zs = [
            nn(x, weights[index][...])
            + nn(inner_low, padded_right(right[index], index, 2, SCALE))
            for index in range(2)
        ]
        gate = zs[0] * factors[0:1, :]
        upper = zs[1] * factors[1:2, :]
        sigmoid = 1.0 / (1.0 + jnp.exp(-gate))
        activated = gate * sigmoid
        hidden = (activated * upper).astype(bf16)
        right_low = right_down[...].astype(bf16)
        inner_down = nt(hidden, lt_down[...])

        parts[block] = (
            nn(hidden, w_down[...]) + SCALE * nn(inner_down.astype(bf16), right_low)
        ).astype(bf16)

        @pl.when(is_end | (step > 0))
        def _():
            part_store(step).start()

        @pl.when(in_middle & (step == 0))
        def _():
            for piece in range(PIECES):
                gather_wait(behind, (piece,), (2, ahead))
                gather_wait(ahead, (piece,), (3, behind))

        @pl.when(in_middle & (step == 3))
        def _():
            pass_on(1, 0)
            pass_on(1, 1)

        cot_load(step).wait()
        gz_down = (cots[slot].astype(f32) * factor_down).astype(bf16)
        gin_down = SCALE * nt(gz_down, right_low)
        grad_hidden = nt(gz_down, w_down[...]) + nn(gin_down.astype(bf16), lt_down[...])
        grad_left_down[...] += nn(gin_down.T.astype(bf16), hidden)
        grad_right_down[...] += SCALE * nn(inner_down.T.astype(bf16), gz_down)
        grads = (
            grad_hidden * upper * sigmoid * (1.0 + gate * (1.0 - sigmoid)),
            grad_hidden * activated,
        )
        gin = jnp.zeros((size, 2 * RANK), f32)
        gzs = []
        for index in range(2):
            grad_mags[index : index + 1, :] += jnp.sum(grads[index] * zs[index], axis=0, keepdims=True)
            gz = (grads[index] * factors[index : index + 1, :]).astype(bf16)
            gin = gin + nt(gz, padded_right(right[index], index, 2, SCALE))
            gzs.append(gz)
        gin_low = gin.astype(bf16)
        mine[block] = (
            nt(gzs[0], w_gate[...]) + nt(gzs[1], w_up[...]) + nn(gin_low, lth[...])
        ).astype(bf16)

        @pl.when(is_end & (step > 0))
        def _():
            for piece in range(PIECES):
                outer_copy(step - 1, piece, block).start()

        grad_left[...] += nn(gin.T.astype(bf16), x)
        inner_turned = inner.T.astype(bf16)
        for index in range(2):
            grad_right[index][...] += (
                SCALE * nn(inner_turned, gzs[index])[index * RANK : (index + 1) * RANK]
            )

    @pl.when(in_middle)
    def _():
        pass_on(1, 2)
        pass_on(1, 3)

    for index in range(2):
        block = slice(index * RANK, (index + 1) * RANK)
        norms = norms_ref[index : index + 1, :]
        factor_grad = grad_mags[index : index + 1, :]
        shape = -factor_grad * mags[index : index + 1, :] / (norms * norms * norms)
        shaped = right[index] * shape
        pieces = nt(split_rows(shaped), weights[index][...])
        lt = lt_pair[block, :]
        grad_left[block, :] += SCALE * (
            pieces[:RANK]
            + pieces[RANK:]
            + SCALE * nn_exact(nt_exact(shaped, right[index]), lt)
        )
        grad_right[index][...] += SCALE * fulls[index] * shape
        grad_mags[index : index + 1, :] = factor_grad / norms

    @pl.when(is_end)
    def _():
        part_store(0).wait()
        for piece in range(PIECES):
            gather_copy(0, me, piece, ahead).wait_send()

    @pl.when(in_middle)
    def _():
        for piece in range(PIECES):
            for slot in range(5):
                gather_copy(slot, me, piece, ahead).wait_send()

    for step in range(1, 4):
        part_store(step).wait()
    for step in range(1, 4):
        table_copy(step).wait()
    behind_part = jnp.where(is_end, me, ahead + inward)
    width = depth // 2
    exits = [
        (middle_any, grad_middle),
        (summed_any, parts.at[behind_part]),
        (cot.at[own_rows, :], cot_own),
        (w_full_any.at[:, :width], w_gate.at[:, :width]),
        (w_full_any.at[:, width:], w_up.at[:, :width]),
    ] + [
        (gathered_any.at[index], sec.at[index, :, group : 2 * group]) for index in range(4)
    ]
    exit_loads = [
        pltpu.make_async_copy(source, target, exit_sem.at[index])
        for index, (source, target) in enumerate(exits)
    ]
    for load in exit_loads:
        load.start()
    edge = 0
    for index in range(3):
        for peer in range(4):
            at = slice(index * group, (index + 1) * group)
            norm_table[0:1, edge : edge + group] = tables[peer, 4:5, at]
            norm_table[1:2, edge : edge + group] = tables[peer, 5:6, at]
            edge += group
    for index in range(2):
        for peer in range(4):
            norm_table[0:1, edge : edge + units] = tables[peer, index : index + 1, :units]
            norm_table[1:2, edge : edge + units] = tables[peer, index + 2 : index + 3, :units]
            edge += units
    for norm, magnitude in ((norms_out, mags_out), (norms_down, mags_down)):
        norm_table[0:1, edge : edge + depth] = norm[...]
        norm_table[1:2, edge : edge + depth] = magnitude[...] - norm[...]
        edge += depth

    @pl.when(in_middle)
    def _():
        pass_on(2, 0)
        pass_on(2, 1)
        hand_out(0)
        pass_on(2, 2)
        hand_out(1)
        pass_on(2, 3)
        hand_out(2)
        hand_out(3)
        for piece in range(PIECES):
            outer_copy(0, piece, me).wait_recv()
            inner_copy(0, piece, me, 0, ahead).wait_recv()
        grad_second[...] = (
            mine[me].astype(f32) + outer[0].astype(f32) + inner_sums[0].astype(f32)
        )

    @pl.when(is_end)
    def _():
        near_copy.start()
        for slot in range(3):
            for piece in range(PIECES):
                outer_copy(slot, piece, me).wait_send()
        for piece in range(PIECES):
            inner_copy(0, piece, me, 0, ahead).wait_recv()
        grad_second[...] = mine[me].astype(f32) + inner_sums[0].astype(f32)

    for load in exit_loads:
        load.wait()
    rows = grad_middle[...]
    gain = gain_ref[...].astype(f32)
    inverse = lax.rsqrt(jnp.mean(rows * rows, axis=-1, keepdims=True) + norm_eps)
    scaled = grad_second[...] * gain
    grad = (
        cot_own[...].astype(f32)
        + inverse * scaled
        - rows * (inverse * inverse * inverse) * jnp.mean(rows * scaled, axis=-1, keepdims=True)
    )
    grad_middle[...] = grad
    norm = norms_out[...]
    factor_grad = jnp.sum(grad * parts[behind_part].astype(f32), axis=0, keepdims=True)
    shape = -factor_grad * mags_out[...] / (norm * norm * norm)
    shaped = right_out[...] * shape
    adapted[:size, :] = (grad * (mags_out[...] / norm)).astype(bf16)
    adapted[size:, :] = split_rows(shaped)
    gz = adapted[:size, :]
    gin = SCALE * nt(gz, right_out[...].astype(bf16))
    gin_low = gin.astype(bf16)
    gin_turned = gin.T.astype(bf16)
    mixing = nt_exact(shaped, right_out[...])
    early_mags[...] = factor_grad / norm
    early_out[:RANK, :] = SCALE * (nn(inner_out[...].T.astype(bf16), gz) + full_out[...] * shape)

    def mixed_copy(step):
        peer = lax.rem(me + step, 4)
        return move(
            sec.at[peer, :, :group], mixed.at[me], mixed_send.at[step], mixed_recv.at[step], peer
        )

    for step in (2, 1, 3, 4):
        peer = lax.rem(me + step, 4)
        columns = pl.ds(pl.multiple_of(peer * group, group), group)
        moved = nt(adapted[:, :width], w_gate[columns, :width]) + nt(
            adapted[:, width:], w_up[columns, :width]
        )
        result = (moved[:size] + nn(gin_low, lt_out[:, columns].astype(bf16))).astype(bf16)
        if step == 4:
            mixed[me] = result
        else:
            sec[peer, :, :group] = result
            mixed_copy(step).start()
        lt = lt_out[:, columns]
        early_out[RANK:, columns] = nn(gin_turned, sec[peer, :, group : 2 * group]) + SCALE * (
            moved[size : size + RANK] + moved[size + RANK :] + SCALE * nn_exact(mixing, lt)
        )

    @pl.when(in_middle)
    def _():
        near_copy.wait_recv()
        parts[me, early_rows_near, :] = (
            parts[me, early_rows_near, :].astype(f32) + near[early_rows_near, :].astype(f32)
        ).astype(bf16)
        near_store.start()
        for piece in range(PIECES):
            for send in range(3):
                inner_copy(0, piece, me, send, ahead).wait_send()
        near_store.wait()

    @pl.when(is_end)
    def _():
        near_copy.wait_send()

    for step in range(1, 4):
        mixed_copy(step).wait()


def attention_back_kernel(
    teams,
    length_ref,
    query,
    keys,
    values,
    att,
    lse,
    mixed,
    summed,
    norms_ref,
    mags,
    fulls,
    inner,
    lt_triple,
    right,
    angles,
    gain_ref,
    early,
    early_out,
    early_rows,
    early_mags,
    norms_down,
    mags_down,
    right_down,
    full_down,
    lt_down,
    first_any,
    part,
    weights_any_query,
    weights_any_key,
    weights_any_value,
    w_down,
    x_own,
    grad_middle,
    middle,
    cot_own,
    outputs,
    input_grad,
    grad_qkv_left,
    grad_qkv_right,
    grad_qkv_mags,
    grad_mlp_left,
    grad_mlp_right,
    grad_mlp_mags,
    grad_out_left,
    grad_down_left,
    grad_exit_right,
    grad_out_mags,
    grad_down_mags,
    lth,
    gz,
    key_sums,
    value_sums,
    query_turned,
    factors,
    weights,
    mine,
    outer,
    inner_sums,
    outer_down,
    inner_down,
    block_part,
    last_down,
    wide,
    wide_in,
    line_in,
    whole,
    group_in,
    unit_in,
    small,
    small_line,
    small_rows,
    load_sem,
    part_sem,
    sum_send,
    outer_recv,
    inner_recv,
    down_send,
    down_outer_recv,
    down_inner_recv,
    last_sem,
    wide_send,
    wide_recv,
    line_send,
    line_recv,
    whole_send,
    whole_recv,
    group_send,
    group_recv,
    unit_send,
    unit_recv,
    small_send,
    small_recv,
    final_send,
    final_recv,
):
    total = query.shape[0]
    depth = mine.shape[1]
    size = total // 4
    half = size // PIECES
    team, me = lax.axis_index("rows"), lax.axis_index("heads")
    inward = jnp.where(me < 2, 1, -1)
    is_end = (me == 0) | (me == 3)
    in_middle = jnp.logical_not(is_end)
    ahead, behind = me + inward, me - inward

    def move(source, target, send, recv, peer, peer_team=team):
        return pltpu.make_async_remote_copy(
            src_ref=source,
            dst_ref=target,
            send_sem=send,
            recv_sem=recv,
            device_id=(peer_team, peer),
            device_id_type=MESH,
        )

    def rows_of(block, piece=None):
        if piece is None:
            return pl.ds(pl.multiple_of(block * size, size), size)
        return pl.ds(pl.multiple_of(block * size + piece * half, half), half)

    def piece_of(piece):
        return pl.ds(piece * half, half)

    barrier = pltpu.get_barrier_semaphore()
    for step in range(1, 4):
        pl.semaphore_signal(
            barrier, inc=1, device_id=(team, lax.rem(me + step, 4)), device_id_type=MESH
        )
    for step in range(1, teams):
        pl.semaphore_signal(
            barrier, inc=1, device_id=(lax.rem(team + step, teams), me), device_id_type=MESH
        )
    pl.semaphore_wait(barrier, teams + 2)

    def down_outer(slot, piece, block):
        return move(
            part.at[rows_of(block, piece), :],
            outer_down.at[slot, piece_of(piece), :],
            down_send.at[slot, piece],
            down_outer_recv.at[slot, piece],
            ahead,
        )

    def down_last(block):
        return move(
            part.at[rows_of(block, PIECES - 1), :],
            last_down,
            last_sem.at[0],
            last_sem.at[1],
            ahead,
        )

    def down_inner(slot, piece, send, peer):
        return move(
            block_part.at[send, piece_of(piece), :],
            inner_down.at[slot, piece_of(piece), :],
            down_send.at[send, piece],
            down_inner_recv.at[slot, piece],
            peer,
        )

    @pl.when(is_end)
    def _():
        for piece in range(PIECES):
            down_outer(1, piece, me + inward * 3).start()
        for piece in range(PIECES):
            down_outer(0, piece, me + inward * 2).start()
        down_last(ahead).start()

    def part_load(slot, block):
        return pltpu.make_async_copy(part.at[rows_of(block), :], block_part.at[slot], part_sem.at[slot])

    @pl.when(in_middle)
    def _():
        part_load(0, ahead).start()
        part_load(1, ahead + inward).start()
        part_load(3, behind).start()

    part_load(2, me).start()

    def unit_copy(step):
        return move(
            unit_in.at[team],
            unit_in.at[team],
            unit_send.at[step],
            unit_recv.at[step],
            me,
            lax.rem(team + step, teams),
        )

    def group_copy(step):
        return move(
            group_in.at[team],
            group_in.at[team],
            group_send.at[step],
            group_recv.at[step],
            me,
            lax.rem(team + step, teams),
        )

    unit_in[team] = early_rows[...].astype(bf16)
    for step in range(1, teams):
        unit_copy(step).start()

    loads = [
        pltpu.make_async_copy(source, weights.at[index], load_sem.at[index])
        for index, source in enumerate((weights_any_query, weights_any_key, weights_any_value))
    ]
    load_first = pltpu.make_async_copy(first_any, mine, load_sem.at[3])
    for load in loads:
        load.start()
    load_first.start()

    lth[...] = lt_triple[...].astype(bf16)
    heads = query.shape[1] // HEAD_DIM
    length = length_ref[0]
    factor = 1.0 / math.sqrt(HEAD_DIM)
    factors[:3, :] = mags[...] / norms_ref[...]

    def finish(index, head, grad):
        place = slice(head * HEAD_DIM, (head + 1) * HEAD_DIM)
        if index < 2:
            cosines, sines = turning(angles[...])
            grad = grad * cosines - pltpu.roll(grad, HEAD_DIM // 2, 1) * sines
        factors[index + 3 : index + 4, place] = jnp.sum(
            grad * summed[index, :, place].astype(f32), axis=0, keepdims=True
        )
        gz[index, :, place] = (grad * factors[index : index + 1, place]).astype(bf16)

    for head in range(heads):
        place = slice(head * HEAD_DIM, (head + 1) * HEAD_DIM)
        turned_keys = keys[:, place].astype(f32).T.astype(bf16)
        key_sums[...] = jnp.zeros_like(key_sums)
        value_sums[...] = jnp.zeros_like(value_sums)
        for block in range(total // 256):
            reach = (block + 1) * 256
            at = slice(block * 256, reach)
            grad_rows = mixed[at, place]
            rows = query[at, place]
            scores = nt(keys[:reach, place], rows)
            spots = lax.broadcasted_iota(jnp.int32, (reach, 256), 0)
            asking = lax.broadcasted_iota(jnp.int32, (reach, 256), 1) + block * 256
            allowed = (spots <= asking) & (spots < length)
            scores = jnp.where(allowed, scores * factor, mask_fill)
            probs = jnp.exp(scores - lse[head : head + 1, at])
            grad_probs = nt(values[:reach, place], grad_rows)
            centre = jnp.sum(
                (grad_rows.astype(f32) * att[at, place].astype(f32)).T, axis=0, keepdims=True
            )
            raw = (probs * (grad_probs - centre) * factor).astype(bf16)
            value_sums[:reach, :] += nn(probs.astype(bf16), grad_rows)
            key_sums[:reach, :] += nn(raw, rows)
            query_turned[:, at] = nn(turned_keys[:, :reach], raw)
        finish(0, head, query_turned[...].T)
        finish(1, head, key_sums[...])
        finish(2, head, value_sums[...])

    gin = jnp.zeros((total, 3 * RANK), f32)
    for index in range(3):
        gin = gin + nt(gz[index], padded_right(right[index], index, 3, SCALE))
    gin_low = gin.astype(bf16)
    load_first.wait()
    left = nn(gin.T.astype(bf16), mine[...])
    inner_turned = inner[...].astype(f32).T.astype(bf16)
    for index in range(3):
        block = slice(index * RANK, (index + 1) * RANK)
        norms = norms_ref[index : index + 1, :]
        factor_grad = factors[index + 3 : index + 4, :]
        shape = -factor_grad * mags[index : index + 1, :] / (norms * norms * norms)
        shaped = right[index] * shape
        loads[index].wait()
        pieces = nt(split_rows(shaped), weights[index])
        lt = lt_triple[block, :]
        extra = pieces[:RANK] + pieces[RANK:] + SCALE * nn_exact(nt_exact(shaped, right[index]), lt)
        wide[block, :] = (left[block, :] + SCALE * extra).astype(bf16)
        group_in[team, block, :] = (
            SCALE * (nn(inner_turned, gz[index])[block] + fulls[index] * shape)
        ).astype(bf16)
    tail = group_in.shape[1] - 3 * RANK
    group_in[team, 3 * RANK :, :] = jnp.concatenate(
        [factors[3:6, :] / norms_ref[...], jnp.zeros((tail - 3, factors.shape[1]), f32)], axis=0
    ).astype(bf16)
    wide[3 * RANK : 6 * RANK, :] = early[...].astype(bf16)
    wide[6 * RANK :, :] = early_out[...].astype(bf16)
    for step in range(1, teams):
        group_copy(step).start()

    tiles = wide.shape[0] // 16
    parts_of_tile = teams // tiles
    stretch = depth // parts_of_tile

    def tile_of(owner):
        return (
            pl.ds(pl.multiple_of(lax.rem(owner, tiles) * 16, 16), 16),
            pl.ds(pl.multiple_of((owner // tiles) * stretch, stretch), stretch),
        )

    def wide_copy(step):
        owner = lax.rem(team + step, teams)
        across, along = tile_of(owner)
        return move(
            wide.at[across, along],
            wide_in.at[team],
            wide_send.at[step],
            wide_recv.at[step],
            me,
            owner,
        )

    for step in range(1, teams):
        wide_copy(step).start()
    across, along = tile_of(team)
    wide_in[team] = wide[across, along]

    def add_down(send, piece, ref):
        at = piece_of(piece)
        block_part[send, at, :] = (
            block_part[send, at, :].astype(f32) + ref[at, :].astype(f32)
        ).astype(bf16)

    @pl.when(in_middle)
    def _():
        part_load(1, me).wait()
        for piece in range(PIECES):
            down_outer(1, piece, me).wait_recv()
            add_down(1, piece, outer_down.at[1])
            down_inner(1, piece, 1, ahead).start()

    def grad_block(block):
        at = rows_of(block)
        mine[at, :] = (
            nt(gz[0, at, :], weights[0])
            + nt(gz[1, at, :], weights[1])
            + nt(gz[2, at, :], weights[2])
            + nn(
                (
                    SCALE
                    * (
                        nt(gz[0, at, :], padded_right(right[0], 0, 3, 1.0))
                        + nt(gz[1, at, :], padded_right(right[1], 1, 3, 1.0))
                        + nt(gz[2, at, :], padded_right(right[2], 2, 3, 1.0))
                    )
                ).astype(bf16),
                lth[...],
            )
        ).astype(bf16)

    def outer_copy(slot, piece, block):
        return move(
            mine.at[rows_of(block, piece), :],
            outer.at[slot, piece_of(piece), :],
            sum_send.at[slot, piece],
            outer_recv.at[slot, piece],
            ahead,
        )

    def inner_copy(slot, piece, block, send, peer):
        return move(
            mine.at[rows_of(block, piece), :],
            inner_sums.at[slot, piece_of(piece), :],
            sum_send.at[send, piece],
            inner_recv.at[slot, piece],
            peer,
        )

    @pl.loop(0, 4)
    def _(step):
        middle_block = jnp.where(
            step == 0, ahead + inward, jnp.where(step == 1, ahead, jnp.where(step == 2, behind, me))
        )
        grad_block(jnp.where(is_end, me + inward * (3 - step), middle_block))

        @pl.when(is_end & (step == 0))
        def _():
            for piece in range(PIECES):
                outer_copy(2, piece, me + inward * 3).start()

    def add_into(block, piece, ref):
        at = rows_of(block, piece)
        mine[at, :] = (
            mine[at, :].astype(f32) + ref[piece_of(piece), :].astype(f32)
        ).astype(bf16)

    for step in range(1, teams):
        wide_copy(step).wait_recv()
    gathered = jnp.zeros((16, stretch), f32)
    for index in range(teams):
        gathered = gathered + wide_in[index].astype(f32)
    line_in[me] = gathered.astype(bf16)

    def line_copy(step):
        return move(
            line_in.at[me],
            line_in.at[me],
            line_send.at[step],
            line_recv.at[step],
            lax.rem(me + step, 4),
        )

    for step in range(1, 4):
        line_copy(step).start()

    @pl.when(in_middle)
    def _():
        part_load(0, me).wait()
        part_load(3, me).wait()
        for piece in range(PIECES):
            down_outer(0, piece, me).wait_recv()
            add_down(0, piece, outer_down.at[0])
            down_inner(0, piece, 0, ahead).start()
        for piece in range(PIECES):
            down_inner(1, piece, 0, ahead).wait_recv()
            add_down(3, piece, inner_down.at[1])
            down_inner(0, piece, 3, behind).start()
        for piece in range(PIECES):
            outer_copy(2, piece, me).wait_recv()
            add_into(ahead + inward, piece, outer.at[2])
            inner_copy(1, piece, ahead + inward, 1, ahead).start()

    part_load(2, me).wait()

    for piece in range(PIECES):
        down_inner(0, piece, 0, ahead).wait_recv()

    @pl.when(in_middle)
    def _():
        down_last(me).wait_recv()
        at = piece_of(PIECES - 1)
        block_part[2, at, :] = (
            block_part[2, at, :].astype(f32) + last_down[...].astype(f32)
        ).astype(bf16)

    load_own = [
        pltpu.make_async_copy(source, target, load_sem.at[index])
        for index, (source, target) in enumerate(
            ((middle, input_grad), (cot_own.at[rows_of(me), :], outputs))
        )
    ]
    for load in load_own:
        load.start()
    norm_down = norms_down[...]
    done = block_part[2].astype(f32) + inner_down[0].astype(f32)
    for load in load_own:
        load.wait()
    small[0:1, :] = jnp.sum(outputs[...].astype(f32) * done, axis=0, keepdims=True)
    small[1:2, :] = early_mags[...]
    outputs[...] = (input_grad[...] + done * (mags_down[...] / norm_down)).astype(bf16)
    small_line[me] = small[...]

    def small_copy(step):
        return move(
            small_line.at[me],
            small_line.at[me],
            small_send.at[step],
            small_recv.at[step],
            lax.rem(me + step, 4),
        )

    for step in range(1, 4):
        small_copy(step).start()

    @pl.when(is_end)
    def _():
        for piece in range(PIECES):
            outer_copy(1, piece, ahead + inward).start()
        for piece in range(PIECES):
            outer_copy(0, piece, ahead).start()

    load_wide = [
        pltpu.make_async_copy(
            w_down.at[:, index * 512 : (index + 1) * 512],
            weights.at[index, : w_down.shape[0], :],
            load_sem.at[index],
        )
        for index in range(3)
    ]
    load_wide.append(
        pltpu.make_async_copy(w_down.at[:1024, 1536:], gz.at[0], load_sem.at[3])
    )
    load_wide.append(
        pltpu.make_async_copy(
            w_down.at[1024:, 1536:], gz.at[1, : w_down.shape[0] - 1024, :], load_sem.at[4]
        )
    )
    for load in load_wide:
        load.start()

    for step in range(1, 4):
        line_copy(step).wait_recv()
    whole[team] = (
        line_in[0].astype(f32)
        + line_in[1].astype(f32)
        + line_in[2].astype(f32)
        + line_in[3].astype(f32)
    ).astype(bf16)

    def whole_copy(step):
        return move(
            whole.at[team],
            whole.at[team],
            whole_send.at[step],
            whole_recv.at[step],
            me,
            lax.rem(team + step, teams),
        )

    for step in range(1, teams):
        whole_copy(step).start()
    for step in range(1, 4):
        small_copy(step).wait_recv()
    small_rows[team] = small_line[0] + small_line[1] + small_line[2] + small_line[3]

    def final_copy(step):
        return move(
            small_rows.at[team],
            small_rows.at[team],
            final_send.at[step],
            final_recv.at[step],
            me,
            lax.rem(team + step, teams),
        )

    for step in range(1, teams):
        final_copy(step).start()

    @pl.when(in_middle)
    def _():
        for piece in range(PIECES):
            inner_copy(1, piece, me, 0, ahead).wait_recv()
            add_into(behind, piece, inner_sums.at[1])
            inner_copy(0, piece, behind, 2, behind).start()
            outer_copy(1, piece, me).wait_recv()
            add_into(ahead, piece, outer.at[1])
            inner_copy(0, piece, ahead, 0, ahead).start()

    for step in range(1, teams):
        final_copy(step).wait_recv()
    sums = jnp.zeros((2, depth), f32)
    for index in range(teams):
        sums = sums + small_rows[index]
    grad_down_mags[...] = sums[0:1] / norm_down
    grad_out_mags[...] = sums[1:2]
    shape = -sums[0:1] * mags_down[...] / (norm_down * norm_down * norm_down)
    shaped = right_down[...] * shape
    right_extra = SCALE * full_down[...] * shape
    for load in load_wide:
        load.wait()
    cut = split_rows(shaped)
    units = w_down.shape[0]
    pieces = (
        nt(cut[:, :512], weights[0, :units, :])
        + nt(cut[:, 512:1024], weights[1, :units, :])
        + nt(cut[:, 1024:1536], weights[2, :units, :])
    )
    last = cut[:, 1536:]
    mixing = nt_exact(shaped, right_down[...])
    lt = lt_down[...]
    extra = pieces[:RANK] + pieces[RANK:] + SCALE * nn_exact(mixing, lt)
    ends = [nt(last, gz[0]), nt(last, gz[1, : units - 1024, :])]
    grad_down_left[:, :1024] = SCALE * (extra[:, :1024] + ends[0][:RANK] + ends[0][RANK:])
    grad_down_left[:, 1024:] = SCALE * (extra[:, 1024:] + ends[1][:RANK] + ends[1][RANK:])

    for step in range(1, teams):
        group_copy(step).wait_recv()
        unit_copy(step).wait_recv()
        whole_copy(step).wait_recv()
    group_total = jnp.zeros(group_in.shape[1:], f32)
    unit_total = jnp.zeros(unit_in.shape[1:], f32)
    for index in range(teams):
        group_total = group_total + group_in[index].astype(f32)
        unit_total = unit_total + unit_in[index].astype(f32)
    for index in range(3):
        grad_qkv_right[index] = group_total[index * RANK : (index + 1) * RANK]
    grad_qkv_mags[...] = group_total[3 * RANK : 3 * RANK + 3]
    for index in range(2):
        grad_mlp_right[index] = unit_total[index * RANK : (index + 1) * RANK]
    grad_down_left[...] += unit_total[2 * RANK : 3 * RANK]
    grad_mlp_mags[...] = unit_total[3 * RANK : 3 * RANK + 2]
    for part_index in range(parts_of_tile):
        along = slice(part_index * stretch, (part_index + 1) * stretch)
        tile = [whole[part_index * tiles + index].astype(f32) for index in range(7)]
        for index in range(3):
            grad_qkv_left[index, :, along] = tile[index]
        for index in range(2):
            grad_mlp_left[index, :, along] = tile[3 + index]
        grad_exit_right[1, :, along] = tile[5] + right_extra[:, along]
        grad_exit_right[0, :, along] = tile[6]
    group = query.shape[1]
    within = min(group, stretch)
    for index in range(group // within):
        spot = me * group + index * within
        grad_out_left[:, index * within : (index + 1) * within] = whole[
            (spot // stretch) * tiles + 7,
            :,
            pl.ds(pl.multiple_of(lax.rem(spot, stretch), within), within),
        ].astype(f32)

    load_end = [
        pltpu.make_async_copy(source, target, load_sem.at[index])
        for index, (source, target) in enumerate(
            ((grad_middle, input_grad), (x_own.at[rows_of(me), :], block_part.at[2]))
        )
    ]
    for load in load_end:
        load.start()
    for load in load_end:
        load.wait()
    gain = gain_ref[...].astype(f32)

    def close(grad):
        rows = block_part[2].astype(f32)
        inverse = lax.rsqrt(jnp.mean(rows * rows, axis=-1, keepdims=True) + norm_eps)
        scaled = grad * gain
        input_grad[...] = (
            input_grad[...]
            + inverse * scaled
            - rows
            * (inverse * inverse * inverse)
            * jnp.mean(rows * scaled, axis=-1, keepdims=True)
        )

    @pl.when(in_middle)
    def _():
        for piece in range(PIECES):
            outer_copy(0, piece, me).wait_recv()
            inner_copy(0, piece, me, 0, ahead).wait_recv()
        close(mine[rows_of(me), :].astype(f32) + outer[0].astype(f32) + inner_sums[0].astype(f32))
        for piece in range(PIECES):
            for send in (0, 1, 3):
                down_inner(0, piece, send, ahead).wait_send()
            for send in range(3):
                inner_copy(0, piece, me, send, ahead).wait_send()

    @pl.when(is_end)
    def _():
        for piece in range(PIECES):
            inner_copy(0, piece, me, 0, ahead).wait_recv()
        close(mine[rows_of(me), :].astype(f32) + inner_sums[0].astype(f32))
        for piece in range(PIECES):
            for slot in range(2):
                down_outer(slot, piece, me).wait_send()
            for slot in range(3):
                outer_copy(slot, piece, me).wait_send()
        down_last(me).wait_send()

    for step in range(1, 4):
        line_copy(step).wait_send()
        small_copy(step).wait_send()
    for step in range(1, teams):
        unit_copy(step).wait_send()
        group_copy(step).wait_send()
        wide_copy(step).wait_send()
        whole_copy(step).wait_send()
        final_copy(step).wait_send()


def call(kernel, outs, ins, specs=None, out_specs=None, scratch=(), flops=0, moved=0, collective=None):
    extra = {} if collective is None else {"collective_id": collective, "has_side_effects": True}
    return pl.pallas_call(
        kernel,
        out_shape=[jax.ShapeDtypeStruct(shape, kind) for shape, kind in outs],
        in_specs=specs or [VMEM] * len(ins),
        out_specs=out_specs or [VMEM] * len(outs),
        scratch_shapes=list(scratch),
        cost_estimate=pl.CostEstimate(flops=flops, bytes_accessed=moved, transcendentals=0),
        compiler_params=pltpu.CompilerParams(vmem_limit_bytes=LIMIT, **extra),
    )(*ins)


def rope_table(length, width):
    half = width // 2
    freqs = np.float32(rope_base) ** (-(np.arange(half, dtype=np.float32) * 2.0) / width)
    angles = np.arange(length, dtype=np.float32)[:, None] * freqs[None, :].astype(np.float32)
    return np.concatenate([np.cos(angles), np.sin(angles)], axis=1).astype(np.float32)


def local(
    inputs,
    cotangent,
    lengths,
    gain_attn,
    gain_mlp,
    w_query,
    w_key,
    w_value,
    w_out,
    w_gate,
    w_up,
    w_down,
    qkv_left,
    qkv_right,
    qkv_mags,
    mlp_left,
    mlp_right,
    mlp_mags,
    out_left,
    down_left,
    exit_right,
    out_mags,
    down_mags,
):
    count = lax.axis_size("heads")
    teams = lax.axis_size("rows")
    total, depth = inputs.shape
    share = total // count
    group = w_query.shape[1]
    units = w_gate.shape[1]
    heads = group // HEAD_DIM
    deep = group // teams
    lt_qkv = jnp.transpose(qkv_left, (0, 2, 1)).reshape(3 * RANK, depth)
    lt_mlp = jnp.transpose(mlp_left, (0, 2, 1)).reshape(2 * RANK, depth)
    angles = jnp.asarray(rope_table(total, HEAD_DIM))
    gain_first = gain_attn.reshape(1, depth)
    gain_second = gain_mlp.reshape(1, depth)
    out_mag, down_mag = out_mags.reshape(1, depth), down_mags.reshape(1, depth)
    bits = teams.bit_length() - 1
    assert teams == 1 << bits
    slots = 3 * (2 * (2 ** (bits - 1) - 1) + 2 ** (bits - 1))

    (
        first,
        query,
        keys,
        values,
        att,
        qkv_summed,
        w_full,
        lse,
        qkv_inner,
        qkv_norms,
        qkv_full,
        gathered,
        middle,
        second,
        out_summed,
        out_inner,
        full_out,
        lt_out,
        exit_norms,
        full_down,
    ) = call(
        functools.partial(attention_forward_kernel, count, teams),
        [
            ((total, depth), bf16),
            ((total, group), bf16),
            ((total, group), bf16),
            ((total, group), bf16),
            ((total, group), bf16),
            ((3, total, group), bf16),
            ((depth, depth), bf16),
            ((heads, total), f32),
            ((total, 3 * RANK), bf16),
            ((3, group), f32),
            ((3, RANK, group), f32),
            ((count, share, group), bf16),
            ((share, depth), f32),
            ((share, depth), bf16),
            ((share, depth), bf16),
            ((share, RANK), f32),
            ((RANK, depth), f32),
            ((RANK, depth), f32),
            ((2, depth), f32),
            ((RANK, depth), f32),
        ],
        (
            lengths,
            gain_first,
            lt_qkv,
            qkv_right,
            qkv_mags,
            angles,
            out_left.T,
            down_left.T,
            exit_right,
            out_mag,
            gain_second,
            inputs,
            w_query,
            w_key,
            w_value,
            w_out,
            w_down,
        ),
        specs=[SMEM] + [VMEM] * 10 + [ANY] * 6,
        out_specs=[ANY] * 7 + [VMEM] * 13,
        scratch=(
            pltpu.VMEM((total + 2 * RANK, depth), bf16),
            pltpu.VMEM((3, depth, group), bf16),
            pltpu.VMEM((total, group), bf16),
            pltpu.VMEM((total, group), bf16),
            pltpu.VMEM((total, group), bf16),
            pltpu.VMEM((total, group), bf16),
            pltpu.VMEM((3, total, group), bf16),
            pltpu.VMEM((count, teams, deep, depth), bf16),
            pltpu.VMEM((units, depth), bf16),
            pltpu.VMEM((share, depth), bf16),
            pltpu.VMEM((share + 2 * RANK, depth), bf16),
            pltpu.VMEM((count, RANK, group), f32),
            pltpu.VMEM((count, 8, depth), f32),
            pltpu.VMEM((count, RANK, depth), bf16),
            pltpu.SemaphoreType.DMA((6 + teams,)),
            pltpu.SemaphoreType.DMA((6 + count * teams,)),
            pltpu.SemaphoreType.DMA((heads, count)),
            pltpu.SemaphoreType.DMA((heads, count)),
            pltpu.SemaphoreType.DMA((count,)),
            pltpu.SemaphoreType.DMA((count,)),
            pltpu.SemaphoreType.DMA((slots,)),
            pltpu.SemaphoreType.DMA((slots,)),
            pltpu.SemaphoreType.DMA((3, count)),
            pltpu.SemaphoreType.DMA((3, count)),
        ),
        flops=6 * total * depth * group + 4 * total * total * group,
        moved=2 * (2 * total * depth + 3 * depth * group + 8 * total * group),
        collective=0,
    )
    out_norms, down_norms = exit_norms[0:1], exit_norms[1:2]
    assert count == 4
    (
        part,
        early,
        early_rows,
        norm_stats,
        grad_middle,
        mixed,
        early_out,
        early_mags,
    ) = call(
        feed_forward_kernel,
        [
            ((total, depth), bf16),
            ((3 * RANK, depth), f32),
            ((4 * RANK, units), f32),
            ((2, 3 * count * group + 2 * count * units + 2 * depth), f32),
            ((share, depth), f32),
            ((count, share, group), bf16),
            ((2 * RANK, depth), f32),
            ((1, depth), f32),
        ],
        (
            second,
            cotangent,
            w_gate,
            w_up,
            w_down,
            lt_mlp,
            down_left.T,
            mlp_right,
            mlp_mags,
            exit_right[1],
            down_mag,
            down_norms,
            qkv_norms,
            qkv_mags,
            out_norms,
            out_mag,
            gain_second,
            out_inner,
            lt_out,
            exit_right[0],
            full_out,
            middle,
            out_summed,
            gathered,
            w_full,
        ),
        specs=[ANY] * 5 + [VMEM] * 16 + [ANY] * 4,
        out_specs=[ANY] + [VMEM] * 7,
        scratch=(
            pltpu.VMEM((share, depth), f32),
            pltpu.VMEM((share + 2 * RANK, depth), bf16),
            pltpu.VMEM((2 * RANK, depth), bf16),
            pltpu.VMEM((RANK, units), bf16),
            pltpu.VMEM((2, units), f32),
            pltpu.VMEM((2, units), f32),
            pltpu.VMEM((depth, units), bf16),
            pltpu.VMEM((depth, units), bf16),
            pltpu.VMEM((units, depth), bf16),
            pltpu.VMEM((count, share, depth), bf16),
            pltpu.VMEM((2, share, depth), bf16),
            pltpu.VMEM((share, depth), bf16),
            pltpu.VMEM((count, share, depth), bf16),
            pltpu.VMEM((count, share, depth), bf16),
            pltpu.VMEM((3, share, depth), bf16),
            pltpu.VMEM((2, share, depth), bf16),
            pltpu.VMEM((share, depth), bf16),
            pltpu.VMEM((count, 8, depth), f32),
            pltpu.SemaphoreType.DMA((3,)),
            pltpu.SemaphoreType.DMA((2,)),
            pltpu.SemaphoreType.DMA((4,)),
            pltpu.SemaphoreType.DMA((5, PIECES)),
            pltpu.SemaphoreType.DMA((4, PIECES)),
            pltpu.SemaphoreType.DMA((3, PIECES)),
            pltpu.SemaphoreType.DMA((3, PIECES)),
            pltpu.SemaphoreType.DMA((2, PIECES)),
            pltpu.SemaphoreType.DMA,
            pltpu.SemaphoreType.DMA,
            pltpu.SemaphoreType.DMA((4,)),
            pltpu.SemaphoreType.DMA((4,)),
            pltpu.SemaphoreType.DMA((9,)),
            pltpu.SemaphoreType.DMA,
            pltpu.SemaphoreType.DMA((4,)),
            pltpu.SemaphoreType.DMA((4,)),
        ),
        flops=12 * total * depth * units,
        moved=2 * (3 * depth * units + 4 * total * depth),
        collective=1,
    )
    results = call(
        functools.partial(attention_back_kernel, teams),
        [
            ((share, depth), bf16),
            ((share, depth), f32),
            ((3, RANK, depth), f32),
            ((3, RANK, group), f32),
            ((3, group), f32),
            ((2, RANK, depth), f32),
            ((2, RANK, units), f32),
            ((2, units), f32),
            ((RANK, group), f32),
            ((RANK, units), f32),
            ((2, RANK, depth), f32),
            ((1, depth), f32),
            ((1, depth), f32),
        ],
        (
            lengths,
            query,
            keys,
            values,
            att,
            lse,
            mixed.reshape(total, group),
            qkv_summed,
            qkv_norms,
            qkv_mags,
            qkv_full,
            qkv_inner,
            lt_qkv,
            qkv_right,
            angles,
            gain_first,
            early,
            early_out,
            early_rows,
            early_mags,
            down_norms,
            down_mag,
            exit_right[1],
            full_down,
            down_left.T,
            first,
            part,
            w_query,
            w_key,
            w_value,
            w_down,
            inputs,
            grad_middle,
            middle,
            cotangent,
        ),
        specs=[SMEM] + [VMEM] * 24 + [ANY] * 10,
        scratch=(
            pltpu.VMEM((3 * RANK, depth), bf16),
            pltpu.VMEM((3, total, group), bf16),
            pltpu.VMEM((total, HEAD_DIM), f32),
            pltpu.VMEM((total, HEAD_DIM), f32),
            pltpu.VMEM((HEAD_DIM, total), f32),
            pltpu.VMEM((8, group), f32),
            pltpu.VMEM((3, depth, group), bf16),
            pltpu.VMEM((total, depth), bf16),
            pltpu.VMEM((3, share, depth), bf16),
            pltpu.VMEM((2, share, depth), bf16),
            pltpu.VMEM((2, share, depth), bf16),
            pltpu.VMEM((2, share, depth), bf16),
            pltpu.VMEM((4, share, depth), bf16),
            pltpu.VMEM((share // PIECES, depth), bf16),
            pltpu.VMEM((8 * RANK, depth), bf16),
            pltpu.VMEM((teams, 16, depth * 8 // teams), bf16),
            pltpu.VMEM((count, 16, depth * 8 // teams), bf16),
            pltpu.VMEM((teams, 16, depth * 8 // teams), bf16),
            pltpu.VMEM((teams, 4 * RANK, group), bf16),
            pltpu.VMEM((teams, 4 * RANK, units), bf16),
            pltpu.VMEM((2, depth), f32),
            pltpu.VMEM((count, 2, depth), f32),
            pltpu.VMEM((teams, 2, depth), f32),
            pltpu.SemaphoreType.DMA((5,)),
            pltpu.SemaphoreType.DMA((4,)),
            pltpu.SemaphoreType.DMA((3, PIECES)),
            pltpu.SemaphoreType.DMA((3, PIECES)),
            pltpu.SemaphoreType.DMA((2, PIECES)),
            pltpu.SemaphoreType.DMA((4, PIECES)),
            pltpu.SemaphoreType.DMA((2, PIECES)),
            pltpu.SemaphoreType.DMA((2, PIECES)),
            pltpu.SemaphoreType.DMA((2,)),
            pltpu.SemaphoreType.DMA((teams,)),
            pltpu.SemaphoreType.DMA((teams,)),
            pltpu.SemaphoreType.DMA((count,)),
            pltpu.SemaphoreType.DMA((count,)),
            pltpu.SemaphoreType.DMA((teams,)),
            pltpu.SemaphoreType.DMA((teams,)),
            pltpu.SemaphoreType.DMA((teams,)),
            pltpu.SemaphoreType.DMA((teams,)),
            pltpu.SemaphoreType.DMA((teams,)),
            pltpu.SemaphoreType.DMA((teams,)),
            pltpu.SemaphoreType.DMA((count,)),
            pltpu.SemaphoreType.DMA((count,)),
            pltpu.SemaphoreType.DMA((teams,)),
            pltpu.SemaphoreType.DMA((teams,)),
        ),
        flops=6 * total * depth * group + 10 * total * total * group,
        moved=2 * (2 * total * depth + 3 * depth * group + 8 * total * group),
        collective=2,
    )
    (
        outputs,
        input_grad,
        grad_qkv_left,
        grad_qkv_right,
        grad_qkv_mags,
        grad_mlp_left,
        grad_mlp_right,
        grad_mlp_mags,
        grad_out_left,
        grad_down_left,
        grad_exit_right,
        grad_out_mags,
        grad_down_mags,
    ) = results
    return (
        outputs,
        input_grad,
        jnp.transpose(grad_qkv_left, (0, 2, 1)),
        grad_qkv_right,
        grad_qkv_mags,
        jnp.transpose(grad_mlp_left, (0, 2, 1)),
        grad_mlp_right,
        grad_mlp_mags,
        grad_out_left.T,
        grad_down_left.T,
        grad_exit_right,
        grad_out_mags.reshape(depth),
        grad_down_mags.reshape(depth),
        norm_stats,
    )


def solution(mesh):
    placed = (
        P("rows", None),
        P("rows", None),
        P("rows"),
        P(),
        P(),
        P(None, "heads"),
        P(None, "heads"),
        P(None, "heads"),
        P("heads", None),
        P(None, "heads"),
        P(None, "heads"),
        P("heads", None),
        P(),
        P(None, None, "heads"),
        P(None, "heads"),
        P(),
        P(None, None, "heads"),
        P(None, "heads"),
        P("heads", None),
        P("heads", None),
        P(),
        P(),
        P(),
    )
    return jax.shard_map(
        local,
        mesh=mesh,
        in_specs=placed,
        out_specs=(
            P(("rows", "heads"), None),
            P(("rows", "heads"), None),
            P(),
            P(None, None, "heads"),
            P(None, "heads"),
            P(),
            P(None, None, "heads"),
            P(None, "heads"),
            P("heads", None),
            P("heads", None),
            P(),
            P(),
            P(),
            P(),
        ),
        check_vma=False,
    )
```

```python
import functools
import math

import jax
import jax.numpy as jnp
import numpy as np
from jax import lax
from jax.experimental import pallas as pl
from jax.experimental.pallas import tpu as pltpu
from jax.sharding import PartitionSpec as P

HEAD_DIM = 128
RANK = 16
norm_eps = 1e-05
rope_base = 10000.0
mask_fill = -1e30
SCALE = 32.0 / RANK

f32 = jnp.float32
bf16 = jnp.bfloat16
MESH = pl.DeviceIdType.MESH
VMEM = pl.BlockSpec(memory_space=pltpu.VMEM)
SMEM = pl.BlockSpec(memory_space=pltpu.SMEM)
ANY = pl.BlockSpec(memory_space=pl.ANY)
LIMIT = 63 << 20
PIECES = 4


def nn(left, right):
    return jnp.dot(left, right, preferred_element_type=f32)


def nt(left, right):
    return lax.dot_general(left, right, (((1,), (1,)), ((), ())), preferred_element_type=f32)


def nn_exact(left, right):
    return jnp.dot(left, right, precision=lax.Precision.HIGHEST, preferred_element_type=f32)


def nt_exact(left, right):
    return lax.dot_general(
        left,
        right,
        (((1,), (1,)), ((), ())),
        precision=lax.Precision.HIGHEST,
        preferred_element_type=f32,
    )


def split_rows(field):
    high = field.astype(bf16)
    return jnp.concatenate([high, (field - high.astype(f32)).astype(bf16)], axis=0)


def square_sums(ref, columns, chunk=128):
    depth = ref.shape[0]
    width = columns.size if isinstance(columns, pl.Slice) else columns.stop - columns.start

    def step(index, total):
        piece = ref[pl.ds(pl.multiple_of(index * chunk, chunk), chunk), columns].astype(f32)
        return total + jnp.sum((piece * piece).reshape(chunk // 8, 8, width), axis=0)

    total = lax.fori_loop(0, depth // chunk, step, jnp.zeros((8, width), f32))
    return jnp.sum(total, axis=0, keepdims=True)


def direction(squares, pieces, gram, right):
    plain = pieces[:RANK] + pieces[RANK:]
    turned = nn_exact(gram, jnp.concatenate([right, right], axis=0))
    full = plain + SCALE * (turned[:RANK] + turned[RANK:])
    return squares + SCALE * jnp.sum(right * (plain + full), axis=0, keepdims=True), full


def padded_right(right, at, count, factor):
    low = factor * right.astype(bf16).astype(f32)
    zero = jnp.zeros_like(low)
    return jnp.concatenate([low if slot == at else zero for slot in range(count)], axis=0).astype(bf16)


def norm_value(rows, gain):
    inverse = lax.rsqrt(jnp.mean(rows * rows, axis=-1, keepdims=True) + norm_eps)
    return rows * inverse * gain, inverse


def row_of(ref):
    return ref[...].astype(f32).reshape(1, ref.shape[0])


def turning(angles):
    swapped = pltpu.roll(angles, HEAD_DIM // 2, 1)
    first = lax.broadcasted_iota(jnp.int32, angles.shape, 1) < HEAD_DIM // 2
    return jnp.where(first, angles, swapped), jnp.where(first, -swapped, angles)


def greet(count):
    row, me = lax.axis_index("rows"), lax.axis_index("heads")
    barrier = pltpu.get_barrier_semaphore()
    for step in range(1, count):
        pl.semaphore_signal(
            barrier, inc=1, device_id=(row, lax.rem(me + step, count)), device_id_type=MESH
        )
    pl.semaphore_wait(barrier, count - 1)


def attention_forward_kernel(
    count,
    teams,
    length_ref,
    gain_ref,
    lt,
    right,
    mags,
    angles,
    lt_out,
    lt_down,
    right_exit,
    mags_out,
    mags_down,
    gain_second,
    lt_mlp,
    right_mlp,
    mags_mlp,
    x_any,
    w_query,
    w_key,
    w_value,
    w_out,
    w_down_any,
    w_gate_any,
    w_up_any,
    first,
    query_any,
    keys_any,
    values_any,
    att_any,
    summed_any,
    w_full,
    lse,
    inner_ref,
    norms_ref,
    full_ref,
    gathered,
    middle,
    second,
    summed_out,
    inner_out,
    full_out,
    lt_full,
    exit_norms,
    full_down,
    norms_mlp,
    full_mlp,
    norm_table,
    ext,
    weights,
    query,
    keys,
    values,
    att,
    summed,
    wf,
    w_down,
    w_mlp,
    x_own,
    ext_out,
    lt_in,
    squares_in,
    down_in,
    tables,
    load_sem,
    store_sem,
    send_sem,
    recv_sem,
    line_send,
    line_recv,
    team_send,
    team_recv,
    small_send,
    small_recv,
):
    team, me = lax.axis_index("rows"), lax.axis_index("heads")
    total, depth = x_any.shape
    share = total // count
    group = query.shape[1]
    heads = group // HEAD_DIM
    deep = wf.shape[2]
    bits = teams.bit_length() - 1

    def move(source, target, send, recv, peer_team, peer):
        return pltpu.make_async_remote_copy(
            src_ref=source,
            dst_ref=target,
            send_sem=send,
            recv_sem=recv,
            device_id=(peer_team, peer),
            device_id_type=MESH,
        )

    def flip(index, bit):
        weight = 1 << bit
        return index + weight - 2 * weight * lax.rem(index // weight, 2)

    x_load = pltpu.make_async_copy(x_any, ext.at[:total], load_sem.at[0])
    own_load = pltpu.make_async_copy(
        x_any.at[pl.ds(pl.multiple_of(me * share, share), share), :], x_own, load_sem.at[1]
    )
    loads = [
        pltpu.make_async_copy(source, weights.at[index], load_sem.at[2 + index])
        for index, source in enumerate((w_query, w_key, w_value))
    ]
    shard_loads = [
        pltpu.make_async_copy(
            w_out.at[index * deep : (index + 1) * deep, :], wf.at[me, index], load_sem.at[6 + index]
        )
        for index in range(teams)
    ]
    down_load = pltpu.make_async_copy(w_down_any, w_down, load_sem.at[5])
    mlp_loads = [
        pltpu.make_async_copy(source, w_mlp.at[index], load_sem.at[6 + teams + index])
        for index, source in enumerate((w_gate_any, w_up_any))
    ]
    x_load.start()
    for load in loads:
        load.start()
    own_load.start()

    barrier = pltpu.get_barrier_semaphore()
    for step in range(1, count):
        pl.semaphore_signal(
            barrier, inc=1, device_id=(team, lax.rem(me + step, count)), device_id_type=MESH
        )
    for bit in range(bits):
        pl.semaphore_signal(barrier, inc=1, device_id=(flip(team, bit), me), device_id_type=MESH)
    pl.semaphore_wait(barrier, count - 1 + bits)

    def line_copy(step):
        peer = lax.rem(me + step, count)
        return move(
            w_out.at[pl.ds(pl.multiple_of(team * deep, deep), deep), :],
            wf.at[me, team],
            line_send.at[step],
            line_recv.at[step],
            team,
            peer,
        )

    for step in range(1, count):
        line_copy(step).start()

    half = depth // 2
    outer_bits = list(range(1, bits))
    rounds = []
    slot = 0
    for stage in range(bits - 1):
        copies = []
        for side, order in enumerate((outer_bits, outer_bits[::-1])):
            held = [team]
            for bit in order[:stage]:
                held = held + [flip(index, bit) for index in held]
            for index in held:
                for step in range(1, count):
                    copies.append((slot, index, side, step, order[stage]))
                    slot += 1
        rounds.append(copies)
    held = [team]
    for bit in outer_bits:
        held = held + [flip(index, bit) for index in held]
    copies = []
    for index in held:
        for step in range(1, count):
            copies.append((slot, index, None, step, 0))
            slot += 1
    rounds.append(copies)

    def team_copy(entry):
        slot, index, side, step, bit = entry
        block = lax.rem(me + step, count)
        if side is None:
            place = wf.at[block, index]
        else:
            place = wf.at[block, index, :, side * half : (side + 1) * half]
        return move(place, place, team_send.at[slot], team_recv.at[slot], flip(team, bit), me)

    def advance(stage, distance):
        if stage == 0:
            line_copy(distance).wait_recv()
        else:
            for entry in rounds[stage - 1]:
                if entry[3] == count - distance:
                    team_copy(entry).wait_recv()
        if stage < len(rounds):
            for entry in rounds[stage]:
                if entry[3] == count - distance:
                    team_copy(entry).start()

    order = sorted(
        ((stage, distance) for stage in range(len(rounds) + 1) for distance in range(1, count)),
        key=lambda item: (2 * item[0] + 3 * item[1], item[0]),
    )

    def progress(steps):
        for _ in range(steps):
            if order:
                advance(*order.pop(0))

    def small_copy(kind, step):
        ref = (lt_in, squares_in, down_in, tables)[kind]
        return move(
            ref.at[me],
            ref.at[me],
            small_send.at[kind, step],
            small_recv.at[kind, step],
            team,
            lax.rem(me + step, count),
        )

    lt_in[me] = lt_out[...]
    for step in range(1, count):
        small_copy(0, step).start()

    gain = row_of(gain_ref)
    x_load.wait()

    @pl.loop(0, total // 128)
    def _(index):
        rows = pl.ds(pl.multiple_of(index * 128, 128), 128)
        normed, _ = norm_value(ext[rows, :].astype(f32), gain)
        ext[rows, :] = normed.astype(bf16)

    stores = [pltpu.make_async_copy(ext.at[:total], first, store_sem.at[0])]
    stores[0].start()
    for load in shard_loads:
        load.start()
    down_load.start()
    for load in mlp_loads:
        load.start()
    inner = nt(ext[:total, :], lt[...].astype(bf16)).astype(bf16)
    inner_ref[...] = inner
    length = length_ref[0]
    factor = 1.0 / math.sqrt(HEAD_DIM)
    copies = []

    def project(index, start):
        block = slice(index * RANK, (index + 1) * RANK)
        adapters = split_rows(lt[block, :])
        ext[total:, :] = adapters
        gram = nt(adapters, adapters)
        columns = slice(start, start + 256)
        product = nn(ext[...], weights[index, :, columns])
        local_right = right[index, :, columns]
        squares, full = direction(
            square_sums(weights.at[index], columns), product[total:], gram, local_right
        )
        norms = jnp.sqrt(squares)
        norms_ref[index : index + 1, columns] = norms
        full_ref[index, :, columns] = full
        z = product[:total] + nn(inner, padded_right(local_right, index, 3, SCALE))
        summed[index, :, columns] = z.astype(bf16)
        y = z * (mags[index : index + 1, columns] / norms)
        if index == 2:
            values[:, columns] = y.astype(bf16)
        else:
            for head in range(2):
                part = y[:, head * HEAD_DIM : (head + 1) * HEAD_DIM]
                cosines, sines = turning(angles[...])
                turned = part * cosines + pltpu.roll(part, HEAD_DIM // 2, 1) * sines
                place = slice(start + head * HEAD_DIM, start + (head + 1) * HEAD_DIM)
                (query if index == 0 else keys)[:, place] = turned.astype(bf16)

    def attend(head):
        place = slice(head * HEAD_DIM, (head + 1) * HEAD_DIM)
        turned_values = values[:, place].astype(f32).T.astype(bf16)
        for block in range(total // 256):
            reach = (block + 1) * 256
            at = slice(block * 256, reach)
            scores = nt(keys[:reach, place], query[at, place])
            spots = lax.broadcasted_iota(jnp.int32, (reach, 256), 0)
            asking = lax.broadcasted_iota(jnp.int32, (reach, 256), 1) + block * 256
            allowed = (spots <= asking) & (spots < length)
            scores = jnp.where(allowed, scores * factor, mask_fill)
            peak = jnp.max(scores, axis=0, keepdims=True)
            exps = jnp.exp(scores - peak)
            totals = jnp.sum(exps, axis=0, keepdims=True)
            probs = (exps * (1.0 / totals)).astype(bf16)
            mixed = nn(turned_values[:, :reach], probs)
            att[at, place] = mixed.T.astype(bf16)
            lse[head : head + 1, at] = peak + jnp.log(totals)
        for step in range(1, count):
            peer = lax.rem(me + step, count)
            copy = move(
                att.at[pl.ds(pl.multiple_of(peer * share, share), share), place],
                gathered.at[me, :, place],
                send_sem.at[head, step],
                recv_sem.at[head, step],
                team,
                peer,
            )
            copy.start()
            copies.append(copy)

    def exit_stats():
        for load in shard_loads:
            load.wait()
        down_load.wait()
        for index, (pieces, chunk) in enumerate(((lt_out[...], 64), (lt_down[...], 128))):
            adapters = split_rows(pieces)
            gram = nt(adapters, adapters)
            for start in range(0, depth, 512):
                columns = slice(start, start + 512)
                if index == 0:
                    weight = wf[me, :, :, columns].reshape(group, 512)
                    low = weight.astype(f32)
                    sums = jnp.sum(low * low, axis=0, keepdims=True)
                else:
                    weight = w_down[:, columns]
                    sums = square_sums(w_down, columns)
                squares, full = direction(
                    sums, nn(adapters, weight), gram, right_exit[index, :, columns]
                )
                squares_in[me, index : index + 1, columns] = squares
                if index == 1:
                    down_in[me, :, columns] = full.astype(bf16)
        for step in range(1, count):
            small_copy(1, step).start()
        for step in range(1, count):
            small_copy(2, step).start()

    for load in loads:
        load.wait()
    for start in range(0, group, 256):
        for index in range(3):
            project(index, start)
        for head in range(start // HEAD_DIM, start // HEAD_DIM + 2):
            attend(head)
            progress(1)
        if start == 0:
            exit_stats()
            progress(2)
    for source, target in (
        (summed, summed_any),
        (query, query_any),
        (keys, keys_any),
        (values, values_any),
        (att, att_any),
    ):
        stores.append(pltpu.make_async_copy(source, target, store_sem.at[len(stores)]))
        stores[-1].start()
    progress(1)
    gathered[me] = att[pl.ds(pl.multiple_of(me * share, share), share), :]

    units = mags_mlp.shape[1]
    for index in range(2):
        mlp_loads[index].wait()
        adapters = split_rows(lt_mlp[index * RANK : (index + 1) * RANK, :])
        squares, full = direction(
            square_sums(w_mlp.at[index], slice(0, units)),
            nn(adapters, w_mlp[index]),
            nt(adapters, adapters),
            right_mlp[index],
        )
        norms = jnp.sqrt(squares)
        norms_mlp[index : index + 1, :] = norms
        full_mlp[index] = full
        tables[me, index : index + 1, :units] = norms
        tables[me, index + 2 : index + 3, :units] = mags_mlp[index : index + 1, :] - norms
        progress(1)
    for index in range(3):
        norms = norms_ref[index : index + 1, :]
        at = slice(index * group, (index + 1) * group)
        tables[me, 4:5, at] = norms
        tables[me, 5:6, at] = mags[index : index + 1, :] - norms
    for step in range(1, count):
        small_copy(3, step).start()
    for step in range(1, count):
        small_copy(0, step).wait()
    for index in range(count):
        lt_full[:, index * group : (index + 1) * group] = lt_in[index]
    for copy in copies:
        copy.wait()
    for index in range(count):
        ext_out[:share, index * group : (index + 1) * group] = gathered[index]
    adapters = split_rows(lt_full[...])
    ext_out[share:, :] = adapters
    gram = nt(adapters, adapters)
    inner_low = adapters[:RANK]
    inner = nt(ext_out[:share, :], inner_low)
    inner_out[...] = inner
    low = inner.astype(bf16)
    own_load.wait()
    for step in range(1, count):
        small_copy(1, step).wait()
    squares = squares_in[0]
    for index in range(1, count):
        squares = squares + squares_in[index]
    exit_norms[...] = jnp.sqrt(squares)
    progress(len(order))
    store_full = [
        pltpu.make_async_copy(
            wf.at[index // teams, index % teams],
            w_full.at[index * deep : (index + 1) * deep, :],
            store_sem.at[6 + index],
        )
        for index in range(count * teams)
    ]
    for store in store_full:
        store.start()
    for start in range(0, depth, 512):
        columns = slice(start, start + 512)
        weight = wf[:, :, :, columns].reshape(depth, 512)
        local_right = right_exit[0, :, columns]
        product = nn(ext_out[...], weight)
        _, full = direction(0.0, product[share:], gram, local_right)
        full_out[:, columns] = full
        z = product[:share] + nn(low, padded_right(local_right, 0, 1, SCALE))
        summed_out[:, columns] = z.astype(bf16)
        middle[:, columns] = x_own[:, columns].astype(f32) + z * (
            mags_out[:, columns] / exit_norms[0:1, columns]
        )
    normed, _ = norm_value(middle[...], row_of(gain_second))
    second[...] = normed.astype(bf16)
    for step in range(1, count):
        small_copy(2, step).wait()
        small_copy(3, step).wait()
    edge = 0
    for index in range(3):
        for peer in range(count):
            at = slice(index * group, (index + 1) * group)
            norm_table[0:1, edge : edge + group] = tables[peer, 4:5, at]
            norm_table[1:2, edge : edge + group] = tables[peer, 5:6, at]
            edge += group
    for index in range(2):
        for peer in range(count):
            norm_table[0:1, edge : edge + units] = tables[peer, index : index + 1, :units]
            norm_table[1:2, edge : edge + units] = tables[peer, index + 2 : index + 3, :units]
            edge += units
    for index, magnitude in ((0, mags_out), (1, mags_down)):
        norm = exit_norms[index : index + 1, :]
        norm_table[0:1, edge : edge + depth] = norm
        norm_table[1:2, edge : edge + depth] = magnitude[...] - norm
        edge += depth
    full = down_in[0].astype(f32)
    for index in range(1, count):
        full = full + down_in[index].astype(f32)
    full_down[...] = full
    for store in stores + store_full:
        store.wait()
    for step in range(1, count):
        line_copy(step).wait_send()
    for copies in rounds:
        for entry in copies:
            team_copy(entry).wait_send()


def feed_forward_kernel(
    own,
    cot,
    w_gate_any,
    w_up_any,
    w_down_any,
    lt_pair,
    lt_down_pair,
    right,
    mags,
    right_exit,
    mags_down,
    exit_norms,
    norms_ref,
    fulls,
    mags_out,
    gain_ref,
    inner_out,
    lt_out,
    full_out,
    middle_any,
    summed_any,
    gathered_any,
    w_full_any,
    part,
    early,
    early_rows,
    grad_middle,
    mixed,
    early_out,
    early_mags,
    grad_second,
    adapted,
    pieces_out,
    lth,
    lt_down,
    factors,
    w_gate,
    w_up,
    w_down,
    sec,
    cots,
    cot_own,
    parts,
    mine,
    outer,
    inner_sums,
    near,
    load_sem,
    cot_sem,
    part_sem,
    gather_send,
    gather_recv,
    sum_send,
    outer_recv,
    inner_recv,
    near_send,
    near_recv,
    exit_sem,
    own_sem,
    mixed_send,
    mixed_recv,
):
    row, me = lax.axis_index("rows"), lax.axis_index("heads")
    size, depth = own.shape
    half = size // PIECES
    inward = jnp.where(me < 2, 1, -1)
    is_end = (me == 0) | (me == 3)
    in_middle = jnp.logical_not(is_end)
    ahead, behind = me + inward, me - inward

    def move(source, target, send, recv, peer):
        return pltpu.make_async_remote_copy(
            src_ref=source,
            dst_ref=target,
            send_sem=send,
            recv_sem=recv,
            device_id=(row, peer),
            device_id_type=MESH,
        )

    def rows_of(piece):
        start = piece * half
        return pl.ds(start if isinstance(piece, int) else pl.multiple_of(start, half), half)

    def gather_copy(slot, block, piece, peer):
        place = sec.at[block, rows_of(piece), :]
        return move(place, place, gather_send.at[slot, piece], gather_recv.at[block, piece], peer)

    def gather_start(slot, block, peer):
        for piece in range(PIECES):
            gather_copy(slot, block, piece, peer).start()

    def gather_wait(block, pieces, forward=None):
        for piece in pieces:
            gather_copy(0, block, piece, ahead).wait_recv()
            if forward is not None:
                slot, peer = forward
                gather_copy(slot, block, piece, peer).start()

    right_out, right_down = right_exit.at[0], right_exit.at[1]
    norms_out, norms_down = exit_norms.at[0:1], exit_norms.at[1:2]
    greet(4)
    lth[...] = lt_pair[...].astype(bf16)
    lt_down[...] = lt_down_pair[...].astype(bf16)
    loads = [
        pltpu.make_async_copy(source, target, load_sem.at[index])
        for index, (source, target) in enumerate(
            ((w_gate_any, w_gate), (w_up_any, w_up), (w_down_any, w_down))
        )
    ]
    load_own = pltpu.make_async_copy(own, sec.at[me], own_sem)
    load_own.start()
    load_own.wait()
    gather_start(0, me, ahead)

    @pl.when(jnp.logical_not(is_end))
    def _():
        gather_start(1, me, behind)

    for load in loads:
        load.start()

    def block_at(step):
        middle = jnp.where(
            step == 0, me, jnp.where(step == 1, ahead, jnp.where(step == 2, behind, ahead + inward))
        )
        return jnp.where(is_end, jnp.where(step == 3, me, me + inward * (step + 1)), middle)

    def token_rows(step):
        return pl.ds(pl.multiple_of(block_at(step) * size, size), size)

    def cot_load(step):
        slot = lax.rem(step, 2)
        return pltpu.make_async_copy(cot.at[token_rows(step), :], cots.at[slot], cot_sem.at[slot])

    def part_store(step):
        return pltpu.make_async_copy(
            parts.at[block_at(step)], part.at[token_rows(step), :], part_sem.at[step]
        )

    own_rows = pl.ds(pl.multiple_of(me * size, size), size)
    near_store = pltpu.make_async_copy(parts.at[me], part.at[own_rows, :], part_sem.at[0])
    near_copy = move(parts.at[ahead], near, near_send, near_recv, ahead)

    cot_load(0).start()
    weights = (w_gate, w_up)
    group = gathered_any.shape[2]
    factors[...] = mags[...] / norms_ref[...]
    factor_down = mags_down[...] / norms_down[...]
    grad_left, grad_right_down = early.at[: 2 * RANK], early.at[2 * RANK :]
    grad_right = [early_rows.at[index * RANK : (index + 1) * RANK] for index in range(2)]
    grad_left_down = early_rows.at[2 * RANK : 3 * RANK]
    grad_mags = early_rows.at[3 * RANK :]
    early[...] = jnp.zeros_like(early)
    early_rows[...] = jnp.zeros_like(early_rows)
    for load in loads:
        load.wait()

    def outer_copy(slot, piece, block):
        return move(
            mine.at[block, rows_of(piece), :],
            outer.at[slot, rows_of(piece), :],
            sum_send.at[slot, piece],
            outer_recv.at[slot, piece],
            ahead,
        )

    def inner_copy(slot, piece, block, send, peer):
        return move(
            mine.at[block, rows_of(piece), :],
            inner_sums.at[slot, rows_of(piece), :],
            sum_send.at[send, piece],
            inner_recv.at[slot, piece],
            peer,
        )

    def add_into(block, piece, ref):
        at = rows_of(piece)
        mine[block, at, :] = (
            mine[block, at, :].astype(f32) + ref[at, :].astype(f32)
        ).astype(bf16)

    def pass_on(distance, piece):
        block = me + inward * distance
        outer_copy(distance, piece, me).wait_recv()
        add_into(block, piece, outer.at[distance])
        inner_copy(distance - 1, piece, block, distance - 1, ahead).start()

    def hand_out(piece):
        inner_copy(1, piece, me, 2, behind).wait_recv()
        add_into(behind, piece, inner_sums.at[1])
        inner_copy(0, piece, behind, 2, behind).start()

    def work(block, first_row, width, slot, between, after):
        at = pl.ds(first_row, width)
        x = sec[block, at, :]
        inner = nt(x, lth[...])
        inner_low = inner.astype(bf16)
        zs = [
            nn(x, weights[index][...])
            + nn(inner_low, padded_right(right[index], index, 2, SCALE))
            for index in range(2)
        ]
        gate = zs[0] * factors[0:1, :]
        upper = zs[1] * factors[1:2, :]
        sigmoid = 1.0 / (1.0 + jnp.exp(-gate))
        activated = gate * sigmoid
        hidden = (activated * upper).astype(bf16)
        right_low = right_down[...].astype(bf16)
        inner_down = nt(hidden, lt_down[...])

        parts[block, at, :] = (
            nn(hidden, w_down[...]) + SCALE * nn(inner_down.astype(bf16), right_low)
        ).astype(bf16)

        between()
        gz_down = (cots[slot, at, :].astype(f32) * factor_down).astype(bf16)
        gin_down = SCALE * nt(gz_down, right_low)
        grad_hidden = nt(gz_down, w_down[...]) + nn(gin_down.astype(bf16), lt_down[...])
        grad_left_down[...] += nn(gin_down.T.astype(bf16), hidden)
        grad_right_down[...] += SCALE * nn(inner_down.T.astype(bf16), gz_down)
        grads = (
            grad_hidden * upper * sigmoid * (1.0 + gate * (1.0 - sigmoid)),
            grad_hidden * activated,
        )
        gin = jnp.zeros((width, 2 * RANK), f32)
        gzs = []
        for index in range(2):
            grad_mags[index : index + 1, :] += jnp.sum(grads[index] * zs[index], axis=0, keepdims=True)
            gz = (grads[index] * factors[index : index + 1, :]).astype(bf16)
            gin = gin + nt(gz, padded_right(right[index], index, 2, SCALE))
            gzs.append(gz)
        gin_low = gin.astype(bf16)
        mine[block, at, :] = (
            nt(gzs[0], w_gate[...]) + nt(gzs[1], w_up[...]) + nn(gin_low, lth[...])
        ).astype(bf16)

        after()
        grad_left[...] += nn(gin.T.astype(bf16), x)
        inner_turned = inner.T.astype(bf16)
        for index in range(2):
            grad_right[index][...] += (
                SCALE * nn(inner_turned, gzs[index])[index * RANK : (index + 1) * RANK]
            )

    wide = size // 2

    @pl.when(is_end)
    def _():
        @pl.loop(0, 6)
        def _(half_step):
            step, side = half_step // 2, lax.rem(half_step, 2)
            block = block_at(step)
            for piece in range(PIECES // 2):
                gather_copy(0, block, side * (PIECES // 2) + piece, ahead).wait_recv()

            def between():
                @pl.when(side == 0)
                def _():
                    cot_load(step + 1).start()
                    cot_load(step).wait()

                @pl.when(side == 1)
                def _():
                    part_store(step).start()

            def after():
                for piece in range(PIECES // 2):
                    outer_copy(step, side * (PIECES // 2) + piece, block).start()

            work(block, pl.multiple_of(side * wide, wide), wide, lax.rem(step, 2), between, after)

        near_copy.start()

    @pl.loop(0, 4)
    def _(step):
        @pl.when(in_middle | (step == 3))
        def _():
            block = block_at(step)

            @pl.when(in_middle & (step == 2))
            def _():
                gather_wait(ahead + inward, range(PIECES), (4, behind))

            @pl.when(in_middle & (step == 3))
            def _():
                pass_on(1, 1)

            def between():
                @pl.when(in_middle & (step < 3))
                def _():
                    cot_load(step + 1).start()

                cot_load(step).wait()

                @pl.when(is_end | (step > 0))
                def _():
                    part_store(step).start()

                @pl.when(in_middle & (step == 0))
                def _():
                    for piece in range(PIECES):
                        gather_wait(behind, (piece,), (2, ahead))
                        gather_wait(ahead, (piece,), (3, behind))

                @pl.when(in_middle & (step == 2))
                def _():
                    pass_on(1, 0)

                @pl.when(in_middle & (step == 3))
                def _():
                    pass_on(1, 2)
                    pass_on(1, 3)

            work(block, 0, size, lax.rem(step, 2), between, lambda: None)

    @pl.when(in_middle)
    def _():
        pass_on(2, 0)
        pass_on(2, 1)

    for index in range(2):
        block = slice(index * RANK, (index + 1) * RANK)
        norms = norms_ref[index : index + 1, :]
        factor_grad = grad_mags[index : index + 1, :]
        shape = -factor_grad * mags[index : index + 1, :] / (norms * norms * norms)
        shaped = right[index] * shape
        pieces = nt(split_rows(shaped), weights[index][...])
        lt = lt_pair[block, :]
        grad_left[block, :] += SCALE * (
            pieces[:RANK]
            + pieces[RANK:]
            + SCALE * nn_exact(nt_exact(shaped, right[index]), lt)
        )
        grad_right[index][...] += SCALE * fulls[index] * shape
        grad_mags[index : index + 1, :] = factor_grad / norms

    @pl.when(is_end)
    def _():
        part_store(0).wait()
        for piece in range(PIECES):
            gather_copy(0, me, piece, ahead).wait_send()

    @pl.when(in_middle)
    def _():
        for piece in range(PIECES):
            for slot in range(5):
                gather_copy(slot, me, piece, ahead).wait_send()

    for step in range(1, 4):
        part_store(step).wait()
    behind_part = jnp.where(is_end, me, ahead + inward)
    width = depth // 2
    exits = [
        (middle_any, grad_middle),
        (summed_any, parts.at[behind_part]),
        (cot.at[own_rows, :], cot_own),
        (w_full_any.at[:, :width], w_gate.at[:, :width]),
        (w_full_any.at[:, width:], w_up.at[:, :width]),
    ] + [
        (gathered_any.at[index], sec.at[index, :, group : 2 * group]) for index in range(4)
    ]
    exit_loads = [
        pltpu.make_async_copy(source, target, exit_sem.at[index])
        for index, (source, target) in enumerate(exits)
    ]
    for load in exit_loads:
        load.start()

    @pl.when(in_middle)
    def _():
        hand_out(0)
        pass_on(2, 2)
        hand_out(1)
        pass_on(2, 3)
        hand_out(2)
        hand_out(3)
        for piece in range(PIECES):
            outer_copy(0, piece, me).wait_recv()
            inner_copy(0, piece, me, 0, ahead).wait_recv()
        grad_second[...] = (
            mine[me].astype(f32) + outer[0].astype(f32) + inner_sums[0].astype(f32)
        )

    @pl.when(is_end)
    def _():
        for slot in range(3):
            for piece in range(PIECES):
                outer_copy(slot, piece, me).wait_send()
        for piece in range(PIECES):
            inner_copy(0, piece, me, 0, ahead).wait_recv()
        grad_second[...] = mine[me].astype(f32) + inner_sums[0].astype(f32)

    for load in exit_loads:
        load.wait()
    rows = grad_middle[...]
    gain = row_of(gain_ref)
    inverse = lax.rsqrt(jnp.mean(rows * rows, axis=-1, keepdims=True) + norm_eps)
    scaled = grad_second[...] * gain
    grad = (
        cot_own[...].astype(f32)
        + inverse * scaled
        - rows * (inverse * inverse * inverse) * jnp.mean(rows * scaled, axis=-1, keepdims=True)
    )
    grad_middle[...] = grad
    norm = norms_out[...]
    factor_grad = jnp.sum(grad * parts[behind_part].astype(f32), axis=0, keepdims=True)
    shape = -factor_grad * mags_out[...] / (norm * norm * norm)
    shaped = right_out[...] * shape
    adapted[:size, :] = (grad * (mags_out[...] / norm)).astype(bf16)
    adapted[size:, :] = split_rows(shaped)
    gz = adapted[:size, :]
    gin = SCALE * nt(gz, right_out[...].astype(bf16))
    gin_low = gin.astype(bf16)
    def mixed_copy(step):
        peer = lax.rem(me + step, 4)
        return move(
            sec.at[peer, :, :group], mixed.at[me], mixed_send.at[step], mixed_recv.at[step], peer
        )

    for step in (2, 1, 3, 4):
        peer = lax.rem(me + step, 4)
        columns = pl.ds(pl.multiple_of(peer * group, group), group)
        moved = nt(adapted[:, :width], w_gate[columns, :width]) + nt(
            adapted[:, width:], w_up[columns, :width]
        )
        result = (moved[:size] + nn(gin_low, lt_out[:, columns].astype(bf16))).astype(bf16)
        if step == 4:
            mixed[me] = result
        else:
            sec[peer, :, :group] = result
            mixed_copy(step).start()
        pieces_out[:, columns] = moved[size:]

    gin_turned = gin.T.astype(bf16)
    mixing = nt_exact(shaped, right_out[...])
    early_mags[...] = factor_grad / norm
    early_out[:RANK, :] = SCALE * (nn(inner_out[...].T.astype(bf16), gz) + full_out[...] * shape)
    early_out[RANK:, :] = SCALE * (
        pieces_out[:RANK, :] + pieces_out[RANK:, :] + SCALE * nn_exact(mixing, lt_out[...])
    )
    for index in range(4):
        at = slice(index * group, (index + 1) * group)
        early_out[RANK:, at] += nn(gin_turned, sec[index, :, group : 2 * group])

    @pl.when(in_middle)
    def _():
        near_copy.wait_recv()
        parts[me] = (parts[me].astype(f32) + near[...].astype(f32)).astype(bf16)
        near_store.start()
        for piece in range(PIECES):
            for send in range(3):
                inner_copy(0, piece, me, send, ahead).wait_send()
        near_store.wait()

    @pl.when(is_end)
    def _():
        near_copy.wait_send()

    for step in range(1, 4):
        mixed_copy(step).wait()


def attention_back_kernel(
    teams,
    length_ref,
    query,
    keys,
    values,
    att,
    lse,
    mixed,
    summed,
    norms_ref,
    mags,
    fulls,
    inner,
    lt_triple,
    right,
    angles,
    gain_ref,
    early,
    early_out,
    early_rows,
    early_mags,
    exit_norms,
    mags_down,
    right_exit,
    full_down,
    lt_down,
    first_any,
    part,
    weights_any_query,
    weights_any_key,
    weights_any_value,
    w_down,
    x_own,
    grad_middle,
    middle,
    cot_own,
    outputs,
    input_grad,
    grad_qkv_left,
    grad_qkv_right,
    grad_qkv_mags,
    grad_mlp_left,
    grad_mlp_right,
    grad_mlp_mags,
    grad_out_left,
    grad_down_left,
    grad_exit_right,
    grad_out_mags,
    grad_down_mags,
    lth,
    gz,
    key_sums,
    value_sums,
    query_turned,
    factors,
    weights,
    mine,
    outer,
    inner_sums,
    outer_down,
    inner_down,
    block_part,
    wide,
    wide_in,
    line_in,
    whole,
    group_in,
    unit_in,
    small,
    small_line,
    small_rows,
    load_sem,
    part_sem,
    sum_send,
    outer_recv,
    inner_recv,
    down_send,
    down_outer_recv,
    down_inner_recv,
    wide_send,
    wide_recv,
    line_send,
    line_recv,
    whole_send,
    whole_recv,
    group_send,
    group_recv,
    unit_send,
    unit_recv,
    small_send,
    small_recv,
    final_send,
    final_recv,
):
    right_down, norms_down = right_exit.at[1], exit_norms.at[1:2]
    total = query.shape[0]
    depth = mine.shape[1]
    size = total // 4
    half = size // PIECES
    team, me = lax.axis_index("rows"), lax.axis_index("heads")
    inward = jnp.where(me < 2, 1, -1)
    is_end = (me == 0) | (me == 3)
    in_middle = jnp.logical_not(is_end)
    ahead, behind = me + inward, me - inward

    def move(source, target, send, recv, peer, peer_team=team):
        return pltpu.make_async_remote_copy(
            src_ref=source,
            dst_ref=target,
            send_sem=send,
            recv_sem=recv,
            device_id=(peer_team, peer),
            device_id_type=MESH,
        )

    def rows_of(block, piece=None):
        if piece is None:
            return pl.ds(pl.multiple_of(block * size, size), size)
        return pl.ds(pl.multiple_of(block * size + piece * half, half), half)

    def piece_of(piece):
        return pl.ds(piece * half, half)

    barrier = pltpu.get_barrier_semaphore()
    for step in range(1, 4):
        pl.semaphore_signal(
            barrier, inc=1, device_id=(team, lax.rem(me + step, 4)), device_id_type=MESH
        )
    for step in range(1, teams):
        pl.semaphore_signal(
            barrier, inc=1, device_id=(lax.rem(team + step, teams), me), device_id_type=MESH
        )
    pl.semaphore_wait(barrier, teams + 2)

    def down_outer(slot, piece, block):
        return move(
            part.at[rows_of(block, piece), :],
            outer_down.at[slot, piece_of(piece), :],
            down_send.at[slot, piece],
            down_outer_recv.at[slot, piece],
            ahead,
        )

    def down_inner(slot, piece, send, peer):
        return move(
            block_part.at[send, piece_of(piece), :],
            inner_down.at[slot, piece_of(piece), :],
            down_send.at[send, piece],
            down_inner_recv.at[slot, piece],
            peer,
        )

    @pl.when(is_end)
    def _():
        for piece in range(PIECES):
            down_outer(1, piece, me + inward * 3).start()
        for piece in range(PIECES):
            down_outer(0, piece, me + inward * 2).start()

    def part_load(slot, block):
        return pltpu.make_async_copy(part.at[rows_of(block), :], block_part.at[slot], part_sem.at[slot])

    @pl.when(in_middle)
    def _():
        part_load(0, ahead).start()
        part_load(1, ahead + inward).start()
        part_load(3, behind).start()

    part_load(2, me).start()

    def unit_copy(step):
        return move(
            unit_in.at[team],
            unit_in.at[team],
            unit_send.at[step],
            unit_recv.at[step],
            me,
            lax.rem(team + step, teams),
        )

    def group_copy(step):
        return move(
            group_in.at[team],
            group_in.at[team],
            group_send.at[step],
            group_recv.at[step],
            me,
            lax.rem(team + step, teams),
        )

    unit_in[team] = early_rows[...].astype(bf16)
    for step in range(1, teams):
        unit_copy(step).start()

    loads = [
        pltpu.make_async_copy(source, weights.at[index], load_sem.at[index])
        for index, source in enumerate((weights_any_query, weights_any_key, weights_any_value))
    ]
    load_first = pltpu.make_async_copy(first_any, mine, load_sem.at[3])
    for load in loads:
        load.start()
    load_first.start()

    lth[...] = lt_triple[...].astype(bf16)
    heads = query.shape[1] // HEAD_DIM
    length = length_ref[0]
    factor = 1.0 / math.sqrt(HEAD_DIM)
    factors[:3, :] = mags[...] / norms_ref[...]

    def finish(index, head, grad):
        place = slice(head * HEAD_DIM, (head + 1) * HEAD_DIM)
        if index < 2:
            cosines, sines = turning(angles[...])
            grad = grad * cosines - pltpu.roll(grad, HEAD_DIM // 2, 1) * sines
        factors[index + 3 : index + 4, place] = jnp.sum(
            grad * summed[index, :, place].astype(f32), axis=0, keepdims=True
        )
        gz[index, :, place] = (grad * factors[index : index + 1, place]).astype(bf16)

    for head in range(heads):
        place = slice(head * HEAD_DIM, (head + 1) * HEAD_DIM)
        turned_keys = keys[:, place].astype(f32).T.astype(bf16)
        key_sums[...] = jnp.zeros_like(key_sums)
        value_sums[...] = jnp.zeros_like(value_sums)
        for block in range(total // 256):
            reach = (block + 1) * 256
            at = slice(block * 256, reach)
            grad_rows = mixed[at, place]
            rows = query[at, place]
            scores = nt(keys[:reach, place], rows)
            spots = lax.broadcasted_iota(jnp.int32, (reach, 256), 0)
            asking = lax.broadcasted_iota(jnp.int32, (reach, 256), 1) + block * 256
            allowed = (spots <= asking) & (spots < length)
            scores = jnp.where(allowed, scores * factor, mask_fill)
            probs = jnp.exp(scores - lse[head : head + 1, at])
            grad_probs = nt(values[:reach, place], grad_rows)
            centre = jnp.sum(
                (grad_rows.astype(f32) * att[at, place].astype(f32)).T, axis=0, keepdims=True
            )
            raw = (probs * (grad_probs - centre) * factor).astype(bf16)
            value_sums[:reach, :] += nn(probs.astype(bf16), grad_rows)
            key_sums[:reach, :] += nn(raw, rows)
            query_turned[:, at] = nn(turned_keys[:, :reach], raw)
        finish(0, head, query_turned[...].T)
        finish(1, head, key_sums[...])
        finish(2, head, value_sums[...])

    gin = jnp.zeros((total, 3 * RANK), f32)
    for index in range(3):
        gin = gin + nt(gz[index], padded_right(right[index], index, 3, SCALE))
    gin_low = gin.astype(bf16)
    load_first.wait()
    left = nn(gin.T.astype(bf16), mine[...])
    inner_turned = inner[...].astype(f32).T.astype(bf16)
    for index in range(3):
        block = slice(index * RANK, (index + 1) * RANK)
        norms = norms_ref[index : index + 1, :]
        factor_grad = factors[index + 3 : index + 4, :]
        shape = -factor_grad * mags[index : index + 1, :] / (norms * norms * norms)
        shaped = right[index] * shape
        loads[index].wait()
        pieces = nt(split_rows(shaped), weights[index])
        lt = lt_triple[block, :]
        extra = pieces[:RANK] + pieces[RANK:] + SCALE * nn_exact(nt_exact(shaped, right[index]), lt)
        wide[block, :] = (left[block, :] + SCALE * extra).astype(bf16)
        group_in[team, block, :] = (
            SCALE * (nn(inner_turned, gz[index])[block] + fulls[index] * shape)
        ).astype(bf16)
    tail = group_in.shape[1] - 3 * RANK
    group_in[team, 3 * RANK :, :] = jnp.concatenate(
        [factors[3:6, :] / norms_ref[...], jnp.zeros((tail - 3, factors.shape[1]), f32)], axis=0
    ).astype(bf16)
    wide[3 * RANK : 6 * RANK, :] = early[...].astype(bf16)
    wide[6 * RANK :, :] = early_out[...].astype(bf16)
    for step in range(1, teams):
        group_copy(step).start()

    tiles = wide.shape[0] // 16
    parts_of_tile = teams // tiles
    stretch = depth // parts_of_tile

    def tile_of(owner):
        return (
            pl.ds(pl.multiple_of(lax.rem(owner, tiles) * 16, 16), 16),
            pl.ds(pl.multiple_of((owner // tiles) * stretch, stretch), stretch),
        )

    def wide_copy(step):
        owner = lax.rem(team + step, teams)
        across, along = tile_of(owner)
        return move(
            wide.at[across, along],
            wide_in.at[team],
            wide_send.at[step],
            wide_recv.at[step],
            me,
            owner,
        )

    for step in range(1, teams):
        wide_copy(step).start()
    across, along = tile_of(team)
    wide_in[team] = wide[across, along]

    def add_down(send, piece, ref):
        at = piece_of(piece)
        block_part[send, at, :] = (
            block_part[send, at, :].astype(f32) + ref[at, :].astype(f32)
        ).astype(bf16)

    @pl.when(in_middle)
    def _():
        part_load(1, me).wait()
        for piece in range(PIECES):
            down_outer(1, piece, me).wait_recv()
            add_down(1, piece, outer_down.at[1])
            down_inner(1, piece, 1, ahead).start()

    def grad_block(block):
        at = rows_of(block)
        mine[at, :] = (
            nt(gz[0, at, :], weights[0])
            + nt(gz[1, at, :], weights[1])
            + nt(gz[2, at, :], weights[2])
            + nn(
                (
                    SCALE
                    * (
                        nt(gz[0, at, :], padded_right(right[0], 0, 3, 1.0))
                        + nt(gz[1, at, :], padded_right(right[1], 1, 3, 1.0))
                        + nt(gz[2, at, :], padded_right(right[2], 2, 3, 1.0))
                    )
                ).astype(bf16),
                lth[...],
            )
        ).astype(bf16)

    def outer_copy(slot, piece, block):
        return move(
            mine.at[rows_of(block, piece), :],
            outer.at[slot, piece_of(piece), :],
            sum_send.at[slot, piece],
            outer_recv.at[slot, piece],
            ahead,
        )

    def inner_copy(slot, piece, block, send, peer):
        return move(
            mine.at[rows_of(block, piece), :],
            inner_sums.at[slot, piece_of(piece), :],
            sum_send.at[send, piece],
            inner_recv.at[slot, piece],
            peer,
        )

    @pl.loop(0, 4)
    def _(step):
        middle_block = jnp.where(
            step == 0, ahead + inward, jnp.where(step == 1, ahead, jnp.where(step == 2, behind, me))
        )
        grad_block(jnp.where(is_end, me + inward * (3 - step), middle_block))

        @pl.when(is_end & (step == 0))
        def _():
            for piece in range(PIECES):
                outer_copy(2, piece, me + inward * 3).start()

    def add_into(block, piece, ref):
        at = rows_of(block, piece)
        mine[at, :] = (
            mine[at, :].astype(f32) + ref[piece_of(piece), :].astype(f32)
        ).astype(bf16)

    for step in range(1, teams):
        wide_copy(step).wait_recv()
    gathered = jnp.zeros((16, stretch), f32)
    for index in range(teams):
        gathered = gathered + wide_in[index].astype(f32)
    line_in[me] = gathered.astype(bf16)

    def line_copy(step):
        return move(
            line_in.at[me],
            line_in.at[me],
            line_send.at[step],
            line_recv.at[step],
            lax.rem(me + step, 4),
        )

    for step in range(1, 4):
        line_copy(step).start()

    @pl.when(in_middle)
    def _():
        part_load(0, me).wait()
        part_load(3, me).wait()
        for piece in range(PIECES):
            down_outer(0, piece, me).wait_recv()
            add_down(0, piece, outer_down.at[0])
            down_inner(0, piece, 0, ahead).start()
        for piece in range(PIECES):
            down_inner(1, piece, 0, ahead).wait_recv()
            add_down(3, piece, inner_down.at[1])
            down_inner(0, piece, 3, behind).start()
        for piece in range(PIECES):
            outer_copy(2, piece, me).wait_recv()
            add_into(ahead + inward, piece, outer.at[2])
            inner_copy(1, piece, ahead + inward, 1, ahead).start()

    part_load(2, me).wait()

    for piece in range(PIECES):
        down_inner(0, piece, 0, ahead).wait_recv()

    load_own = [
        pltpu.make_async_copy(source, target, load_sem.at[index])
        for index, (source, target) in enumerate(
            ((middle, input_grad), (cot_own.at[rows_of(me), :], outputs))
        )
    ]
    for load in load_own:
        load.start()
    norm_down = norms_down[...]
    done = block_part[2].astype(f32) + inner_down[0].astype(f32)
    for load in load_own:
        load.wait()
    small[0:1, :] = jnp.sum(outputs[...].astype(f32) * done, axis=0, keepdims=True)
    small[1:2, :] = early_mags[...]
    outputs[...] = (input_grad[...] + done * (mags_down[...] / norm_down)).astype(bf16)
    small_line[me] = small[...]

    def small_copy(step):
        return move(
            small_line.at[me],
            small_line.at[me],
            small_send.at[step],
            small_recv.at[step],
            lax.rem(me + step, 4),
        )

    for step in range(1, 4):
        small_copy(step).start()

    @pl.when(is_end)
    def _():
        for piece in range(PIECES):
            outer_copy(1, piece, ahead + inward).start()
        for piece in range(PIECES):
            outer_copy(0, piece, ahead).start()

    load_wide = [
        pltpu.make_async_copy(
            w_down.at[:, index * 512 : (index + 1) * 512],
            weights.at[index, : w_down.shape[0], :],
            load_sem.at[index],
        )
        for index in range(3)
    ]
    load_wide.append(
        pltpu.make_async_copy(w_down.at[:1024, 1536:], gz.at[0], load_sem.at[3])
    )
    load_wide.append(
        pltpu.make_async_copy(
            w_down.at[1024:, 1536:], gz.at[1, : w_down.shape[0] - 1024, :], load_sem.at[4]
        )
    )
    for load in load_wide:
        load.start()

    for step in range(1, 4):
        line_copy(step).wait_recv()
    whole[team] = (
        line_in[0].astype(f32)
        + line_in[1].astype(f32)
        + line_in[2].astype(f32)
        + line_in[3].astype(f32)
    ).astype(bf16)

    def whole_copy(step):
        return move(
            whole.at[team],
            whole.at[team],
            whole_send.at[step],
            whole_recv.at[step],
            me,
            lax.rem(team + step, teams),
        )

    for step in range(1, teams):
        whole_copy(step).start()
    for step in range(1, 4):
        small_copy(step).wait_recv()
    small_rows[team] = small_line[0] + small_line[1] + small_line[2] + small_line[3]

    def final_copy(step):
        return move(
            small_rows.at[team],
            small_rows.at[team],
            final_send.at[step],
            final_recv.at[step],
            me,
            lax.rem(team + step, teams),
        )

    for step in range(1, teams):
        final_copy(step).start()

    @pl.when(in_middle)
    def _():
        for piece in range(PIECES):
            inner_copy(1, piece, me, 0, ahead).wait_recv()
            add_into(behind, piece, inner_sums.at[1])
            inner_copy(0, piece, behind, 2, behind).start()
            outer_copy(1, piece, me).wait_recv()
            add_into(ahead, piece, outer.at[1])
            inner_copy(0, piece, ahead, 0, ahead).start()

    for step in range(1, teams):
        final_copy(step).wait_recv()
    sums = jnp.zeros((2, depth), f32)
    for index in range(teams):
        sums = sums + small_rows[index]
    grad_down_mags[...] = sums[0:1] / norm_down
    grad_out_mags[...] = sums[1:2]
    shape = -sums[0:1] * mags_down[...] / (norm_down * norm_down * norm_down)
    shaped = right_down[...] * shape
    right_extra = SCALE * full_down[...] * shape
    for load in load_wide:
        load.wait()
    cut = split_rows(shaped)
    units = w_down.shape[0]
    pieces = (
        nt(cut[:, :512], weights[0, :units, :])
        + nt(cut[:, 512:1024], weights[1, :units, :])
        + nt(cut[:, 1024:1536], weights[2, :units, :])
    )
    last = cut[:, 1536:]
    mixing = nt_exact(shaped, right_down[...])
    lt = lt_down[...]
    extra = pieces[:RANK] + pieces[RANK:] + SCALE * nn_exact(mixing, lt)
    ends = [nt(last, gz[0]), nt(last, gz[1, : units - 1024, :])]
    grad_down_left[:, :1024] = SCALE * (extra[:, :1024] + ends[0][:RANK] + ends[0][RANK:])
    grad_down_left[:, 1024:] = SCALE * (extra[:, 1024:] + ends[1][:RANK] + ends[1][RANK:])

    for step in range(1, teams):
        group_copy(step).wait_recv()
        unit_copy(step).wait_recv()
        whole_copy(step).wait_recv()
    group_total = jnp.zeros(group_in.shape[1:], f32)
    unit_total = jnp.zeros(unit_in.shape[1:], f32)
    for index in range(teams):
        group_total = group_total + group_in[index].astype(f32)
        unit_total = unit_total + unit_in[index].astype(f32)
    for index in range(3):
        grad_qkv_right[index] = group_total[index * RANK : (index + 1) * RANK]
    grad_qkv_mags[...] = group_total[3 * RANK : 3 * RANK + 3]
    for index in range(2):
        grad_mlp_right[index] = unit_total[index * RANK : (index + 1) * RANK]
    grad_down_left[...] += unit_total[2 * RANK : 3 * RANK]
    grad_mlp_mags[...] = unit_total[3 * RANK : 3 * RANK + 2]
    for part_index in range(parts_of_tile):
        along = slice(part_index * stretch, (part_index + 1) * stretch)
        tile = [whole[part_index * tiles + index].astype(f32) for index in range(7)]
        for index in range(3):
            grad_qkv_left[index, :, along] = tile[index]
        for index in range(2):
            grad_mlp_left[index, :, along] = tile[3 + index]
        grad_exit_right[1, :, along] = tile[5] + right_extra[:, along]
        grad_exit_right[0, :, along] = tile[6]
    group = query.shape[1]
    within = min(group, stretch)
    for index in range(group // within):
        spot = me * group + index * within
        grad_out_left[:, index * within : (index + 1) * within] = whole[
            (spot // stretch) * tiles + 7,
            :,
            pl.ds(pl.multiple_of(lax.rem(spot, stretch), within), within),
        ].astype(f32)

    load_end = [
        pltpu.make_async_copy(source, target, load_sem.at[index])
        for index, (source, target) in enumerate(
            ((grad_middle, input_grad), (x_own.at[rows_of(me), :], block_part.at[2]))
        )
    ]
    for load in load_end:
        load.start()
    for load in load_end:
        load.wait()
    gain = row_of(gain_ref)

    def close(grad):
        rows = block_part[2].astype(f32)
        inverse = lax.rsqrt(jnp.mean(rows * rows, axis=-1, keepdims=True) + norm_eps)
        scaled = grad * gain
        input_grad[...] = (
            input_grad[...]
            + inverse * scaled
            - rows
            * (inverse * inverse * inverse)
            * jnp.mean(rows * scaled, axis=-1, keepdims=True)
        )

    @pl.when(in_middle)
    def _():
        for piece in range(PIECES):
            outer_copy(0, piece, me).wait_recv()
            inner_copy(0, piece, me, 0, ahead).wait_recv()
        close(mine[rows_of(me), :].astype(f32) + outer[0].astype(f32) + inner_sums[0].astype(f32))
        for piece in range(PIECES):
            for send in (0, 1, 3):
                down_inner(0, piece, send, ahead).wait_send()
            for send in range(3):
                inner_copy(0, piece, me, send, ahead).wait_send()

    @pl.when(is_end)
    def _():
        for piece in range(PIECES):
            inner_copy(0, piece, me, 0, ahead).wait_recv()
        close(mine[rows_of(me), :].astype(f32) + inner_sums[0].astype(f32))
        for piece in range(PIECES):
            for slot in range(2):
                down_outer(slot, piece, me).wait_send()
            for slot in range(3):
                outer_copy(slot, piece, me).wait_send()

    for step in range(1, 4):
        line_copy(step).wait_send()
        small_copy(step).wait_send()
    for step in range(1, teams):
        unit_copy(step).wait_send()
        group_copy(step).wait_send()
        wide_copy(step).wait_send()
        whole_copy(step).wait_send()
        final_copy(step).wait_send()


def call(kernel, outs, ins, specs=None, out_specs=None, scratch=(), flops=0, moved=0, collective=None):
    extra = {} if collective is None else {"collective_id": collective, "has_side_effects": True}
    return pl.pallas_call(
        kernel,
        out_shape=[jax.ShapeDtypeStruct(shape, kind) for shape, kind in outs],
        in_specs=specs or [VMEM] * len(ins),
        out_specs=out_specs or [VMEM] * len(outs),
        scratch_shapes=list(scratch),
        cost_estimate=pl.CostEstimate(flops=flops, bytes_accessed=moved, transcendentals=0),
        compiler_params=pltpu.CompilerParams(vmem_limit_bytes=LIMIT, **extra),
    )(*ins)


def rope_table(length, width):
    half = width // 2
    freqs = np.float32(rope_base) ** (-(np.arange(half, dtype=np.float32) * 2.0) / width)
    angles = np.arange(length, dtype=np.float32)[:, None] * freqs[None, :].astype(np.float32)
    return np.concatenate([np.cos(angles), np.sin(angles)], axis=1).astype(np.float32)


def local(
    inputs,
    cotangent,
    lengths,
    gain_attn,
    gain_mlp,
    w_query,
    w_key,
    w_value,
    w_out,
    w_gate,
    w_up,
    w_down,
    qkv_left,
    qkv_right,
    qkv_mags,
    mlp_left,
    mlp_right,
    mlp_mags,
    out_left,
    down_left,
    exit_right,
    out_mags,
    down_mags,
):
    count = lax.axis_size("heads")
    teams = lax.axis_size("rows")
    total, depth = inputs.shape
    share = total // count
    group = w_query.shape[1]
    units = w_gate.shape[1]
    heads = group // HEAD_DIM
    deep = group // teams
    lt_qkv = jnp.transpose(qkv_left, (0, 2, 1)).reshape(3 * RANK, depth)
    lt_mlp = jnp.transpose(mlp_left, (0, 2, 1)).reshape(2 * RANK, depth)
    angles = jnp.asarray(rope_table(total, HEAD_DIM))
    out_mag, down_mag = out_mags.reshape(1, depth), down_mags.reshape(1, depth)
    bits = teams.bit_length() - 1
    assert teams == 1 << bits
    slots = 3 * (2 * (2 ** (bits - 1) - 1) + 2 ** (bits - 1))

    (
        first,
        query,
        keys,
        values,
        att,
        qkv_summed,
        w_full,
        lse,
        qkv_inner,
        qkv_norms,
        qkv_full,
        gathered,
        middle,
        second,
        out_summed,
        out_inner,
        full_out,
        lt_out,
        exit_norms,
        full_down,
        mlp_norms,
        mlp_full,
        norm_stats,
    ) = call(
        functools.partial(attention_forward_kernel, count, teams),
        [
            ((total, depth), bf16),
            ((total, group), bf16),
            ((total, group), bf16),
            ((total, group), bf16),
            ((total, group), bf16),
            ((3, total, group), bf16),
            ((depth, depth), bf16),
            ((heads, total), f32),
            ((total, 3 * RANK), bf16),
            ((3, group), f32),
            ((3, RANK, group), f32),
            ((count, share, group), bf16),
            ((share, depth), f32),
            ((share, depth), bf16),
            ((share, depth), bf16),
            ((share, RANK), f32),
            ((RANK, depth), f32),
            ((RANK, depth), f32),
            ((2, depth), f32),
            ((RANK, depth), f32),
            ((2, units), f32),
            ((2, RANK, units), f32),
            ((2, 3 * count * group + 2 * count * units + 2 * depth), f32),
        ],
        (
            lengths,
            gain_attn,
            lt_qkv,
            qkv_right,
            qkv_mags,
            angles,
            out_left.T,
            down_left.T,
            exit_right,
            out_mag,
            down_mag,
            gain_mlp,
            lt_mlp,
            mlp_right,
            mlp_mags,
            inputs,
            w_query,
            w_key,
            w_value,
            w_out,
            w_down,
            w_gate,
            w_up,
        ),
        specs=[SMEM] + [VMEM] * 14 + [ANY] * 8,
        out_specs=[ANY] * 7 + [VMEM] * 16,
        scratch=(
            pltpu.VMEM((total + 2 * RANK, depth), bf16),
            pltpu.VMEM((3, depth, group), bf16),
            pltpu.VMEM((total, group), bf16),
            pltpu.VMEM((total, group), bf16),
            pltpu.VMEM((total, group), bf16),
            pltpu.VMEM((total, group), bf16),
            pltpu.VMEM((3, total, group), bf16),
            pltpu.VMEM((count, teams, deep, depth), bf16),
            pltpu.VMEM((units, depth), bf16),
            pltpu.VMEM((2, depth, units), bf16),
            pltpu.VMEM((share, depth), bf16),
            pltpu.VMEM((share + 2 * RANK, depth), bf16),
            pltpu.VMEM((count, RANK, group), f32),
            pltpu.VMEM((count, 2, depth), f32),
            pltpu.VMEM((count, RANK, depth), bf16),
            pltpu.VMEM((count, 8, depth), f32),
            pltpu.SemaphoreType.DMA((8 + teams,)),
            pltpu.SemaphoreType.DMA((6 + count * teams,)),
            pltpu.SemaphoreType.DMA((heads, count)),
            pltpu.SemaphoreType.DMA((heads, count)),
            pltpu.SemaphoreType.DMA((count,)),
            pltpu.SemaphoreType.DMA((count,)),
            pltpu.SemaphoreType.DMA((slots,)),
            pltpu.SemaphoreType.DMA((slots,)),
            pltpu.SemaphoreType.DMA((4, count)),
            pltpu.SemaphoreType.DMA((4, count)),
        ),
        flops=6 * total * depth * group + 4 * total * total * group,
        moved=2 * (2 * total * depth + 3 * depth * group + 8 * total * group),
        collective=0,
    )
    assert count == 4
    (
        part,
        early,
        early_rows,
        grad_middle,
        mixed,
        early_out,
        early_mags,
    ) = call(
        feed_forward_kernel,
        [
            ((total, depth), bf16),
            ((3 * RANK, depth), f32),
            ((4 * RANK, units), f32),
            ((share, depth), f32),
            ((count, share, group), bf16),
            ((2 * RANK, depth), f32),
            ((1, depth), f32),
        ],
        (
            second,
            cotangent,
            w_gate,
            w_up,
            w_down,
            lt_mlp,
            down_left.T,
            mlp_right,
            mlp_mags,
            exit_right,
            down_mag,
            exit_norms,
            mlp_norms,
            mlp_full,
            out_mag,
            gain_mlp,
            out_inner,
            lt_out,
            full_out,
            middle,
            out_summed,
            gathered,
            w_full,
        ),
        specs=[ANY] * 5 + [VMEM] * 14 + [ANY] * 4,
        out_specs=[ANY] + [VMEM] * 6,
        scratch=(
            pltpu.VMEM((share, depth), f32),
            pltpu.VMEM((share + 2 * RANK, depth), bf16),
            pltpu.VMEM((2 * RANK, depth), f32),
            pltpu.VMEM((2 * RANK, depth), bf16),
            pltpu.VMEM((RANK, units), bf16),
            pltpu.VMEM((2, units), f32),
            pltpu.VMEM((depth, units), bf16),
            pltpu.VMEM((depth, units), bf16),
            pltpu.VMEM((units, depth), bf16),
            pltpu.VMEM((count, share, depth), bf16),
            pltpu.VMEM((2, share, depth), bf16),
            pltpu.VMEM((share, depth), bf16),
            pltpu.VMEM((count, share, depth), bf16),
            pltpu.VMEM((count, share, depth), bf16),
            pltpu.VMEM((3, share, depth), bf16),
            pltpu.VMEM((2, share, depth), bf16),
            pltpu.VMEM((share, depth), bf16),
            pltpu.SemaphoreType.DMA((3,)),
            pltpu.SemaphoreType.DMA((2,)),
            pltpu.SemaphoreType.DMA((4,)),
            pltpu.SemaphoreType.DMA((5, PIECES)),
            pltpu.SemaphoreType.DMA((4, PIECES)),
            pltpu.SemaphoreType.DMA((3, PIECES)),
            pltpu.SemaphoreType.DMA((3, PIECES)),
            pltpu.SemaphoreType.DMA((2, PIECES)),
            pltpu.SemaphoreType.DMA,
            pltpu.SemaphoreType.DMA,
            pltpu.SemaphoreType.DMA((9,)),
            pltpu.SemaphoreType.DMA,
            pltpu.SemaphoreType.DMA((4,)),
            pltpu.SemaphoreType.DMA((4,)),
        ),
        flops=12 * total * depth * units,
        moved=2 * (3 * depth * units + 4 * total * depth),
        collective=1,
    )
    results = call(
        functools.partial(attention_back_kernel, teams),
        [
            ((share, depth), bf16),
            ((share, depth), f32),
            ((3, RANK, depth), f32),
            ((3, RANK, group), f32),
            ((3, group), f32),
            ((2, RANK, depth), f32),
            ((2, RANK, units), f32),
            ((2, units), f32),
            ((RANK, group), f32),
            ((RANK, units), f32),
            ((2, RANK, depth), f32),
            ((1, depth), f32),
            ((1, depth), f32),
        ],
        (
            lengths,
            query,
            keys,
            values,
            att,
            lse,
            mixed.reshape(total, group),
            qkv_summed,
            qkv_norms,
            qkv_mags,
            qkv_full,
            qkv_inner,
            lt_qkv,
            qkv_right,
            angles,
            gain_attn,
            early,
            early_out,
            early_rows,
            early_mags,
            exit_norms,
            down_mag,
            exit_right,
            full_down,
            down_left.T,
            first,
            part,
            w_query,
            w_key,
            w_value,
            w_down,
            inputs,
            grad_middle,
            middle,
            cotangent,
        ),
        specs=[SMEM] + [VMEM] * 24 + [ANY] * 10,
        scratch=(
            pltpu.VMEM((3 * RANK, depth), bf16),
            pltpu.VMEM((3, total, group), bf16),
            pltpu.VMEM((total, HEAD_DIM), f32),
            pltpu.VMEM((total, HEAD_DIM), f32),
            pltpu.VMEM((HEAD_DIM, total), f32),
            pltpu.VMEM((8, group), f32),
            pltpu.VMEM((3, depth, group), bf16),
            pltpu.VMEM((total, depth), bf16),
            pltpu.VMEM((3, share, depth), bf16),
            pltpu.VMEM((2, share, depth), bf16),
            pltpu.VMEM((2, share, depth), bf16),
            pltpu.VMEM((2, share, depth), bf16),
            pltpu.VMEM((4, share, depth), bf16),
            pltpu.VMEM((8 * RANK, depth), bf16),
            pltpu.VMEM((teams, 16, depth * 8 // teams), bf16),
            pltpu.VMEM((count, 16, depth * 8 // teams), bf16),
            pltpu.VMEM((teams, 16, depth * 8 // teams), bf16),
            pltpu.VMEM((teams, 4 * RANK, group), bf16),
            pltpu.VMEM((teams, 4 * RANK, units), bf16),
            pltpu.VMEM((2, depth), f32),
            pltpu.VMEM((count, 2, depth), f32),
            pltpu.VMEM((teams, 2, depth), f32),
            pltpu.SemaphoreType.DMA((5,)),
            pltpu.SemaphoreType.DMA((4,)),
            pltpu.SemaphoreType.DMA((3, PIECES)),
            pltpu.SemaphoreType.DMA((3, PIECES)),
            pltpu.SemaphoreType.DMA((2, PIECES)),
            pltpu.SemaphoreType.DMA((4, PIECES)),
            pltpu.SemaphoreType.DMA((2, PIECES)),
            pltpu.SemaphoreType.DMA((2, PIECES)),
            pltpu.SemaphoreType.DMA((teams,)),
            pltpu.SemaphoreType.DMA((teams,)),
            pltpu.SemaphoreType.DMA((count,)),
            pltpu.SemaphoreType.DMA((count,)),
            pltpu.SemaphoreType.DMA((teams,)),
            pltpu.SemaphoreType.DMA((teams,)),
            pltpu.SemaphoreType.DMA((teams,)),
            pltpu.SemaphoreType.DMA((teams,)),
            pltpu.SemaphoreType.DMA((teams,)),
            pltpu.SemaphoreType.DMA((teams,)),
            pltpu.SemaphoreType.DMA((count,)),
            pltpu.SemaphoreType.DMA((count,)),
            pltpu.SemaphoreType.DMA((teams,)),
            pltpu.SemaphoreType.DMA((teams,)),
        ),
        flops=6 * total * depth * group + 10 * total * total * group,
        moved=2 * (2 * total * depth + 3 * depth * group + 8 * total * group),
        collective=2,
    )
    (
        outputs,
        input_grad,
        grad_qkv_left,
        grad_qkv_right,
        grad_qkv_mags,
        grad_mlp_left,
        grad_mlp_right,
        grad_mlp_mags,
        grad_out_left,
        grad_down_left,
        grad_exit_right,
        grad_out_mags,
        grad_down_mags,
    ) = results
    results = [*results, norm_stats]

    def hand_over(*refs):
        half = len(results)
        for index in range(half):
            refs[half + index][...] = refs[index][...]

    (
        outputs,
        input_grad,
        grad_qkv_left,
        grad_qkv_right,
        grad_qkv_mags,
        grad_mlp_left,
        grad_mlp_right,
        grad_mlp_mags,
        grad_out_left,
        grad_down_left,
        grad_exit_right,
        grad_out_mags,
        grad_down_mags,
        norm_stats,
    ) = call(
        hand_over,
        [(item.shape, item.dtype) for item in results],
        results,
        moved=2 * share * depth * 6,
    )
    return (
        outputs,
        input_grad,
        jnp.transpose(grad_qkv_left, (0, 2, 1)),
        grad_qkv_right,
        grad_qkv_mags,
        jnp.transpose(grad_mlp_left, (0, 2, 1)),
        grad_mlp_right,
        grad_mlp_mags,
        grad_out_left.T,
        grad_down_left.T,
        grad_exit_right,
        grad_out_mags.reshape(depth),
        grad_down_mags.reshape(depth),
        norm_stats,
    )


def solution(mesh):
    placed = (
        P("rows", None),
        P("rows", None),
        P("rows"),
        P(),
        P(),
        P(None, "heads"),
        P(None, "heads"),
        P(None, "heads"),
        P("heads", None),
        P(None, "heads"),
        P(None, "heads"),
        P("heads", None),
        P(),
        P(None, None, "heads"),
        P(None, "heads"),
        P(),
        P(None, None, "heads"),
        P(None, "heads"),
        P("heads", None),
        P("heads", None),
        P(),
        P(),
        P(),
    )
    return jax.shard_map(
        local,
        mesh=mesh,
        in_specs=placed,
        out_specs=(
            P(("rows", "heads"), None),
            P(("rows", "heads"), None),
            P(),
            P(None, None, "heads"),
            P(None, "heads"),
            P(),
            P(None, None, "heads"),
            P(None, "heads"),
            P("heads", None),
            P("heads", None),
            P(),
            P(),
            P(),
            P(),
        ),
        check_vma=False,
    )
```

```python
import functools
import math

import jax
import jax.numpy as jnp
import numpy as np
from jax import lax
from jax.experimental import pallas as pl
from jax.experimental.pallas import tpu as pltpu
from jax.sharding import PartitionSpec as P

HEAD_DIM = 128
RANK = 16
norm_eps = 1e-05
rope_base = 10000.0
mask_fill = -1e30
SCALE = 32.0 / RANK

f32 = jnp.float32
bf16 = jnp.bfloat16
MESH = pl.DeviceIdType.MESH
VMEM = pl.BlockSpec(memory_space=pltpu.VMEM)
SMEM = pl.BlockSpec(memory_space=pltpu.SMEM)
ANY = pl.BlockSpec(memory_space=pl.ANY)
LIMIT = 63 << 20
PIECES = 4


def nn(left, right):
    return jnp.dot(left, right, preferred_element_type=f32)


def nt(left, right):
    return lax.dot_general(left, right, (((1,), (1,)), ((), ())), preferred_element_type=f32)


def nn_exact(left, right):
    return jnp.dot(left, right, precision=lax.Precision.HIGHEST, preferred_element_type=f32)


def nt_exact(left, right):
    return lax.dot_general(
        left,
        right,
        (((1,), (1,)), ((), ())),
        precision=lax.Precision.HIGHEST,
        preferred_element_type=f32,
    )


def split_rows(field):
    high = field.astype(bf16)
    return jnp.concatenate([high, (field - high.astype(f32)).astype(bf16)], axis=0)


def square_sums(ref, columns, chunk=128):
    depth = ref.shape[0]
    width = columns.size if isinstance(columns, pl.Slice) else columns.stop - columns.start

    def step(index, total):
        piece = ref[pl.ds(pl.multiple_of(index * chunk, chunk), chunk), columns].astype(f32)
        return total + jnp.sum((piece * piece).reshape(chunk // 8, 8, width), axis=0)

    total = lax.fori_loop(0, depth // chunk, step, jnp.zeros((8, width), f32))
    return jnp.sum(total, axis=0, keepdims=True)


def direction(squares, pieces, gram, right):
    plain = pieces[:RANK] + pieces[RANK:]
    turned = nn_exact(gram, jnp.concatenate([right, right], axis=0))
    full = plain + SCALE * (turned[:RANK] + turned[RANK:])
    return squares + SCALE * jnp.sum(right * (plain + full), axis=0, keepdims=True), full


def padded_right(right, at, count, factor):
    low = factor * right.astype(bf16).astype(f32)
    zero = jnp.zeros_like(low)
    return jnp.concatenate([low if slot == at else zero for slot in range(count)], axis=0).astype(bf16)


def norm_value(rows, gain):
    inverse = lax.rsqrt(jnp.mean(rows * rows, axis=-1, keepdims=True) + norm_eps)
    return rows * inverse * gain, inverse


def row_of(ref):
    return ref[...].astype(f32).reshape(1, ref.shape[0])


def turning(angles):
    swapped = pltpu.roll(angles, HEAD_DIM // 2, 1)
    first = lax.broadcasted_iota(jnp.int32, angles.shape, 1) < HEAD_DIM // 2
    return jnp.where(first, angles, swapped), jnp.where(first, -swapped, angles)


def greet(count):
    row, me = lax.axis_index("rows"), lax.axis_index("heads")
    barrier = pltpu.get_barrier_semaphore()
    for step in range(1, count):
        pl.semaphore_signal(
            barrier, inc=1, device_id=(row, lax.rem(me + step, count)), device_id_type=MESH
        )
    pl.semaphore_wait(barrier, count - 1)


def attention_forward_kernel(
    count,
    teams,
    length_ref,
    gain_ref,
    lt,
    right,
    mags,
    angles,
    lt_out,
    lt_down,
    right_exit,
    mags_out,
    mags_down,
    gain_second,
    lt_mlp,
    right_mlp,
    mags_mlp,
    x_any,
    w_query,
    w_key,
    w_value,
    w_out,
    w_down_any,
    w_gate_any,
    w_up_any,
    first,
    query_any,
    keys_any,
    values_any,
    att_any,
    summed_any,
    w_full,
    lse,
    inner_ref,
    norms_ref,
    full_ref,
    gathered,
    middle,
    second,
    summed_out,
    inner_out,
    full_out,
    lt_full,
    exit_norms,
    full_down,
    norms_mlp,
    full_mlp,
    norm_table,
    ext,
    weights,
    query,
    keys,
    values,
    att,
    summed,
    wf,
    w_down,
    w_mlp,
    x_own,
    ext_out,
    lt_in,
    squares_in,
    down_in,
    tables,
    load_sem,
    store_sem,
    send_sem,
    recv_sem,
    line_send,
    line_recv,
    team_send,
    team_recv,
    small_send,
    small_recv,
):
    team, me = lax.axis_index("rows"), lax.axis_index("heads")
    total, depth = x_any.shape
    share = total // count
    group = query.shape[1]
    heads = group // HEAD_DIM
    deep = wf.shape[2]
    bits = teams.bit_length() - 1

    def move(source, target, send, recv, peer_team, peer):
        return pltpu.make_async_remote_copy(
            src_ref=source,
            dst_ref=target,
            send_sem=send,
            recv_sem=recv,
            device_id=(peer_team, peer),
            device_id_type=MESH,
        )

    def flip(index, bit):
        weight = 1 << bit
        return index + weight - 2 * weight * lax.rem(index // weight, 2)

    x_load = pltpu.make_async_copy(x_any, ext.at[:total], load_sem.at[0])
    own_load = pltpu.make_async_copy(
        x_any.at[pl.ds(pl.multiple_of(me * share, share), share), :], x_own, load_sem.at[1]
    )
    loads = [
        pltpu.make_async_copy(source, weights.at[index], load_sem.at[2 + index])
        for index, source in enumerate((w_query, w_key, w_value))
    ]
    shard_loads = [
        pltpu.make_async_copy(
            w_out.at[index * deep : (index + 1) * deep, :], wf.at[me, index], load_sem.at[6 + index]
        )
        for index in range(teams)
    ]
    down_load = pltpu.make_async_copy(w_down_any, w_down, load_sem.at[5])
    mlp_loads = [
        pltpu.make_async_copy(source, w_mlp.at[index], load_sem.at[6 + teams + index])
        for index, source in enumerate((w_gate_any, w_up_any))
    ]
    x_load.start()
    for load in loads:
        load.start()
    own_load.start()

    barrier = pltpu.get_barrier_semaphore()
    for step in range(1, count):
        pl.semaphore_signal(
            barrier, inc=1, device_id=(team, lax.rem(me + step, count)), device_id_type=MESH
        )
    for bit in range(bits):
        pl.semaphore_signal(barrier, inc=1, device_id=(flip(team, bit), me), device_id_type=MESH)
    pl.semaphore_wait(barrier, count - 1 + bits)

    def line_copy(step):
        peer = lax.rem(me + step, count)
        return move(
            w_out.at[pl.ds(pl.multiple_of(team * deep, deep), deep), :],
            wf.at[me, team],
            line_send.at[step],
            line_recv.at[step],
            team,
            peer,
        )

    for step in range(1, count):
        line_copy(step).start()

    half = depth // 2
    outer_bits = list(range(1, bits))
    rounds = []
    slot = 0
    for stage in range(bits - 1):
        copies = []
        for side, order in enumerate((outer_bits, outer_bits[::-1])):
            held = [team]
            for bit in order[:stage]:
                held = held + [flip(index, bit) for index in held]
            for index in held:
                for step in range(1, count):
                    copies.append((slot, index, side, step, order[stage]))
                    slot += 1
        rounds.append(copies)
    held = [team]
    for bit in outer_bits:
        held = held + [flip(index, bit) for index in held]
    copies = []
    for index in held:
        for step in range(1, count):
            copies.append((slot, index, None, step, 0))
            slot += 1
    rounds.append(copies)

    def team_copy(entry):
        slot, index, side, step, bit = entry
        block = lax.rem(me + step, count)
        if side is None:
            place = wf.at[block, index]
        else:
            place = wf.at[block, index, :, side * half : (side + 1) * half]
        return move(place, place, team_send.at[slot], team_recv.at[slot], flip(team, bit), me)

    def advance(stage, distance):
        if stage == 0:
            line_copy(distance).wait_recv()
        else:
            for entry in rounds[stage - 1]:
                if entry[3] == count - distance:
                    team_copy(entry).wait_recv()
        if stage < len(rounds):
            for entry in rounds[stage]:
                if entry[3] == count - distance:
                    team_copy(entry).start()

    order = sorted(
        ((stage, distance) for stage in range(len(rounds) + 1) for distance in range(1, count)),
        key=lambda item: (2 * item[0] + 3 * item[1], item[0]),
    )

    def progress(steps):
        for _ in range(steps):
            if order:
                advance(*order.pop(0))

    def small_copy(kind, step):
        ref = (lt_in, squares_in, down_in, tables)[kind]
        return move(
            ref.at[me],
            ref.at[me],
            small_send.at[kind, step],
            small_recv.at[kind, step],
            team,
            lax.rem(me + step, count),
        )

    lt_in[me] = lt_out[...]
    for step in range(1, count):
        small_copy(0, step).start()

    gain = row_of(gain_ref)
    x_load.wait()

    @pl.loop(0, total // 128)
    def _(index):
        rows = pl.ds(pl.multiple_of(index * 128, 128), 128)
        normed, _ = norm_value(ext[rows, :].astype(f32), gain)
        ext[rows, :] = normed.astype(bf16)

    stores = [pltpu.make_async_copy(ext.at[:total], first, store_sem.at[0])]
    stores[0].start()
    for load in shard_loads:
        load.start()
    down_load.start()
    for load in mlp_loads:
        load.start()
    inner = nt(ext[:total, :], lt[...].astype(bf16)).astype(bf16)
    inner_ref[...] = inner
    length = length_ref[0]
    factor = 1.0 / math.sqrt(HEAD_DIM)
    copies = []

    def project(index, start):
        block = slice(index * RANK, (index + 1) * RANK)
        adapters = split_rows(lt[block, :])
        ext[total:, :] = adapters
        gram = nt(adapters, adapters)
        columns = slice(start, start + 256)
        product = nn(ext[...], weights[index, :, columns])
        local_right = right[index, :, columns]
        squares, full = direction(
            square_sums(weights.at[index], columns), product[total:], gram, local_right
        )
        norms = jnp.sqrt(squares)
        norms_ref[index : index + 1, columns] = norms
        full_ref[index, :, columns] = full
        z = product[:total] + nn(inner, padded_right(local_right, index, 3, SCALE))
        summed[index, :, columns] = z.astype(bf16)
        y = z * (mags[index : index + 1, columns] / norms)
        if index == 2:
            values[:, columns] = y.astype(bf16)
        else:
            for head in range(2):
                part = y[:, head * HEAD_DIM : (head + 1) * HEAD_DIM]
                cosines, sines = turning(angles[...])
                turned = part * cosines + pltpu.roll(part, HEAD_DIM // 2, 1) * sines
                place = slice(start + head * HEAD_DIM, start + (head + 1) * HEAD_DIM)
                (query if index == 0 else keys)[:, place] = turned.astype(bf16)

    def attend(head):
        place = slice(head * HEAD_DIM, (head + 1) * HEAD_DIM)
        turned_values = values[:, place].astype(f32).T.astype(bf16)
        for block in range(total // 256):
            reach = (block + 1) * 256
            at = slice(block * 256, reach)
            scores = nt(keys[:reach, place], query[at, place])
            spots = lax.broadcasted_iota(jnp.int32, (reach, 256), 0)
            asking = lax.broadcasted_iota(jnp.int32, (reach, 256), 1) + block * 256
            allowed = (spots <= asking) & (spots < length)
            scores = jnp.where(allowed, scores * factor, mask_fill)
            peak = jnp.max(scores, axis=0, keepdims=True)
            exps = jnp.exp(scores - peak)
            totals = jnp.sum(exps, axis=0, keepdims=True)
            probs = (exps * (1.0 / totals)).astype(bf16)
            mixed = nn(turned_values[:, :reach], probs)
            att[at, place] = mixed.T.astype(bf16)
            lse[head : head + 1, at] = peak + jnp.log(totals)
        for step in range(1, count):
            peer = lax.rem(me + step, count)
            copy = move(
                att.at[pl.ds(pl.multiple_of(peer * share, share), share), place],
                gathered.at[me, :, place],
                send_sem.at[head, step],
                recv_sem.at[head, step],
                team,
                peer,
            )
            copy.start()
            copies.append(copy)

    def exit_stats():
        for load in shard_loads:
            load.wait()
        down_load.wait()
        for index, (pieces, chunk) in enumerate(((lt_out[...], 64), (lt_down[...], 128))):
            adapters = split_rows(pieces)
            gram = nt(adapters, adapters)
            for start in range(0, depth, 512):
                columns = slice(start, start + 512)
                if index == 0:
                    weight = wf[me, :, :, columns].reshape(group, 512)
                    low = weight.astype(f32)
                    sums = jnp.sum(low * low, axis=0, keepdims=True)
                else:
                    weight = w_down[:, columns]
                    sums = square_sums(w_down, columns)
                squares, full = direction(
                    sums, nn(adapters, weight), gram, right_exit[index, :, columns]
                )
                squares_in[me, index : index + 1, columns] = squares
                if index == 1:
                    down_in[me, :, columns] = full.astype(bf16)
        for step in range(1, count):
            small_copy(1, step).start()
        for step in range(1, count):
            small_copy(2, step).start()

    for load in loads:
        load.wait()
    for start in range(0, group, 256):
        for index in range(3):
            project(index, start)
        for head in range(start // HEAD_DIM, start // HEAD_DIM + 2):
            attend(head)
            progress(1)
        if start == 0:
            exit_stats()
            progress(2)
    for source, target in (
        (summed, summed_any),
        (query, query_any),
        (keys, keys_any),
        (values, values_any),
        (att, att_any),
    ):
        stores.append(pltpu.make_async_copy(source, target, store_sem.at[len(stores)]))
        stores[-1].start()
    progress(1)
    gathered[me] = att[pl.ds(pl.multiple_of(me * share, share), share), :]

    units = mags_mlp.shape[1]
    for index in range(2):
        mlp_loads[index].wait()
        adapters = split_rows(lt_mlp[index * RANK : (index + 1) * RANK, :])
        squares, full = direction(
            square_sums(w_mlp.at[index], slice(0, units)),
            nn(adapters, w_mlp[index]),
            nt(adapters, adapters),
            right_mlp[index],
        )
        norms = jnp.sqrt(squares)
        norms_mlp[index : index + 1, :] = norms
        full_mlp[index] = full
        tables[me, index : index + 1, :units] = norms
        tables[me, index + 2 : index + 3, :units] = mags_mlp[index : index + 1, :] - norms
        progress(1)
    for index in range(3):
        norms = norms_ref[index : index + 1, :]
        at = slice(index * group, (index + 1) * group)
        tables[me, 4:5, at] = norms
        tables[me, 5:6, at] = mags[index : index + 1, :] - norms
    for step in range(1, count):
        small_copy(3, step).start()
    for step in range(1, count):
        small_copy(0, step).wait()
    for index in range(count):
        lt_full[:, index * group : (index + 1) * group] = lt_in[index]
    for copy in copies:
        copy.wait()
    for index in range(count):
        ext_out[:share, index * group : (index + 1) * group] = gathered[index]
    adapters = split_rows(lt_full[...])
    ext_out[share:, :] = adapters
    gram = nt(adapters, adapters)
    inner_low = adapters[:RANK]
    inner = nt(ext_out[:share, :], inner_low)
    inner_out[...] = inner
    low = inner.astype(bf16)
    own_load.wait()
    for step in range(1, count):
        small_copy(1, step).wait()
    squares = squares_in[0]
    for index in range(1, count):
        squares = squares + squares_in[index]
    exit_norms[...] = jnp.sqrt(squares)
    progress(len(order))
    store_full = [
        pltpu.make_async_copy(
            wf.at[index // teams, index % teams],
            w_full.at[index * deep : (index + 1) * deep, :],
            store_sem.at[6 + index],
        )
        for index in range(count * teams)
    ]
    for store in store_full:
        store.start()
    for start in range(0, depth, 512):
        columns = slice(start, start + 512)
        weight = wf[:, :, :, columns].reshape(depth, 512)
        local_right = right_exit[0, :, columns]
        product = nn(ext_out[...], weight)
        _, full = direction(0.0, product[share:], gram, local_right)
        full_out[:, columns] = full
        z = product[:share] + nn(low, padded_right(local_right, 0, 1, SCALE))
        summed_out[:, columns] = z.astype(bf16)
        middle[:, columns] = x_own[:, columns].astype(f32) + z * (
            mags_out[:, columns] / exit_norms[0:1, columns]
        )
    normed, _ = norm_value(middle[...], row_of(gain_second))
    second[...] = normed.astype(bf16)
    for step in range(1, count):
        small_copy(2, step).wait()
        small_copy(3, step).wait()
    edge = 0
    for index in range(3):
        for peer in range(count):
            at = slice(index * group, (index + 1) * group)
            norm_table[0:1, edge : edge + group] = tables[peer, 4:5, at]
            norm_table[1:2, edge : edge + group] = tables[peer, 5:6, at]
            edge += group
    for index in range(2):
        for peer in range(count):
            norm_table[0:1, edge : edge + units] = tables[peer, index : index + 1, :units]
            norm_table[1:2, edge : edge + units] = tables[peer, index + 2 : index + 3, :units]
            edge += units
    for index, magnitude in ((0, mags_out), (1, mags_down)):
        norm = exit_norms[index : index + 1, :]
        norm_table[0:1, edge : edge + depth] = norm
        norm_table[1:2, edge : edge + depth] = magnitude[...] - norm
        edge += depth
    full = down_in[0].astype(f32)
    for index in range(1, count):
        full = full + down_in[index].astype(f32)
    full_down[...] = full
    for store in stores + store_full:
        store.wait()
    for step in range(1, count):
        line_copy(step).wait_send()
    for copies in rounds:
        for entry in copies:
            team_copy(entry).wait_send()


def feed_forward_kernel(
    own,
    cot,
    w_gate_any,
    w_up_any,
    w_down_any,
    lt_pair,
    lt_down_pair,
    right,
    mags,
    right_exit,
    mags_down,
    exit_norms,
    norms_ref,
    fulls,
    mags_out,
    gain_ref,
    inner_out,
    lt_out,
    full_out,
    middle_any,
    summed_any,
    gathered_any,
    w_full_any,
    part,
    early,
    early_rows,
    grad_middle,
    mixed,
    early_out,
    early_mags,
    grad_second,
    adapted,
    pieces_out,
    lth,
    lt_down,
    factors,
    w_gate,
    w_up,
    w_down,
    sec,
    cots,
    cot_own,
    parts,
    mine,
    outer,
    inner_sums,
    near,
    load_sem,
    cot_sem,
    part_sem,
    gather_send,
    gather_recv,
    sum_send,
    outer_recv,
    inner_recv,
    near_send,
    near_recv,
    exit_sem,
    own_sem,
    mixed_send,
    mixed_recv,
):
    row, me = lax.axis_index("rows"), lax.axis_index("heads")
    size, depth = own.shape
    half = size // PIECES
    inward = jnp.where(me < 2, 1, -1)
    is_end = (me == 0) | (me == 3)
    in_middle = jnp.logical_not(is_end)
    ahead, behind = me + inward, me - inward

    def move(source, target, send, recv, peer):
        return pltpu.make_async_remote_copy(
            src_ref=source,
            dst_ref=target,
            send_sem=send,
            recv_sem=recv,
            device_id=(row, peer),
            device_id_type=MESH,
        )

    def rows_of(piece):
        start = piece * half
        return pl.ds(start if isinstance(piece, int) else pl.multiple_of(start, half), half)

    def gather_copy(slot, block, piece, peer):
        place = sec.at[block, rows_of(piece), :]
        return move(place, place, gather_send.at[slot, piece], gather_recv.at[block, piece], peer)

    def gather_start(slot, block, peer):
        for piece in range(PIECES):
            gather_copy(slot, block, piece, peer).start()

    def gather_wait(block, pieces, forward=None):
        for piece in pieces:
            gather_copy(0, block, piece, ahead).wait_recv()
            if forward is not None:
                slot, peer = forward
                gather_copy(slot, block, piece, peer).start()

    right_out, right_down = right_exit.at[0], right_exit.at[1]
    norms_out, norms_down = exit_norms.at[0:1], exit_norms.at[1:2]
    greet(4)
    lth[...] = lt_pair[...].astype(bf16)
    lt_down[...] = lt_down_pair[...].astype(bf16)
    loads = [
        pltpu.make_async_copy(source, target, load_sem.at[index])
        for index, (source, target) in enumerate(
            ((w_gate_any, w_gate), (w_up_any, w_up), (w_down_any, w_down))
        )
    ]
    load_own = pltpu.make_async_copy(own, sec.at[me], own_sem)
    load_own.start()
    load_own.wait()
    gather_start(0, me, ahead)

    @pl.when(jnp.logical_not(is_end))
    def _():
        gather_start(1, me, behind)

    for load in loads:
        load.start()

    def block_at(step):
        middle = jnp.where(
            step == 0, me, jnp.where(step == 1, ahead, jnp.where(step == 2, behind, ahead + inward))
        )
        return jnp.where(is_end, jnp.where(step == 3, me, me + inward * (step + 1)), middle)

    def token_rows(step):
        return pl.ds(pl.multiple_of(block_at(step) * size, size), size)

    def cot_load(step):
        slot = lax.rem(step, 2)
        return pltpu.make_async_copy(cot.at[token_rows(step), :], cots.at[slot], cot_sem.at[slot])

    def part_store(step):
        return pltpu.make_async_copy(
            parts.at[block_at(step)], part.at[token_rows(step), :], part_sem.at[step]
        )

    own_rows = pl.ds(pl.multiple_of(me * size, size), size)
    near_store = pltpu.make_async_copy(parts.at[me], part.at[own_rows, :], part_sem.at[0])
    near_copy = move(parts.at[ahead], near, near_send, near_recv, ahead)

    cot_load(0).start()
    weights = (w_gate, w_up)
    group = gathered_any.shape[2]
    factors[...] = mags[...] / norms_ref[...]
    factor_down = mags_down[...] / norms_down[...]
    grad_left, grad_right_down = early.at[: 2 * RANK], early.at[2 * RANK :]
    grad_right = [early_rows.at[index * RANK : (index + 1) * RANK] for index in range(2)]
    grad_left_down = early_rows.at[2 * RANK : 3 * RANK]
    grad_mags = early_rows.at[3 * RANK :]
    early[...] = jnp.zeros_like(early)
    early_rows[...] = jnp.zeros_like(early_rows)
    for load in loads:
        load.wait()

    def outer_copy(slot, piece, block):
        return move(
            mine.at[block, rows_of(piece), :],
            outer.at[slot, rows_of(piece), :],
            sum_send.at[slot, piece],
            outer_recv.at[slot, piece],
            ahead,
        )

    def inner_copy(slot, piece, block, send, peer):
        return move(
            mine.at[block, rows_of(piece), :],
            inner_sums.at[slot, rows_of(piece), :],
            sum_send.at[send, piece],
            inner_recv.at[slot, piece],
            peer,
        )

    def add_into(block, piece, ref):
        at = rows_of(piece)
        mine[block, at, :] = (
            mine[block, at, :].astype(f32) + ref[at, :].astype(f32)
        ).astype(bf16)

    def pass_on(distance, piece):
        block = me + inward * distance
        outer_copy(distance, piece, me).wait_recv()
        add_into(block, piece, outer.at[distance])
        inner_copy(distance - 1, piece, block, distance - 1, ahead).start()

    def hand_out(piece):
        inner_copy(1, piece, me, 2, behind).wait_recv()
        add_into(behind, piece, inner_sums.at[1])
        inner_copy(0, piece, behind, 2, behind).start()

    def work(block, first_row, width, slot, between, after):
        at = pl.ds(first_row, width)
        x = sec[block, at, :]
        inner = nt(x, lth[...])
        inner_low = inner.astype(bf16)
        zs = [
            nn(x, weights[index][...])
            + nn(inner_low, padded_right(right[index], index, 2, SCALE))
            for index in range(2)
        ]
        gate = zs[0] * factors[0:1, :]
        upper = zs[1] * factors[1:2, :]
        sigmoid = 1.0 / (1.0 + jnp.exp(-gate))
        activated = gate * sigmoid
        hidden = (activated * upper).astype(bf16)
        right_low = right_down[...].astype(bf16)
        inner_down = nt(hidden, lt_down[...])

        parts[block, at, :] = (
            nn(hidden, w_down[...]) + SCALE * nn(inner_down.astype(bf16), right_low)
        ).astype(bf16)

        between()
        gz_down = (cots[slot, at, :].astype(f32) * factor_down).astype(bf16)
        gin_down = SCALE * nt(gz_down, right_low)
        grad_hidden = nt(gz_down, w_down[...]) + nn(gin_down.astype(bf16), lt_down[...])
        grad_left_down[...] += nn(gin_down.T.astype(bf16), hidden)
        grad_right_down[...] += SCALE * nn(inner_down.T.astype(bf16), gz_down)
        grads = (
            grad_hidden * upper * sigmoid * (1.0 + gate * (1.0 - sigmoid)),
            grad_hidden * activated,
        )
        gin = jnp.zeros((width, 2 * RANK), f32)
        gzs = []
        for index in range(2):
            grad_mags[index : index + 1, :] += jnp.sum(grads[index] * zs[index], axis=0, keepdims=True)
            gz = (grads[index] * factors[index : index + 1, :]).astype(bf16)
            gin = gin + nt(gz, padded_right(right[index], index, 2, SCALE))
            gzs.append(gz)
        gin_low = gin.astype(bf16)
        mine[block, at, :] = (
            nt(gzs[0], w_gate[...]) + nt(gzs[1], w_up[...]) + nn(gin_low, lth[...])
        ).astype(bf16)

        after()
        grad_left[...] += nn(gin.T.astype(bf16), x)
        inner_turned = inner.T.astype(bf16)
        for index in range(2):
            grad_right[index][...] += (
                SCALE * nn(inner_turned, gzs[index])[index * RANK : (index + 1) * RANK]
            )

    wide = size // 2

    @pl.when(is_end)
    def _():
        @pl.loop(0, 6)
        def _(half_step):
            step, side = half_step // 2, lax.rem(half_step, 2)
            block = block_at(step)
            for piece in range(PIECES // 2):
                gather_copy(0, block, side * (PIECES // 2) + piece, ahead).wait_recv()

            def between():
                @pl.when(side == 0)
                def _():
                    cot_load(step + 1).start()
                    cot_load(step).wait()

                @pl.when(side == 1)
                def _():
                    part_store(step).start()

            def after():
                for piece in range(PIECES // 2):
                    outer_copy(step, side * (PIECES // 2) + piece, block).start()

            work(block, pl.multiple_of(side * wide, wide), wide, lax.rem(step, 2), between, after)

        near_copy.start()

    @pl.loop(0, 4)
    def _(step):
        @pl.when(in_middle | (step == 3))
        def _():
            block = block_at(step)

            @pl.when(in_middle & (step == 2))
            def _():
                gather_wait(ahead + inward, range(PIECES), (4, behind))

            @pl.when(in_middle & (step == 3))
            def _():
                pass_on(1, 1)

            def between():
                @pl.when(in_middle & (step < 3))
                def _():
                    cot_load(step + 1).start()

                cot_load(step).wait()

                @pl.when(is_end | (step > 0))
                def _():
                    part_store(step).start()

                @pl.when(in_middle & (step == 0))
                def _():
                    for piece in range(PIECES):
                        gather_wait(behind, (piece,), (2, ahead))
                        gather_wait(ahead, (piece,), (3, behind))

                @pl.when(in_middle & (step == 2))
                def _():
                    pass_on(1, 0)

                @pl.when(in_middle & (step == 3))
                def _():
                    pass_on(1, 2)
                    pass_on(1, 3)

            work(block, 0, size, lax.rem(step, 2), between, lambda: None)

    @pl.when(in_middle)
    def _():
        pass_on(2, 0)
        pass_on(2, 1)

    for index in range(2):
        block = slice(index * RANK, (index + 1) * RANK)
        norms = norms_ref[index : index + 1, :]
        factor_grad = grad_mags[index : index + 1, :]
        shape = -factor_grad * mags[index : index + 1, :] / (norms * norms * norms)
        shaped = right[index] * shape
        pieces = nt(split_rows(shaped), weights[index][...])
        lt = lt_pair[block, :]
        grad_left[block, :] += SCALE * (
            pieces[:RANK]
            + pieces[RANK:]
            + SCALE * nn_exact(nt_exact(shaped, right[index]), lt)
        )
        grad_right[index][...] += SCALE * fulls[index] * shape
        grad_mags[index : index + 1, :] = factor_grad / norms

    @pl.when(is_end)
    def _():
        part_store(0).wait()
        for piece in range(PIECES):
            gather_copy(0, me, piece, ahead).wait_send()

    @pl.when(in_middle)
    def _():
        for piece in range(PIECES):
            for slot in range(5):
                gather_copy(slot, me, piece, ahead).wait_send()

    for step in range(1, 4):
        part_store(step).wait()
    behind_part = jnp.where(is_end, me, ahead + inward)
    width = depth // 2
    exits = [
        (middle_any, grad_middle),
        (summed_any, parts.at[behind_part]),
        (cot.at[own_rows, :], cot_own),
        (w_full_any.at[:, :width], w_gate.at[:, :width]),
        (w_full_any.at[:, width:], w_up.at[:, :width]),
    ] + [
        (gathered_any.at[index], sec.at[index, :, group : 2 * group]) for index in range(4)
    ]
    exit_loads = [
        pltpu.make_async_copy(source, target, exit_sem.at[index])
        for index, (source, target) in enumerate(exits)
    ]
    for load in exit_loads:
        load.start()

    @pl.when(in_middle)
    def _():
        hand_out(0)
        pass_on(2, 2)
        hand_out(1)
        pass_on(2, 3)
        hand_out(2)
        hand_out(3)

    @pl.when(is_end)
    def _():
        for slot in range(3):
            for piece in range(PIECES):
                outer_copy(slot, piece, me).wait_send()

    for load in exit_loads:
        load.wait()
    gain = row_of(gain_ref)
    norm = norms_out[...]
    scale_out = mags_out[...] / norm
    factor_grad = jnp.zeros((1, depth), f32)
    for piece in range(PIECES):
        at = rows_of(piece)

        @pl.when(in_middle)
        def _():
            outer_copy(0, piece, me).wait_recv()
            grad_second[at, :] = outer[0, at, :].astype(f32)

        @pl.when(is_end)
        def _():
            grad_second[at, :] = jnp.zeros((half, depth), f32)

        inner_copy(0, piece, me, 0, ahead).wait_recv()
        total = (
            grad_second[at, :] + mine[me, at, :].astype(f32) + inner_sums[0, at, :].astype(f32)
        )
        rows = grad_middle[at, :]
        inverse = lax.rsqrt(jnp.mean(rows * rows, axis=-1, keepdims=True) + norm_eps)
        scaled = total * gain
        grad = (
            cot_own[at, :].astype(f32)
            + inverse * scaled
            - rows * (inverse * inverse * inverse) * jnp.mean(rows * scaled, axis=-1, keepdims=True)
        )
        grad_middle[at, :] = grad
        factor_grad = factor_grad + jnp.sum(
            grad * parts[behind_part, at, :].astype(f32), axis=0, keepdims=True
        )
        adapted[at, :] = (grad * scale_out).astype(bf16)
    shape = -factor_grad * mags_out[...] / (norm * norm * norm)
    shaped = right_out[...] * shape
    adapted[size:, :] = split_rows(shaped)
    gz = adapted[:size, :]
    gin = SCALE * nt(gz, right_out[...].astype(bf16))
    gin_low = gin.astype(bf16)
    def mixed_copy(step):
        peer = lax.rem(me + step, 4)
        return move(
            sec.at[peer, :, :group], mixed.at[me], mixed_send.at[step], mixed_recv.at[step], peer
        )

    for step in (2, 1, 3, 4):
        peer = lax.rem(me + step, 4)
        columns = pl.ds(pl.multiple_of(peer * group, group), group)
        moved = nt(adapted[:, :width], w_gate[columns, :width]) + nt(
            adapted[:, width:], w_up[columns, :width]
        )
        result = (moved[:size] + nn(gin_low, lt_out[:, columns].astype(bf16))).astype(bf16)
        if step == 4:
            mixed[me] = result
        else:
            sec[peer, :, :group] = result
            mixed_copy(step).start()
        pieces_out[:, columns] = moved[size:]

    gin_turned = gin.T.astype(bf16)
    mixing = nt_exact(shaped, right_out[...])
    early_mags[...] = factor_grad / norm
    early_out[:RANK, :] = SCALE * (nn(inner_out[...].T.astype(bf16), gz) + full_out[...] * shape)
    early_out[RANK:, :] = SCALE * (
        pieces_out[:RANK, :] + pieces_out[RANK:, :] + SCALE * nn_exact(mixing, lt_out[...])
    )
    for index in range(4):
        at = slice(index * group, (index + 1) * group)
        early_out[RANK:, at] += nn(gin_turned, sec[index, :, group : 2 * group])

    @pl.when(in_middle)
    def _():
        near_copy.wait_recv()
        parts[me] = (parts[me].astype(f32) + near[...].astype(f32)).astype(bf16)
        near_store.start()
        for piece in range(PIECES):
            for send in range(3):
                inner_copy(0, piece, me, send, ahead).wait_send()
        near_store.wait()

    @pl.when(is_end)
    def _():
        near_copy.wait_send()

    for step in range(1, 4):
        mixed_copy(step).wait()


def attention_back_kernel(
    teams,
    length_ref,
    query_any,
    keys_any,
    values_any,
    att_any,
    lse,
    mixed_any,
    summed_any,
    norms_ref,
    mags,
    fulls,
    inner,
    lt_triple,
    right,
    angles,
    gain_ref,
    early,
    early_out,
    early_rows,
    early_mags,
    exit_norms,
    mags_down,
    right_exit,
    full_down,
    lt_down,
    first_any,
    part,
    weights_any_query,
    weights_any_key,
    weights_any_value,
    w_down,
    x_own,
    grad_middle,
    middle,
    cot_own,
    outputs,
    input_grad,
    grad_qkv_left,
    grad_qkv_right,
    grad_qkv_mags,
    grad_mlp_left,
    grad_mlp_right,
    grad_mlp_mags,
    grad_out_left,
    grad_down_left,
    grad_exit_right,
    grad_out_mags,
    grad_down_mags,
    query,
    keys,
    values,
    att,
    mixed,
    summed,
    act_sem,
    lth,
    gz,
    key_sums,
    value_sums,
    query_turned,
    factors,
    weights,
    mine,
    outer,
    inner_sums,
    outer_down,
    inner_down,
    block_part,
    wide,
    wide_in,
    line_in,
    whole,
    group_in,
    unit_in,
    small,
    small_line,
    small_rows,
    load_sem,
    part_sem,
    sum_send,
    outer_recv,
    inner_recv,
    down_send,
    down_outer_recv,
    down_inner_recv,
    wide_send,
    wide_recv,
    line_send,
    line_recv,
    whole_send,
    whole_recv,
    group_send,
    group_recv,
    unit_send,
    unit_recv,
    small_send,
    small_recv,
    final_send,
    final_recv,
):
    right_down, norms_down = right_exit.at[1], exit_norms.at[1:2]
    total = query.shape[0]
    depth = mine.shape[1]
    size = total // 4
    half = size // PIECES
    team, me = lax.axis_index("rows"), lax.axis_index("heads")
    inward = jnp.where(me < 2, 1, -1)
    is_end = (me == 0) | (me == 3)
    in_middle = jnp.logical_not(is_end)
    ahead, behind = me + inward, me - inward

    def move(source, target, send, recv, peer, peer_team=team):
        return pltpu.make_async_remote_copy(
            src_ref=source,
            dst_ref=target,
            send_sem=send,
            recv_sem=recv,
            device_id=(peer_team, peer),
            device_id_type=MESH,
        )

    def rows_of(block, piece=None):
        if piece is None:
            return pl.ds(pl.multiple_of(block * size, size), size)
        return pl.ds(pl.multiple_of(block * size + piece * half, half), half)

    def piece_of(piece):
        return pl.ds(piece * half, half)

    barrier = pltpu.get_barrier_semaphore()
    for step in range(1, 4):
        pl.semaphore_signal(
            barrier, inc=1, device_id=(team, lax.rem(me + step, 4)), device_id_type=MESH
        )
    for step in range(1, teams):
        pl.semaphore_signal(
            barrier, inc=1, device_id=(lax.rem(team + step, teams), me), device_id_type=MESH
        )
    pl.semaphore_wait(barrier, teams + 2)

    def down_outer(slot, piece, block):
        return move(
            part.at[rows_of(block, piece), :],
            outer_down.at[slot, piece_of(piece), :],
            down_send.at[slot, piece],
            down_outer_recv.at[slot, piece],
            ahead,
        )

    def down_inner(slot, piece, send, peer):
        return move(
            block_part.at[send, piece_of(piece), :],
            inner_down.at[slot, piece_of(piece), :],
            down_send.at[send, piece],
            down_inner_recv.at[slot, piece],
            peer,
        )

    @pl.when(is_end)
    def _():
        for piece in range(PIECES):
            down_outer(1, piece, me + inward * 3).start()
        for piece in range(PIECES):
            down_outer(0, piece, me + inward * 2).start()

    def part_load(slot, block):
        return pltpu.make_async_copy(part.at[rows_of(block), :], block_part.at[slot], part_sem.at[slot])

    @pl.when(in_middle)
    def _():
        part_load(0, ahead).start()
        part_load(1, ahead + inward).start()
        part_load(3, behind).start()

    part_load(2, me).start()

    def unit_copy(step):
        return move(
            unit_in.at[team],
            unit_in.at[team],
            unit_send.at[step],
            unit_recv.at[step],
            me,
            lax.rem(team + step, teams),
        )

    def group_copy(step):
        return move(
            group_in.at[team],
            group_in.at[team],
            group_send.at[step],
            group_recv.at[step],
            me,
            lax.rem(team + step, teams),
        )

    act_loads = [
        pltpu.make_async_copy(source, target, act_sem.at[index])
        for index, (source, target) in enumerate(
            (
                (query_any, query),
                (keys_any, keys),
                (values_any, values),
                (att_any, att),
                (mixed_any, mixed),
                (summed_any, summed),
            )
        )
    ]
    for load in act_loads:
        load.start()
    unit_in[team] = early_rows[...].astype(bf16)
    for step in range(1, teams):
        unit_copy(step).start()

    loads = [
        pltpu.make_async_copy(source, weights.at[index], load_sem.at[index])
        for index, source in enumerate((weights_any_query, weights_any_key, weights_any_value))
    ]
    load_first = pltpu.make_async_copy(first_any, mine, load_sem.at[3])
    for load in loads:
        load.start()
    load_first.start()

    for load in act_loads:
        load.wait()
    lth[...] = lt_triple[...].astype(bf16)
    heads = query.shape[1] // HEAD_DIM
    length = length_ref[0]
    factor = 1.0 / math.sqrt(HEAD_DIM)
    factors[:3, :] = mags[...] / norms_ref[...]

    def finish(index, head, grad):
        place = slice(head * HEAD_DIM, (head + 1) * HEAD_DIM)
        if index < 2:
            cosines, sines = turning(angles[...])
            grad = grad * cosines - pltpu.roll(grad, HEAD_DIM // 2, 1) * sines
        factors[index + 3 : index + 4, place] = jnp.sum(
            grad * summed[index, :, place].astype(f32), axis=0, keepdims=True
        )
        gz[index, :, place] = (grad * factors[index : index + 1, place]).astype(bf16)

    for head in range(heads):
        place = slice(head * HEAD_DIM, (head + 1) * HEAD_DIM)
        turned_keys = keys[:, place].astype(f32).T.astype(bf16)
        key_sums[...] = jnp.zeros_like(key_sums)
        value_sums[...] = jnp.zeros_like(value_sums)
        for block in range(total // 256):
            reach = (block + 1) * 256
            at = slice(block * 256, reach)
            grad_rows = mixed[at, place]
            rows = query[at, place]
            scores = nt(keys[:reach, place], rows)
            spots = lax.broadcasted_iota(jnp.int32, (reach, 256), 0)
            asking = lax.broadcasted_iota(jnp.int32, (reach, 256), 1) + block * 256
            allowed = (spots <= asking) & (spots < length)
            scores = jnp.where(allowed, scores * factor, mask_fill)
            probs = jnp.exp(scores - lse[head : head + 1, at])
            grad_probs = nt(values[:reach, place], grad_rows)
            centre = jnp.sum(
                (grad_rows.astype(f32) * att[at, place].astype(f32)).T, axis=0, keepdims=True
            )
            raw = (probs * (grad_probs - centre) * factor).astype(bf16)
            value_sums[:reach, :] += nn(probs.astype(bf16), grad_rows)
            key_sums[:reach, :] += nn(raw, rows)
            query_turned[:, at] = nn(turned_keys[:, :reach], raw)
        finish(0, head, query_turned[...].T)
        finish(1, head, key_sums[...])
        finish(2, head, value_sums[...])

    gin = jnp.zeros((total, 3 * RANK), f32)
    for index in range(3):
        gin = gin + nt(gz[index], padded_right(right[index], index, 3, SCALE))
    gin_low = gin.astype(bf16)
    load_first.wait()
    left = nn(gin.T.astype(bf16), mine[...])
    inner_turned = inner[...].astype(f32).T.astype(bf16)
    for index in range(3):
        block = slice(index * RANK, (index + 1) * RANK)
        norms = norms_ref[index : index + 1, :]
        factor_grad = factors[index + 3 : index + 4, :]
        shape = -factor_grad * mags[index : index + 1, :] / (norms * norms * norms)
        shaped = right[index] * shape
        loads[index].wait()
        pieces = nt(split_rows(shaped), weights[index])
        lt = lt_triple[block, :]
        extra = pieces[:RANK] + pieces[RANK:] + SCALE * nn_exact(nt_exact(shaped, right[index]), lt)
        wide[block, :] = (left[block, :] + SCALE * extra).astype(bf16)
        group_in[team, block, :] = (
            SCALE * (nn(inner_turned, gz[index])[block] + fulls[index] * shape)
        ).astype(bf16)
    tail = group_in.shape[1] - 3 * RANK
    group_in[team, 3 * RANK :, :] = jnp.concatenate(
        [factors[3:6, :] / norms_ref[...], jnp.zeros((tail - 3, factors.shape[1]), f32)], axis=0
    ).astype(bf16)
    wide[3 * RANK : 6 * RANK, :] = early[...].astype(bf16)
    wide[6 * RANK :, :] = early_out[...].astype(bf16)
    for step in range(1, teams):
        group_copy(step).start()

    tiles = wide.shape[0] // 16
    parts_of_tile = teams // tiles
    stretch = depth // parts_of_tile

    def tile_of(owner):
        return (
            pl.ds(pl.multiple_of(lax.rem(owner, tiles) * 16, 16), 16),
            pl.ds(pl.multiple_of((owner // tiles) * stretch, stretch), stretch),
        )

    def wide_copy(step):
        owner = lax.rem(team + step, teams)
        across, along = tile_of(owner)
        return move(
            wide.at[across, along],
            wide_in.at[team],
            wide_send.at[step],
            wide_recv.at[step],
            me,
            owner,
        )

    for step in range(1, teams):
        wide_copy(step).start()
    across, along = tile_of(team)
    wide_in[team] = wide[across, along]

    def add_down(send, piece, ref):
        at = piece_of(piece)
        block_part[send, at, :] = (
            block_part[send, at, :].astype(f32) + ref[at, :].astype(f32)
        ).astype(bf16)

    @pl.when(in_middle)
    def _():
        part_load(1, me).wait()
        for piece in range(PIECES):
            down_outer(1, piece, me).wait_recv()
            add_down(1, piece, outer_down.at[1])
            down_inner(1, piece, 1, ahead).start()

    def grad_block(block):
        at = rows_of(block)
        mine[at, :] = (
            nt(gz[0, at, :], weights[0])
            + nt(gz[1, at, :], weights[1])
            + nt(gz[2, at, :], weights[2])
            + nn(
                (
                    SCALE
                    * (
                        nt(gz[0, at, :], padded_right(right[0], 0, 3, 1.0))
                        + nt(gz[1, at, :], padded_right(right[1], 1, 3, 1.0))
                        + nt(gz[2, at, :], padded_right(right[2], 2, 3, 1.0))
                    )
                ).astype(bf16),
                lth[...],
            )
        ).astype(bf16)

    def outer_copy(slot, piece, block):
        return move(
            mine.at[rows_of(block, piece), :],
            outer.at[slot, piece_of(piece), :],
            sum_send.at[slot, piece],
            outer_recv.at[slot, piece],
            ahead,
        )

    def inner_copy(slot, piece, block, send, peer):
        return move(
            mine.at[rows_of(block, piece), :],
            inner_sums.at[slot, piece_of(piece), :],
            sum_send.at[send, piece],
            inner_recv.at[slot, piece],
            peer,
        )

    @pl.loop(0, 4)
    def _(step):
        middle_block = jnp.where(
            step == 0, ahead + inward, jnp.where(step == 1, ahead, jnp.where(step == 2, behind, me))
        )
        grad_block(jnp.where(is_end, me + inward * (3 - step), middle_block))

        @pl.when(is_end & (step == 0))
        def _():
            for piece in range(PIECES):
                outer_copy(2, piece, me + inward * 3).start()

    def add_into(block, piece, ref):
        at = rows_of(block, piece)
        mine[at, :] = (
            mine[at, :].astype(f32) + ref[piece_of(piece), :].astype(f32)
        ).astype(bf16)

    for step in range(1, teams):
        wide_copy(step).wait_recv()
    gathered = jnp.zeros((16, stretch), f32)
    for index in range(teams):
        gathered = gathered + wide_in[index].astype(f32)
    line_in[me] = gathered.astype(bf16)

    def line_copy(step):
        return move(
            line_in.at[me],
            line_in.at[me],
            line_send.at[step],
            line_recv.at[step],
            lax.rem(me + step, 4),
        )

    for step in range(1, 4):
        line_copy(step).start()

    @pl.when(is_end)
    def _():
        for piece in range(PIECES):
            outer_copy(1, piece, ahead + inward).start()

    @pl.when(in_middle)
    def _():
        part_load(0, me).wait()
        part_load(3, me).wait()
        for piece in range(PIECES):
            down_outer(0, piece, me).wait_recv()
            add_down(0, piece, outer_down.at[0])
            down_inner(0, piece, 0, ahead).start()
        for piece in range(PIECES):
            down_inner(1, piece, 0, ahead).wait_recv()
            add_down(3, piece, inner_down.at[1])
            down_inner(0, piece, 3, behind).start()
        for piece in range(PIECES):
            outer_copy(2, piece, me).wait_recv()
            add_into(ahead + inward, piece, outer.at[2])
            inner_copy(1, piece, ahead + inward, 1, ahead).start()

    part_load(2, me).wait()

    for piece in range(PIECES):
        down_inner(0, piece, 0, ahead).wait_recv()

    load_own = [
        pltpu.make_async_copy(source, target, load_sem.at[index])
        for index, (source, target) in enumerate(
            ((middle, input_grad), (cot_own.at[rows_of(me), :], outputs))
        )
    ]
    for load in load_own:
        load.start()
    norm_down = norms_down[...]
    done = block_part[2].astype(f32) + inner_down[0].astype(f32)
    for load in load_own:
        load.wait()
    small[0:1, :] = jnp.sum(outputs[...].astype(f32) * done, axis=0, keepdims=True)
    small[1:2, :] = early_mags[...]
    outputs[...] = (input_grad[...] + done * (mags_down[...] / norm_down)).astype(bf16)
    small_line[me] = small[...]

    def small_copy(step):
        return move(
            small_line.at[me],
            small_line.at[me],
            small_send.at[step],
            small_recv.at[step],
            lax.rem(me + step, 4),
        )

    for step in range(1, 4):
        small_copy(step).start()

    @pl.when(is_end)
    def _():
        for piece in range(PIECES):
            outer_copy(0, piece, ahead).start()

    load_wide = [
        pltpu.make_async_copy(
            w_down.at[:, index * 512 : (index + 1) * 512],
            weights.at[index, : w_down.shape[0], :],
            load_sem.at[index],
        )
        for index in range(3)
    ]
    load_wide.append(
        pltpu.make_async_copy(w_down.at[:1024, 1536:], gz.at[0], load_sem.at[3])
    )
    load_wide.append(
        pltpu.make_async_copy(
            w_down.at[1024:, 1536:], gz.at[1, : w_down.shape[0] - 1024, :], load_sem.at[4]
        )
    )
    for load in load_wide:
        load.start()

    for step in range(1, 4):
        line_copy(step).wait_recv()
    whole[team] = (
        line_in[0].astype(f32)
        + line_in[1].astype(f32)
        + line_in[2].astype(f32)
        + line_in[3].astype(f32)
    ).astype(bf16)

    def whole_copy(step):
        return move(
            whole.at[team],
            whole.at[team],
            whole_send.at[step],
            whole_recv.at[step],
            me,
            lax.rem(team + step, teams),
        )

    for step in range(1, teams):
        whole_copy(step).start()
    for step in range(1, 4):
        small_copy(step).wait_recv()
    small_rows[team] = small_line[0] + small_line[1] + small_line[2] + small_line[3]

    def final_copy(step):
        return move(
            small_rows.at[team],
            small_rows.at[team],
            final_send.at[step],
            final_recv.at[step],
            me,
            lax.rem(team + step, teams),
        )

    for step in range(1, teams):
        final_copy(step).start()

    @pl.when(in_middle)
    def _():
        for piece in range(PIECES):
            inner_copy(1, piece, me, 0, ahead).wait_recv()
            add_into(behind, piece, inner_sums.at[1])
            inner_copy(0, piece, behind, 2, behind).start()
            outer_copy(1, piece, me).wait_recv()
            add_into(ahead, piece, outer.at[1])
            inner_copy(0, piece, ahead, 0, ahead).start()

    for step in range(1, teams):
        final_copy(step).wait_recv()
    sums = jnp.zeros((2, depth), f32)
    for index in range(teams):
        sums = sums + small_rows[index]
    grad_down_mags[...] = sums[0:1] / norm_down
    grad_out_mags[...] = sums[1:2]
    shape = -sums[0:1] * mags_down[...] / (norm_down * norm_down * norm_down)
    shaped = right_down[...] * shape
    right_extra = SCALE * full_down[...] * shape
    for load in load_wide:
        load.wait()
    cut = split_rows(shaped)
    units = w_down.shape[0]
    pieces = (
        nt(cut[:, :512], weights[0, :units, :])
        + nt(cut[:, 512:1024], weights[1, :units, :])
        + nt(cut[:, 1024:1536], weights[2, :units, :])
    )
    last = cut[:, 1536:]
    mixing = nt_exact(shaped, right_down[...])
    lt = lt_down[...]
    extra = pieces[:RANK] + pieces[RANK:] + SCALE * nn_exact(mixing, lt)
    ends = [nt(last, gz[0]), nt(last, gz[1, : units - 1024, :])]
    grad_down_left[:, :1024] = SCALE * (extra[:, :1024] + ends[0][:RANK] + ends[0][RANK:])
    grad_down_left[:, 1024:] = SCALE * (extra[:, 1024:] + ends[1][:RANK] + ends[1][RANK:])

    for step in range(1, teams):
        group_copy(step).wait_recv()
        unit_copy(step).wait_recv()
        whole_copy(step).wait_recv()
    group_total = jnp.zeros(group_in.shape[1:], f32)
    unit_total = jnp.zeros(unit_in.shape[1:], f32)
    for index in range(teams):
        group_total = group_total + group_in[index].astype(f32)
        unit_total = unit_total + unit_in[index].astype(f32)
    for index in range(3):
        grad_qkv_right[index] = group_total[index * RANK : (index + 1) * RANK]
    grad_qkv_mags[...] = group_total[3 * RANK : 3 * RANK + 3]
    for index in range(2):
        grad_mlp_right[index] = unit_total[index * RANK : (index + 1) * RANK]
    grad_down_left[...] += unit_total[2 * RANK : 3 * RANK]
    grad_mlp_mags[...] = unit_total[3 * RANK : 3 * RANK + 2]
    for part_index in range(parts_of_tile):
        along = slice(part_index * stretch, (part_index + 1) * stretch)
        tile = [whole[part_index * tiles + index].astype(f32) for index in range(7)]
        for index in range(3):
            grad_qkv_left[index, :, along] = tile[index]
        for index in range(2):
            grad_mlp_left[index, :, along] = tile[3 + index]
        grad_exit_right[1, :, along] = tile[5] + right_extra[:, along]
        grad_exit_right[0, :, along] = tile[6]
    group = query.shape[1]
    within = min(group, stretch)
    for index in range(group // within):
        spot = me * group + index * within
        grad_out_left[:, index * within : (index + 1) * within] = whole[
            (spot // stretch) * tiles + 7,
            :,
            pl.ds(pl.multiple_of(lax.rem(spot, stretch), within), within),
        ].astype(f32)

    load_end = [
        pltpu.make_async_copy(source, target, load_sem.at[index])
        for index, (source, target) in enumerate(
            ((grad_middle, input_grad), (x_own.at[rows_of(me), :], block_part.at[2]))
        )
    ]
    for load in load_end:
        load.start()
    for load in load_end:
        load.wait()
    gain = row_of(gain_ref)

    for piece in range(PIECES):
        at = rows_of(me, piece)
        spot = piece_of(piece)

        @pl.when(in_middle)
        def _():
            outer_copy(0, piece, me).wait_recv()
            add_into(me, piece, outer.at[0])

        inner_copy(0, piece, me, 0, ahead).wait_recv()
        grad = mine[at, :].astype(f32) + inner_sums[0, spot, :].astype(f32)
        rows = block_part[2, spot, :].astype(f32)
        inverse = lax.rsqrt(jnp.mean(rows * rows, axis=-1, keepdims=True) + norm_eps)
        scaled = grad * gain
        input_grad[spot, :] = (
            input_grad[spot, :]
            + inverse * scaled
            - rows
            * (inverse * inverse * inverse)
            * jnp.mean(rows * scaled, axis=-1, keepdims=True)
        )

    @pl.when(in_middle)
    def _():
        for piece in range(PIECES):
            for send in (0, 1, 3):
                down_inner(0, piece, send, ahead).wait_send()
            for send in range(3):
                inner_copy(0, piece, me, send, ahead).wait_send()

    @pl.when(is_end)
    def _():
        for piece in range(PIECES):
            for slot in range(2):
                down_outer(slot, piece, me).wait_send()
            for slot in range(3):
                outer_copy(slot, piece, me).wait_send()

    for step in range(1, 4):
        line_copy(step).wait_send()
        small_copy(step).wait_send()
    for step in range(1, teams):
        unit_copy(step).wait_send()
        group_copy(step).wait_send()
        wide_copy(step).wait_send()
        whole_copy(step).wait_send()
        final_copy(step).wait_send()


def call(kernel, outs, ins, specs=None, out_specs=None, scratch=(), flops=0, moved=0, collective=None):
    extra = {} if collective is None else {"collective_id": collective, "has_side_effects": True}
    return pl.pallas_call(
        kernel,
        out_shape=[jax.ShapeDtypeStruct(shape, kind) for shape, kind in outs],
        in_specs=specs or [VMEM] * len(ins),
        out_specs=out_specs or [VMEM] * len(outs),
        scratch_shapes=list(scratch),
        cost_estimate=pl.CostEstimate(flops=flops, bytes_accessed=moved, transcendentals=0),
        compiler_params=pltpu.CompilerParams(vmem_limit_bytes=LIMIT, **extra),
    )(*ins)


def rope_table(length, width):
    half = width // 2
    freqs = np.float32(rope_base) ** (-(np.arange(half, dtype=np.float32) * 2.0) / width)
    angles = np.arange(length, dtype=np.float32)[:, None] * freqs[None, :].astype(np.float32)
    return np.concatenate([np.cos(angles), np.sin(angles)], axis=1).astype(np.float32)


def local(
    inputs,
    cotangent,
    lengths,
    gain_attn,
    gain_mlp,
    w_query,
    w_key,
    w_value,
    w_out,
    w_gate,
    w_up,
    w_down,
    qkv_left,
    qkv_right,
    qkv_mags,
    mlp_left,
    mlp_right,
    mlp_mags,
    out_left,
    down_left,
    exit_right,
    out_mags,
    down_mags,
):
    count = lax.axis_size("heads")
    teams = lax.axis_size("rows")
    total, depth = inputs.shape
    share = total // count
    group = w_query.shape[1]
    units = w_gate.shape[1]
    heads = group // HEAD_DIM
    deep = group // teams
    lt_qkv = jnp.transpose(qkv_left, (0, 2, 1)).reshape(3 * RANK, depth)
    lt_mlp = jnp.transpose(mlp_left, (0, 2, 1)).reshape(2 * RANK, depth)
    angles = jnp.asarray(rope_table(total, HEAD_DIM))
    out_mag, down_mag = out_mags.reshape(1, depth), down_mags.reshape(1, depth)
    bits = teams.bit_length() - 1
    assert teams == 1 << bits
    slots = 3 * (2 * (2 ** (bits - 1) - 1) + 2 ** (bits - 1))

    (
        first,
        query,
        keys,
        values,
        att,
        qkv_summed,
        w_full,
        lse,
        qkv_inner,
        qkv_norms,
        qkv_full,
        gathered,
        middle,
        second,
        out_summed,
        out_inner,
        full_out,
        lt_out,
        exit_norms,
        full_down,
        mlp_norms,
        mlp_full,
        norm_stats,
    ) = call(
        functools.partial(attention_forward_kernel, count, teams),
        [
            ((total, depth), bf16),
            ((total, group), bf16),
            ((total, group), bf16),
            ((total, group), bf16),
            ((total, group), bf16),
            ((3, total, group), bf16),
            ((depth, depth), bf16),
            ((heads, total), f32),
            ((total, 3 * RANK), bf16),
            ((3, group), f32),
            ((3, RANK, group), f32),
            ((count, share, group), bf16),
            ((share, depth), f32),
            ((share, depth), bf16),
            ((share, depth), bf16),
            ((share, RANK), f32),
            ((RANK, depth), f32),
            ((RANK, depth), f32),
            ((2, depth), f32),
            ((RANK, depth), f32),
            ((2, units), f32),
            ((2, RANK, units), f32),
            ((2, 3 * count * group + 2 * count * units + 2 * depth), f32),
        ],
        (
            lengths,
            gain_attn,
            lt_qkv,
            qkv_right,
            qkv_mags,
            angles,
            out_left.T,
            down_left.T,
            exit_right,
            out_mag,
            down_mag,
            gain_mlp,
            lt_mlp,
            mlp_right,
            mlp_mags,
            inputs,
            w_query,
            w_key,
            w_value,
            w_out,
            w_down,
            w_gate,
            w_up,
        ),
        specs=[SMEM] + [VMEM] * 14 + [ANY] * 8,
        out_specs=[ANY] * 7 + [VMEM] * 16,
        scratch=(
            pltpu.VMEM((total + 2 * RANK, depth), bf16),
            pltpu.VMEM((3, depth, group), bf16),
            pltpu.VMEM((total, group), bf16),
            pltpu.VMEM((total, group), bf16),
            pltpu.VMEM((total, group), bf16),
            pltpu.VMEM((total, group), bf16),
            pltpu.VMEM((3, total, group), bf16),
            pltpu.VMEM((count, teams, deep, depth), bf16),
            pltpu.VMEM((units, depth), bf16),
            pltpu.VMEM((2, depth, units), bf16),
            pltpu.VMEM((share, depth), bf16),
            pltpu.VMEM((share + 2 * RANK, depth), bf16),
            pltpu.VMEM((count, RANK, group), f32),
            pltpu.VMEM((count, 2, depth), f32),
            pltpu.VMEM((count, RANK, depth), bf16),
            pltpu.VMEM((count, 8, depth), f32),
            pltpu.SemaphoreType.DMA((8 + teams,)),
            pltpu.SemaphoreType.DMA((6 + count * teams,)),
            pltpu.SemaphoreType.DMA((heads, count)),
            pltpu.SemaphoreType.DMA((heads, count)),
            pltpu.SemaphoreType.DMA((count,)),
            pltpu.SemaphoreType.DMA((count,)),
            pltpu.SemaphoreType.DMA((slots,)),
            pltpu.SemaphoreType.DMA((slots,)),
            pltpu.SemaphoreType.DMA((4, count)),
            pltpu.SemaphoreType.DMA((4, count)),
        ),
        flops=6 * total * depth * group + 4 * total * total * group,
        moved=2 * (2 * total * depth + 3 * depth * group + 8 * total * group),
        collective=0,
    )
    assert count == 4
    (
        part,
        early,
        early_rows,
        grad_middle,
        mixed,
        early_out,
        early_mags,
    ) = call(
        feed_forward_kernel,
        [
            ((total, depth), bf16),
            ((3 * RANK, depth), f32),
            ((4 * RANK, units), f32),
            ((share, depth), f32),
            ((count, share, group), bf16),
            ((2 * RANK, depth), f32),
            ((1, depth), f32),
        ],
        (
            second,
            cotangent,
            w_gate,
            w_up,
            w_down,
            lt_mlp,
            down_left.T,
            mlp_right,
            mlp_mags,
            exit_right,
            down_mag,
            exit_norms,
            mlp_norms,
            mlp_full,
            out_mag,
            gain_mlp,
            out_inner,
            lt_out,
            full_out,
            middle,
            out_summed,
            gathered,
            w_full,
        ),
        specs=[ANY] * 5 + [VMEM] * 14 + [ANY] * 4,
        out_specs=[ANY] + [VMEM] * 6,
        scratch=(
            pltpu.VMEM((share, depth), f32),
            pltpu.VMEM((share + 2 * RANK, depth), bf16),
            pltpu.VMEM((2 * RANK, depth), f32),
            pltpu.VMEM((2 * RANK, depth), bf16),
            pltpu.VMEM((RANK, units), bf16),
            pltpu.VMEM((2, units), f32),
            pltpu.VMEM((depth, units), bf16),
            pltpu.VMEM((depth, units), bf16),
            pltpu.VMEM((units, depth), bf16),
            pltpu.VMEM((count, share, depth), bf16),
            pltpu.VMEM((2, share, depth), bf16),
            pltpu.VMEM((share, depth), bf16),
            pltpu.VMEM((count, share, depth), bf16),
            pltpu.VMEM((count, share, depth), bf16),
            pltpu.VMEM((3, share, depth), bf16),
            pltpu.VMEM((2, share, depth), bf16),
            pltpu.VMEM((share, depth), bf16),
            pltpu.SemaphoreType.DMA((3,)),
            pltpu.SemaphoreType.DMA((2,)),
            pltpu.SemaphoreType.DMA((4,)),
            pltpu.SemaphoreType.DMA((5, PIECES)),
            pltpu.SemaphoreType.DMA((4, PIECES)),
            pltpu.SemaphoreType.DMA((3, PIECES)),
            pltpu.SemaphoreType.DMA((3, PIECES)),
            pltpu.SemaphoreType.DMA((2, PIECES)),
            pltpu.SemaphoreType.DMA,
            pltpu.SemaphoreType.DMA,
            pltpu.SemaphoreType.DMA((9,)),
            pltpu.SemaphoreType.DMA,
            pltpu.SemaphoreType.DMA((4,)),
            pltpu.SemaphoreType.DMA((4,)),
        ),
        flops=12 * total * depth * units,
        moved=2 * (3 * depth * units + 4 * total * depth),
        collective=1,
    )
    results = call(
        functools.partial(attention_back_kernel, teams),
        [
            ((share, depth), bf16),
            ((share, depth), f32),
            ((3, RANK, depth), f32),
            ((3, RANK, group), f32),
            ((3, group), f32),
            ((2, RANK, depth), f32),
            ((2, RANK, units), f32),
            ((2, units), f32),
            ((RANK, group), f32),
            ((RANK, units), f32),
            ((2, RANK, depth), f32),
            ((1, depth), f32),
            ((1, depth), f32),
        ],
        (
            lengths,
            query,
            keys,
            values,
            att,
            lse,
            mixed.reshape(total, group),
            qkv_summed,
            qkv_norms,
            qkv_mags,
            qkv_full,
            qkv_inner,
            lt_qkv,
            qkv_right,
            angles,
            gain_attn,
            early,
            early_out,
            early_rows,
            early_mags,
            exit_norms,
            down_mag,
            exit_right,
            full_down,
            down_left.T,
            first,
            part,
            w_query,
            w_key,
            w_value,
            w_down,
            inputs,
            grad_middle,
            middle,
            cotangent,
        ),
        specs=[SMEM] + [ANY] * 4 + [VMEM] + [ANY] * 2 + [VMEM] * 17 + [ANY] * 10,
        scratch=(
            pltpu.VMEM((total, group), bf16),
            pltpu.VMEM((total, group), bf16),
            pltpu.VMEM((total, group), bf16),
            pltpu.VMEM((total, group), bf16),
            pltpu.VMEM((total, group), bf16),
            pltpu.VMEM((3, total, group), bf16),
            pltpu.SemaphoreType.DMA((6,)),
            pltpu.VMEM((3 * RANK, depth), bf16),
            pltpu.VMEM((3, total, group), bf16),
            pltpu.VMEM((total, HEAD_DIM), f32),
            pltpu.VMEM((total, HEAD_DIM), f32),
            pltpu.VMEM((HEAD_DIM, total), f32),
            pltpu.VMEM((8, group), f32),
            pltpu.VMEM((3, depth, group), bf16),
            pltpu.VMEM((total, depth), bf16),
            pltpu.VMEM((3, share, depth), bf16),
            pltpu.VMEM((2, share, depth), bf16),
            pltpu.VMEM((2, share, depth), bf16),
            pltpu.VMEM((2, share, depth), bf16),
            pltpu.VMEM((4, share, depth), bf16),
            pltpu.VMEM((8 * RANK, depth), bf16),
            pltpu.VMEM((teams, 16, depth * 8 // teams), bf16),
            pltpu.VMEM((count, 16, depth * 8 // teams), bf16),
            pltpu.VMEM((teams, 16, depth * 8 // teams), bf16),
            pltpu.VMEM((teams, 4 * RANK, group), bf16),
            pltpu.VMEM((teams, 4 * RANK, units), bf16),
            pltpu.VMEM((2, depth), f32),
            pltpu.VMEM((count, 2, depth), f32),
            pltpu.VMEM((teams, 2, depth), f32),
            pltpu.SemaphoreType.DMA((5,)),
            pltpu.SemaphoreType.DMA((4,)),
            pltpu.SemaphoreType.DMA((3, PIECES)),
            pltpu.SemaphoreType.DMA((3, PIECES)),
            pltpu.SemaphoreType.DMA((2, PIECES)),
            pltpu.SemaphoreType.DMA((4, PIECES)),
            pltpu.SemaphoreType.DMA((2, PIECES)),
            pltpu.SemaphoreType.DMA((2, PIECES)),
            pltpu.SemaphoreType.DMA((teams,)),
            pltpu.SemaphoreType.DMA((teams,)),
            pltpu.SemaphoreType.DMA((count,)),
            pltpu.SemaphoreType.DMA((count,)),
            pltpu.SemaphoreType.DMA((teams,)),
            pltpu.SemaphoreType.DMA((teams,)),
            pltpu.SemaphoreType.DMA((teams,)),
            pltpu.SemaphoreType.DMA((teams,)),
            pltpu.SemaphoreType.DMA((teams,)),
            pltpu.SemaphoreType.DMA((teams,)),
            pltpu.SemaphoreType.DMA((count,)),
            pltpu.SemaphoreType.DMA((count,)),
            pltpu.SemaphoreType.DMA((teams,)),
            pltpu.SemaphoreType.DMA((teams,)),
        ),
        flops=6 * total * depth * group + 10 * total * total * group,
        moved=2 * (2 * total * depth + 3 * depth * group + 8 * total * group),
        collective=2,
    )
    (
        outputs,
        input_grad,
        grad_qkv_left,
        grad_qkv_right,
        grad_qkv_mags,
        grad_mlp_left,
        grad_mlp_right,
        grad_mlp_mags,
        grad_out_left,
        grad_down_left,
        grad_exit_right,
        grad_out_mags,
        grad_down_mags,
    ) = results
    results = [*results, norm_stats]

    def hand_over(*refs):
        half = len(results)
        for index in range(half):
            refs[half + index][...] = refs[index][...]

    (
        outputs,
        input_grad,
        grad_qkv_left,
        grad_qkv_right,
        grad_qkv_mags,
        grad_mlp_left,
        grad_mlp_right,
        grad_mlp_mags,
        grad_out_left,
        grad_down_left,
        grad_exit_right,
        grad_out_mags,
        grad_down_mags,
        norm_stats,
    ) = call(
        hand_over,
        [(item.shape, item.dtype) for item in results],
        results,
        moved=2 * share * depth * 6,
    )
    return (
        outputs,
        input_grad,
        jnp.transpose(grad_qkv_left, (0, 2, 1)),
        grad_qkv_right,
        grad_qkv_mags,
        jnp.transpose(grad_mlp_left, (0, 2, 1)),
        grad_mlp_right,
        grad_mlp_mags,
        grad_out_left.T,
        grad_down_left.T,
        grad_exit_right,
        grad_out_mags.reshape(depth),
        grad_down_mags.reshape(depth),
        norm_stats,
    )


def solution(mesh):
    placed = (
        P("rows", None),
        P("rows", None),
        P("rows"),
        P(),
        P(),
        P(None, "heads"),
        P(None, "heads"),
        P(None, "heads"),
        P("heads", None),
        P(None, "heads"),
        P(None, "heads"),
        P("heads", None),
        P(),
        P(None, None, "heads"),
        P(None, "heads"),
        P(),
        P(None, None, "heads"),
        P(None, "heads"),
        P("heads", None),
        P("heads", None),
        P(),
        P(),
        P(),
    )
    return jax.shard_map(
        local,
        mesh=mesh,
        in_specs=placed,
        out_specs=(
            P(("rows", "heads"), None),
            P(("rows", "heads"), None),
            P(),
            P(None, None, "heads"),
            P(None, "heads"),
            P(),
            P(None, None, "heads"),
            P(None, "heads"),
            P("heads", None),
            P("heads", None),
            P(),
            P(),
            P(),
            P(),
        ),
        check_vma=False,
    )
```

```python
import functools
import math

import jax
import jax.numpy as jnp
import numpy as np
from jax import lax
from jax.experimental import pallas as pl
from jax.experimental.pallas import tpu as pltpu
from jax.sharding import PartitionSpec as P

HEAD_DIM = 128
RANK = 16
norm_eps = 1e-05
rope_base = 10000.0
mask_fill = -1e30
SCALE = 32.0 / RANK

f32 = jnp.float32
bf16 = jnp.bfloat16
MESH = pl.DeviceIdType.MESH
VMEM = pl.BlockSpec(memory_space=pltpu.VMEM)
SMEM = pl.BlockSpec(memory_space=pltpu.SMEM)
ANY = pl.BlockSpec(memory_space=pl.ANY)
LIMIT = 63 << 20
PIECES = 4


def nn(left, right):
    return jnp.dot(left, right, preferred_element_type=f32)


def nt(left, right):
    return lax.dot_general(left, right, (((1,), (1,)), ((), ())), preferred_element_type=f32)


def nn_exact(left, right):
    return jnp.dot(left, right, precision=lax.Precision.HIGHEST, preferred_element_type=f32)


def nt_exact(left, right):
    return lax.dot_general(
        left,
        right,
        (((1,), (1,)), ((), ())),
        precision=lax.Precision.HIGHEST,
        preferred_element_type=f32,
    )


def split_rows(field):
    high = field.astype(bf16)
    return jnp.concatenate([high, (field - high.astype(f32)).astype(bf16)], axis=0)


def square_sums(ref, columns, chunk=128):
    depth = ref.shape[0]
    width = columns.size if isinstance(columns, pl.Slice) else columns.stop - columns.start

    def step(index, total):
        piece = ref[pl.ds(pl.multiple_of(index * chunk, chunk), chunk), columns].astype(f32)
        return total + jnp.sum((piece * piece).reshape(chunk // 8, 8, width), axis=0)

    total = lax.fori_loop(0, depth // chunk, step, jnp.zeros((8, width), f32))
    return jnp.sum(total, axis=0, keepdims=True)


def direction(squares, pieces, gram, right):
    plain = pieces[:RANK] + pieces[RANK:]
    turned = nn_exact(gram, jnp.concatenate([right, right], axis=0))
    full = plain + SCALE * (turned[:RANK] + turned[RANK:])
    return squares + SCALE * jnp.sum(right * (plain + full), axis=0, keepdims=True), full


def padded_right(right, at, count, factor):
    low = factor * right.astype(bf16).astype(f32)
    zero = jnp.zeros_like(low)
    return jnp.concatenate([low if slot == at else zero for slot in range(count)], axis=0).astype(bf16)


def norm_value(rows, gain):
    inverse = lax.rsqrt(jnp.mean(rows * rows, axis=-1, keepdims=True) + norm_eps)
    return rows * inverse * gain, inverse


def row_of(ref):
    return ref[...].astype(f32).reshape(1, ref.shape[0])


def turning(angles):
    swapped = pltpu.roll(angles, HEAD_DIM // 2, 1)
    first = lax.broadcasted_iota(jnp.int32, angles.shape, 1) < HEAD_DIM // 2
    return jnp.where(first, angles, swapped), jnp.where(first, -swapped, angles)


def greet(count):
    row, me = lax.axis_index("rows"), lax.axis_index("heads")
    barrier = pltpu.get_barrier_semaphore()
    for step in range(1, count):
        pl.semaphore_signal(
            barrier, inc=1, device_id=(row, lax.rem(me + step, count)), device_id_type=MESH
        )
    pl.semaphore_wait(barrier, count - 1)


def attention_forward_kernel(
    count,
    teams,
    length_ref,
    gain_ref,
    lt,
    right,
    mags,
    angles,
    lt_out,
    lt_down,
    right_exit,
    mags_out,
    mags_down,
    gain_second,
    lt_mlp,
    right_mlp,
    mags_mlp,
    x_any,
    w_query,
    w_key,
    w_value,
    w_out,
    w_down_any,
    w_gate_any,
    w_up_any,
    first,
    query_any,
    keys_any,
    values_any,
    att_any,
    summed_any,
    w_full,
    lse,
    inner_ref,
    norms_ref,
    full_ref,
    gathered,
    middle,
    second,
    summed_out,
    inner_out,
    full_out,
    lt_full,
    exit_norms,
    full_down,
    norms_mlp,
    full_mlp,
    norm_table,
    ext,
    weights,
    query,
    keys,
    values,
    att,
    summed,
    wf,
    w_down,
    w_mlp,
    x_own,
    ext_out,
    lt_in,
    squares_in,
    down_in,
    tables,
    load_sem,
    store_sem,
    send_sem,
    recv_sem,
    line_send,
    line_recv,
    team_send,
    team_recv,
    small_send,
    small_recv,
):
    team, me = lax.axis_index("rows"), lax.axis_index("heads")
    total, depth = x_any.shape
    share = total // count
    group = query.shape[1]
    heads = group // HEAD_DIM
    deep = wf.shape[2]
    bits = teams.bit_length() - 1

    def move(source, target, send, recv, peer_team, peer):
        return pltpu.make_async_remote_copy(
            src_ref=source,
            dst_ref=target,
            send_sem=send,
            recv_sem=recv,
            device_id=(peer_team, peer),
            device_id_type=MESH,
        )

    def flip(index, bit):
        weight = 1 << bit
        return index + weight - 2 * weight * lax.rem(index // weight, 2)

    x_load = pltpu.make_async_copy(x_any, ext.at[:total], load_sem.at[0])
    own_load = pltpu.make_async_copy(
        x_any.at[pl.ds(pl.multiple_of(me * share, share), share), :], x_own, load_sem.at[1]
    )
    loads = [
        pltpu.make_async_copy(source, weights.at[index], load_sem.at[2 + index])
        for index, source in enumerate((w_query, w_key, w_value))
    ]
    shard_loads = [
        pltpu.make_async_copy(
            w_out.at[index * deep : (index + 1) * deep, :], wf.at[me, index], load_sem.at[6 + index]
        )
        for index in range(teams)
    ]
    down_load = pltpu.make_async_copy(w_down_any, w_down, load_sem.at[5])
    mlp_loads = [
        pltpu.make_async_copy(source, w_mlp.at[index], load_sem.at[6 + teams + index])
        for index, source in enumerate((w_gate_any, w_up_any))
    ]
    x_load.start()
    for load in loads:
        load.start()
    own_load.start()

    barrier = pltpu.get_barrier_semaphore()
    for step in range(1, count):
        pl.semaphore_signal(
            barrier, inc=1, device_id=(team, lax.rem(me + step, count)), device_id_type=MESH
        )
    for bit in range(bits):
        pl.semaphore_signal(barrier, inc=1, device_id=(flip(team, bit), me), device_id_type=MESH)
    pl.semaphore_wait(barrier, count - 1 + bits)

    def line_copy(step):
        peer = lax.rem(me + step, count)
        return move(
            w_out.at[pl.ds(pl.multiple_of(team * deep, deep), deep), :],
            wf.at[me, team],
            line_send.at[step],
            line_recv.at[step],
            team,
            peer,
        )

    for step in range(1, count):
        line_copy(step).start()

    half = depth // 2
    outer_bits = list(range(1, bits))
    rounds = []
    slot = 0
    for stage in range(bits - 1):
        copies = []
        for side, order in enumerate((outer_bits, outer_bits[::-1])):
            held = [team]
            for bit in order[:stage]:
                held = held + [flip(index, bit) for index in held]
            for index in held:
                for step in range(1, count):
                    copies.append((slot, index, side, step, order[stage]))
                    slot += 1
        rounds.append(copies)
    held = [team]
    for bit in outer_bits:
        held = held + [flip(index, bit) for index in held]
    copies = []
    for index in held:
        for step in range(1, count):
            copies.append((slot, index, None, step, 0))
            slot += 1
    rounds.append(copies)

    def team_copy(entry):
        slot, index, side, step, bit = entry
        block = lax.rem(me + step, count)
        if side is None:
            place = wf.at[block, index]
        else:
            place = wf.at[block, index, :, side * half : (side + 1) * half]
        return move(place, place, team_send.at[slot], team_recv.at[slot], flip(team, bit), me)

    def advance(stage, distance):
        if stage == 0:
            line_copy(distance).wait_recv()
        else:
            for entry in rounds[stage - 1]:
                if entry[3] == count - distance:
                    team_copy(entry).wait_recv()
        if stage < len(rounds):
            for entry in rounds[stage]:
                if entry[3] == count - distance:
                    team_copy(entry).start()

    order = sorted(
        ((stage, distance) for stage in range(len(rounds) + 1) for distance in range(1, count)),
        key=lambda item: (2 * item[0] + 3 * item[1], item[0]),
    )

    def progress(steps):
        for _ in range(steps):
            if order:
                advance(*order.pop(0))

    def small_copy(kind, step):
        ref = (lt_in, squares_in, down_in, tables)[kind]
        return move(
            ref.at[me],
            ref.at[me],
            small_send.at[kind, step],
            small_recv.at[kind, step],
            team,
            lax.rem(me + step, count),
        )

    lt_in[me] = lt_out[...]
    for step in range(1, count):
        small_copy(0, step).start()

    gain = row_of(gain_ref)
    x_load.wait()

    @pl.loop(0, total // 128)
    def _(index):
        rows = pl.ds(pl.multiple_of(index * 128, 128), 128)
        normed, _ = norm_value(ext[rows, :].astype(f32), gain)
        ext[rows, :] = normed.astype(bf16)

    stores = [pltpu.make_async_copy(ext.at[:total], first, store_sem.at[0])]
    stores[0].start()
    for load in shard_loads:
        load.start()
    down_load.start()
    for load in mlp_loads:
        load.start()
    inner = nt(ext[:total, :], lt[...].astype(bf16)).astype(bf16)
    inner_ref[...] = inner
    length = length_ref[0]
    factor = 1.0 / math.sqrt(HEAD_DIM)
    copies = []

    def project(index, start):
        block = slice(index * RANK, (index + 1) * RANK)
        adapters = split_rows(lt[block, :])
        ext[total:, :] = adapters
        gram = nt(adapters, adapters)
        columns = slice(start, start + 256)
        product = nn(ext[...], weights[index, :, columns])
        local_right = right[index, :, columns]
        squares, full = direction(
            square_sums(weights.at[index], columns), product[total:], gram, local_right
        )
        norms = jnp.sqrt(squares)
        norms_ref[index : index + 1, columns] = norms
        full_ref[index, :, columns] = full
        z = product[:total] + nn(inner, padded_right(local_right, index, 3, SCALE))
        summed[index, :, columns] = z.astype(bf16)
        y = z * (mags[index : index + 1, columns] / norms)
        if index == 2:
            values[:, columns] = y.astype(bf16)
        else:
            for head in range(2):
                part = y[:, head * HEAD_DIM : (head + 1) * HEAD_DIM]
                cosines, sines = turning(angles[...])
                turned = part * cosines + pltpu.roll(part, HEAD_DIM // 2, 1) * sines
                place = slice(start + head * HEAD_DIM, start + (head + 1) * HEAD_DIM)
                (query if index == 0 else keys)[:, place] = turned.astype(bf16)

    def attend(head):
        place = slice(head * HEAD_DIM, (head + 1) * HEAD_DIM)
        turned_values = values[:, place].astype(f32).T.astype(bf16)
        for block in range(total // 256):
            reach = (block + 1) * 256
            at = slice(block * 256, reach)
            scores = nt(keys[:reach, place], query[at, place])
            spots = lax.broadcasted_iota(jnp.int32, (reach, 256), 0)
            asking = lax.broadcasted_iota(jnp.int32, (reach, 256), 1) + block * 256
            allowed = (spots <= asking) & (spots < length)
            scores = jnp.where(allowed, scores * factor, mask_fill)
            peak = jnp.max(scores, axis=0, keepdims=True)
            exps = jnp.exp(scores - peak)
            totals = jnp.sum(exps, axis=0, keepdims=True)
            probs = (exps * (1.0 / totals)).astype(bf16)
            mixed = nn(turned_values[:, :reach], probs)
            att[at, place] = mixed.T.astype(bf16)
            lse[head : head + 1, at] = peak + jnp.log(totals)
        for step in range(1, count):
            peer = lax.rem(me + step, count)
            copy = move(
                att.at[pl.ds(pl.multiple_of(peer * share, share), share), place],
                gathered.at[me, :, place],
                send_sem.at[head, step],
                recv_sem.at[head, step],
                team,
                peer,
            )
            copy.start()
            copies.append(copy)

    def exit_stats():
        for load in shard_loads:
            load.wait()
        down_load.wait()
        for index, (pieces, chunk) in enumerate(((lt_out[...], 64), (lt_down[...], 128))):
            adapters = split_rows(pieces)
            gram = nt(adapters, adapters)
            for start in range(0, depth, 512):
                columns = slice(start, start + 512)
                if index == 0:
                    weight = wf[me, :, :, columns].reshape(group, 512)
                    low = weight.astype(f32)
                    sums = jnp.sum(low * low, axis=0, keepdims=True)
                else:
                    weight = w_down[:, columns]
                    sums = square_sums(w_down, columns)
                squares, full = direction(
                    sums, nn(adapters, weight), gram, right_exit[index, :, columns]
                )
                squares_in[me, index : index + 1, columns] = squares
                if index == 1:
                    down_in[me, :, columns] = full.astype(bf16)
        for step in range(1, count):
            small_copy(1, step).start()
        for step in range(1, count):
            small_copy(2, step).start()

    for load in loads:
        load.wait()
    for start in range(0, group, 256):
        for index in range(3):
            project(index, start)
        for head in range(start // HEAD_DIM, start // HEAD_DIM + 2):
            attend(head)
            progress(1)
        if start == 0:
            progress(2)
    for source, target in (
        (summed, summed_any),
        (query, query_any),
        (keys, keys_any),
        (values, values_any),
        (att, att_any),
    ):
        stores.append(pltpu.make_async_copy(source, target, store_sem.at[len(stores)]))
        stores[-1].start()
    progress(1)
    gathered[me] = att[pl.ds(pl.multiple_of(me * share, share), share), :]

    exit_stats()

    units = mags_mlp.shape[1]
    for index in range(2):
        mlp_loads[index].wait()
        adapters = split_rows(lt_mlp[index * RANK : (index + 1) * RANK, :])
        squares, full = direction(
            square_sums(w_mlp.at[index], slice(0, units)),
            nn(adapters, w_mlp[index]),
            nt(adapters, adapters),
            right_mlp[index],
        )
        norms = jnp.sqrt(squares)
        norms_mlp[index : index + 1, :] = norms
        full_mlp[index] = full
        tables[me, index : index + 1, :units] = norms
        tables[me, index + 2 : index + 3, :units] = mags_mlp[index : index + 1, :] - norms
        progress(1)
    for index in range(3):
        norms = norms_ref[index : index + 1, :]
        at = slice(index * group, (index + 1) * group)
        tables[me, 4:5, at] = norms
        tables[me, 5:6, at] = mags[index : index + 1, :] - norms
    for step in range(1, count):
        small_copy(3, step).start()
    for step in range(1, count):
        small_copy(0, step).wait()
    for index in range(count):
        lt_full[:, index * group : (index + 1) * group] = lt_in[index]
    for copy in copies:
        copy.wait()
    for index in range(count):
        ext_out[:share, index * group : (index + 1) * group] = gathered[index]
    adapters = split_rows(lt_full[...])
    ext_out[share:, :] = adapters
    gram = nt(adapters, adapters)
    inner_low = adapters[:RANK]
    inner = nt(ext_out[:share, :], inner_low)
    inner_out[...] = inner
    low = inner.astype(bf16)
    own_load.wait()
    for step in range(1, count):
        small_copy(1, step).wait()
    squares = squares_in[0]
    for index in range(1, count):
        squares = squares + squares_in[index]
    exit_norms[...] = jnp.sqrt(squares)
    progress(len(order))
    store_full = [
        pltpu.make_async_copy(
            wf.at[index // teams, index % teams],
            w_full.at[index * deep : (index + 1) * deep, :],
            store_sem.at[6 + index],
        )
        for index in range(count * teams)
    ]
    for store in store_full:
        store.start()
    for start in range(0, depth, 512):
        columns = slice(start, start + 512)
        weight = wf[:, :, :, columns].reshape(depth, 512)
        local_right = right_exit[0, :, columns]
        product = nn(ext_out[...], weight)
        _, full = direction(0.0, product[share:], gram, local_right)
        full_out[:, columns] = full
        z = product[:share] + nn(low, padded_right(local_right, 0, 1, SCALE))
        summed_out[:, columns] = z.astype(bf16)
        middle[:, columns] = x_own[:, columns].astype(f32) + z * (
            mags_out[:, columns] / exit_norms[0:1, columns]
        )
    normed, _ = norm_value(middle[...], row_of(gain_second))
    second[...] = normed.astype(bf16)
    for step in range(1, count):
        small_copy(2, step).wait()
        small_copy(3, step).wait()
    edge = 0
    for index in range(3):
        for peer in range(count):
            at = slice(index * group, (index + 1) * group)
            norm_table[0:1, edge : edge + group] = tables[peer, 4:5, at]
            norm_table[1:2, edge : edge + group] = tables[peer, 5:6, at]
            edge += group
    for index in range(2):
        for peer in range(count):
            norm_table[0:1, edge : edge + units] = tables[peer, index : index + 1, :units]
            norm_table[1:2, edge : edge + units] = tables[peer, index + 2 : index + 3, :units]
            edge += units
    for index, magnitude in ((0, mags_out), (1, mags_down)):
        norm = exit_norms[index : index + 1, :]
        norm_table[0:1, edge : edge + depth] = norm
        norm_table[1:2, edge : edge + depth] = magnitude[...] - norm
        edge += depth
    full = down_in[0].astype(f32)
    for index in range(1, count):
        full = full + down_in[index].astype(f32)
    full_down[...] = full
    for store in stores + store_full:
        store.wait()
    for step in range(1, count):
        line_copy(step).wait_send()
    for copies in rounds:
        for entry in copies:
            team_copy(entry).wait_send()


def feed_forward_kernel(
    own,
    cot,
    w_gate_any,
    w_up_any,
    w_down_any,
    lt_pair,
    lt_down_pair,
    right,
    mags,
    right_exit,
    mags_down,
    exit_norms,
    norms_ref,
    fulls,
    mags_out,
    gain_ref,
    inner_out,
    lt_out,
    full_out,
    middle_any,
    summed_any,
    gathered_any,
    w_full_any,
    part,
    early,
    early_rows,
    grad_middle,
    mixed,
    early_out,
    early_mags,
    grad_second,
    adapted,
    pieces_out,
    lth,
    lt_down,
    factors,
    w_gate,
    w_up,
    w_down,
    sec,
    cots,
    cot_own,
    parts,
    mine,
    outer,
    inner_sums,
    near,
    load_sem,
    cot_sem,
    part_sem,
    gather_send,
    gather_recv,
    sum_send,
    outer_recv,
    inner_recv,
    near_send,
    near_recv,
    exit_sem,
    own_sem,
    mixed_send,
    mixed_recv,
):
    row, me = lax.axis_index("rows"), lax.axis_index("heads")
    size, depth = own.shape
    half = size // PIECES
    inward = jnp.where(me < 2, 1, -1)
    is_end = (me == 0) | (me == 3)
    in_middle = jnp.logical_not(is_end)
    ahead, behind = me + inward, me - inward

    def move(source, target, send, recv, peer):
        return pltpu.make_async_remote_copy(
            src_ref=source,
            dst_ref=target,
            send_sem=send,
            recv_sem=recv,
            device_id=(row, peer),
            device_id_type=MESH,
        )

    def rows_of(piece):
        start = piece * half
        return pl.ds(start if isinstance(piece, int) else pl.multiple_of(start, half), half)

    def gather_copy(slot, block, piece, peer):
        place = sec.at[block, rows_of(piece), :]
        return move(place, place, gather_send.at[slot, piece], gather_recv.at[block, piece], peer)

    def gather_start(slot, block, peer):
        for piece in range(PIECES):
            gather_copy(slot, block, piece, peer).start()

    def gather_wait(block, pieces, forward=None):
        for piece in pieces:
            gather_copy(0, block, piece, ahead).wait_recv()
            if forward is not None:
                slot, peer = forward
                gather_copy(slot, block, piece, peer).start()

    right_out, right_down = right_exit.at[0], right_exit.at[1]
    norms_out, norms_down = exit_norms.at[0:1], exit_norms.at[1:2]
    greet(4)
    lth[...] = lt_pair[...].astype(bf16)
    lt_down[...] = lt_down_pair[...].astype(bf16)
    loads = [
        pltpu.make_async_copy(source, target, load_sem.at[index])
        for index, (source, target) in enumerate(
            ((w_gate_any, w_gate), (w_up_any, w_up), (w_down_any, w_down))
        )
    ]
    load_own = pltpu.make_async_copy(own, sec.at[me], own_sem)
    load_own.start()
    load_own.wait()
    gather_start(0, me, ahead)

    @pl.when(jnp.logical_not(is_end))
    def _():
        gather_start(1, me, behind)

    for load in loads:
        load.start()

    def block_at(step):
        middle = jnp.where(
            step == 0, me, jnp.where(step == 1, ahead, jnp.where(step == 2, behind, ahead + inward))
        )
        return jnp.where(is_end, jnp.where(step == 3, me, me + inward * (step + 1)), middle)

    def token_rows(step):
        return pl.ds(pl.multiple_of(block_at(step) * size, size), size)

    def cot_load(step):
        slot = lax.rem(step, 2)
        return pltpu.make_async_copy(cot.at[token_rows(step), :], cots.at[slot], cot_sem.at[slot])

    def part_store(step):
        return pltpu.make_async_copy(
            parts.at[block_at(step)], part.at[token_rows(step), :], part_sem.at[step]
        )

    own_rows = pl.ds(pl.multiple_of(me * size, size), size)
    near_store = pltpu.make_async_copy(parts.at[me], part.at[own_rows, :], part_sem.at[0])
    near_copy = move(parts.at[ahead], near, near_send, near_recv, ahead)

    cot_load(0).start()
    weights = (w_gate, w_up)
    group = gathered_any.shape[2]
    factors[...] = mags[...] / norms_ref[...]
    factor_down = mags_down[...] / norms_down[...]
    grad_left, grad_right_down = early.at[: 2 * RANK], early.at[2 * RANK :]
    grad_right = [early_rows.at[index * RANK : (index + 1) * RANK] for index in range(2)]
    grad_left_down = early_rows.at[2 * RANK : 3 * RANK]
    grad_mags = early_rows.at[3 * RANK :]
    early[...] = jnp.zeros_like(early)
    early_rows[...] = jnp.zeros_like(early_rows)
    for load in loads:
        load.wait()

    def outer_copy(slot, piece, block):
        return move(
            mine.at[block, rows_of(piece), :],
            outer.at[slot, rows_of(piece), :],
            sum_send.at[slot, piece],
            outer_recv.at[slot, piece],
            ahead,
        )

    def inner_copy(slot, piece, block, send, peer):
        return move(
            mine.at[block, rows_of(piece), :],
            inner_sums.at[slot, rows_of(piece), :],
            sum_send.at[send, piece],
            inner_recv.at[slot, piece],
            peer,
        )

    def add_into(block, piece, ref):
        at = rows_of(piece)
        mine[block, at, :] = (
            mine[block, at, :].astype(f32) + ref[at, :].astype(f32)
        ).astype(bf16)

    def pass_on(distance, piece):
        block = me + inward * distance
        outer_copy(distance, piece, me).wait_recv()
        add_into(block, piece, outer.at[distance])
        inner_copy(distance - 1, piece, block, distance - 1, ahead).start()

    def hand_out(piece):
        inner_copy(1, piece, me, 2, behind).wait_recv()
        add_into(behind, piece, inner_sums.at[1])
        inner_copy(0, piece, behind, 2, behind).start()

    def work(block, first_row, width, slot, between, after):
        at = pl.ds(first_row, width)
        x = sec[block, at, :]
        inner = nt(x, lth[...])
        inner_low = inner.astype(bf16)
        zs = [
            nn(x, weights[index][...])
            + nn(inner_low, padded_right(right[index], index, 2, SCALE))
            for index in range(2)
        ]
        gate = zs[0] * factors[0:1, :]
        upper = zs[1] * factors[1:2, :]
        sigmoid = 1.0 / (1.0 + jnp.exp(-gate))
        activated = gate * sigmoid
        hidden = (activated * upper).astype(bf16)
        right_low = right_down[...].astype(bf16)
        inner_down = nt(hidden, lt_down[...])

        parts[block, at, :] = (
            nn(hidden, w_down[...]) + SCALE * nn(inner_down.astype(bf16), right_low)
        ).astype(bf16)

        between()
        gz_down = (cots[slot, at, :].astype(f32) * factor_down).astype(bf16)
        gin_down = SCALE * nt(gz_down, right_low)
        grad_hidden = nt(gz_down, w_down[...]) + nn(gin_down.astype(bf16), lt_down[...])
        grad_left_down[...] += nn(gin_down.T.astype(bf16), hidden)
        grad_right_down[...] += SCALE * nn(inner_down.T.astype(bf16), gz_down)
        grads = (
            grad_hidden * upper * sigmoid * (1.0 + gate * (1.0 - sigmoid)),
            grad_hidden * activated,
        )
        gin = jnp.zeros((width, 2 * RANK), f32)
        gzs = []
        for index in range(2):
            grad_mags[index : index + 1, :] += jnp.sum(grads[index] * zs[index], axis=0, keepdims=True)
            gz = (grads[index] * factors[index : index + 1, :]).astype(bf16)
            gin = gin + nt(gz, padded_right(right[index], index, 2, SCALE))
            gzs.append(gz)
        gin_low = gin.astype(bf16)
        mine[block, at, :] = (
            nt(gzs[0], w_gate[...]) + nt(gzs[1], w_up[...]) + nn(gin_low, lth[...])
        ).astype(bf16)

        after()
        grad_left[...] += nn(gin.T.astype(bf16), x)
        inner_turned = inner.T.astype(bf16)
        for index in range(2):
            grad_right[index][...] += (
                SCALE * nn(inner_turned, gzs[index])[index * RANK : (index + 1) * RANK]
            )

    wide = size // 2

    @pl.when(is_end)
    def _():
        @pl.loop(0, 6)
        def _(half_step):
            step, side = half_step // 2, lax.rem(half_step, 2)
            block = block_at(step)
            for piece in range(PIECES // 2):
                gather_copy(0, block, side * (PIECES // 2) + piece, ahead).wait_recv()

            def between():
                @pl.when(side == 0)
                def _():
                    cot_load(step + 1).start()
                    cot_load(step).wait()

                @pl.when(side == 1)
                def _():
                    part_store(step).start()

            def after():
                for piece in range(PIECES // 2):
                    outer_copy(step, side * (PIECES // 2) + piece, block).start()

            work(block, pl.multiple_of(side * wide, wide), wide, lax.rem(step, 2), between, after)

        near_copy.start()

    @pl.loop(0, 4)
    def _(step):
        @pl.when(in_middle | (step == 3))
        def _():
            block = block_at(step)

            @pl.when(in_middle & (step == 2))
            def _():
                gather_wait(ahead + inward, range(PIECES), (4, behind))

            @pl.when(in_middle & (step == 3))
            def _():
                pass_on(1, 1)

            def between():
                @pl.when(in_middle & (step < 3))
                def _():
                    cot_load(step + 1).start()

                cot_load(step).wait()

                @pl.when(is_end | (step > 0))
                def _():
                    part_store(step).start()

                @pl.when(in_middle & (step == 0))
                def _():
                    for piece in range(PIECES):
                        gather_wait(behind, (piece,), (2, ahead))
                        gather_wait(ahead, (piece,), (3, behind))

                @pl.when(in_middle & (step == 2))
                def _():
                    pass_on(1, 0)

                @pl.when(in_middle & (step == 3))
                def _():
                    pass_on(1, 2)
                    pass_on(1, 3)

            work(block, 0, size, lax.rem(step, 2), between, lambda: None)

    @pl.when(in_middle)
    def _():
        pass_on(2, 0)
        pass_on(2, 1)

    for index in range(2):
        block = slice(index * RANK, (index + 1) * RANK)
        norms = norms_ref[index : index + 1, :]
        factor_grad = grad_mags[index : index + 1, :]
        shape = -factor_grad * mags[index : index + 1, :] / (norms * norms * norms)
        shaped = right[index] * shape
        pieces = nt(split_rows(shaped), weights[index][...])
        lt = lt_pair[block, :]
        grad_left[block, :] += SCALE * (
            pieces[:RANK]
            + pieces[RANK:]
            + SCALE * nn_exact(nt_exact(shaped, right[index]), lt)
        )
        grad_right[index][...] += SCALE * fulls[index] * shape
        grad_mags[index : index + 1, :] = factor_grad / norms

    @pl.when(is_end)
    def _():
        part_store(0).wait()
        for piece in range(PIECES):
            gather_copy(0, me, piece, ahead).wait_send()

    @pl.when(in_middle)
    def _():
        for piece in range(PIECES):
            for slot in range(5):
                gather_copy(slot, me, piece, ahead).wait_send()

    for step in range(1, 4):
        part_store(step).wait()
    behind_part = jnp.where(is_end, me, ahead + inward)
    width = depth // 2
    exits = [
        (middle_any, grad_middle),
        (summed_any, parts.at[behind_part]),
        (cot.at[own_rows, :], cot_own),
        (w_full_any.at[:, :width], w_gate.at[:, :width]),
        (w_full_any.at[:, width:], w_up.at[:, :width]),
    ] + [
        (gathered_any.at[index], sec.at[index, :, group : 2 * group]) for index in range(4)
    ]
    exit_loads = [
        pltpu.make_async_copy(source, target, exit_sem.at[index])
        for index, (source, target) in enumerate(exits)
    ]
    for load in exit_loads:
        load.start()

    @pl.when(in_middle)
    def _():
        hand_out(0)
        pass_on(2, 2)
        hand_out(1)
        pass_on(2, 3)
        hand_out(2)
        hand_out(3)

    @pl.when(is_end)
    def _():
        for slot in range(3):
            for piece in range(PIECES):
                outer_copy(slot, piece, me).wait_send()

    for load in exit_loads:
        load.wait()
    gain = row_of(gain_ref)
    norm = norms_out[...]
    scale_out = mags_out[...] / norm
    factor_grad = jnp.zeros((1, depth), f32)
    for piece in range(PIECES):
        at = rows_of(piece)

        @pl.when(in_middle)
        def _():
            outer_copy(0, piece, me).wait_recv()
            grad_second[at, :] = outer[0, at, :].astype(f32)

        @pl.when(is_end)
        def _():
            grad_second[at, :] = jnp.zeros((half, depth), f32)

        inner_copy(0, piece, me, 0, ahead).wait_recv()
        total = (
            grad_second[at, :] + mine[me, at, :].astype(f32) + inner_sums[0, at, :].astype(f32)
        )
        rows = grad_middle[at, :]
        inverse = lax.rsqrt(jnp.mean(rows * rows, axis=-1, keepdims=True) + norm_eps)
        scaled = total * gain
        grad = (
            cot_own[at, :].astype(f32)
            + inverse * scaled
            - rows * (inverse * inverse * inverse) * jnp.mean(rows * scaled, axis=-1, keepdims=True)
        )
        grad_middle[at, :] = grad
        factor_grad = factor_grad + jnp.sum(
            grad * parts[behind_part, at, :].astype(f32), axis=0, keepdims=True
        )
        adapted[at, :] = (grad * scale_out).astype(bf16)
    shape = -factor_grad * mags_out[...] / (norm * norm * norm)
    shaped = right_out[...] * shape
    adapted[size:, :] = split_rows(shaped)
    gz = adapted[:size, :]
    gin = SCALE * nt(gz, right_out[...].astype(bf16))
    gin_low = gin.astype(bf16)
    def mixed_copy(step):
        peer = lax.rem(me + step, 4)
        return move(
            sec.at[peer, :, :group], mixed.at[me], mixed_send.at[step], mixed_recv.at[step], peer
        )

    for step in (2, 1, 3, 4):
        peer = lax.rem(me + step, 4)
        columns = pl.ds(pl.multiple_of(peer * group, group), group)
        moved = nt(adapted[:, :width], w_gate[columns, :width]) + nt(
            adapted[:, width:], w_up[columns, :width]
        )
        result = (moved[:size] + nn(gin_low, lt_out[:, columns].astype(bf16))).astype(bf16)
        if step == 4:
            mixed[me] = result
        else:
            sec[peer, :, :group] = result
            mixed_copy(step).start()
        pieces_out[:, columns] = moved[size:]

    gin_turned = gin.T.astype(bf16)
    mixing = nt_exact(shaped, right_out[...])
    early_mags[...] = factor_grad / norm
    early_out[:RANK, :] = SCALE * (nn(inner_out[...].T.astype(bf16), gz) + full_out[...] * shape)
    early_out[RANK:, :] = SCALE * (
        pieces_out[:RANK, :] + pieces_out[RANK:, :] + SCALE * nn_exact(mixing, lt_out[...])
    )
    for index in range(4):
        at = slice(index * group, (index + 1) * group)
        early_out[RANK:, at] += nn(gin_turned, sec[index, :, group : 2 * group])

    @pl.when(in_middle)
    def _():
        near_copy.wait_recv()
        parts[me] = (parts[me].astype(f32) + near[...].astype(f32)).astype(bf16)
        near_store.start()
        for piece in range(PIECES):
            for send in range(3):
                inner_copy(0, piece, me, send, ahead).wait_send()
        near_store.wait()

    @pl.when(is_end)
    def _():
        near_copy.wait_send()

    for step in range(1, 4):
        mixed_copy(step).wait()


def attention_back_kernel(
    teams,
    length_ref,
    query_any,
    keys_any,
    values_any,
    att_any,
    lse,
    mixed_any,
    summed_any,
    norms_ref,
    mags,
    fulls,
    inner,
    lt_triple,
    right,
    angles,
    gain_ref,
    early,
    early_out,
    early_rows,
    early_mags,
    exit_norms,
    mags_down,
    right_exit,
    full_down,
    lt_down,
    first_any,
    part,
    weights_any_query,
    weights_any_key,
    weights_any_value,
    w_down,
    x_own,
    grad_middle,
    middle,
    cot_own,
    outputs,
    input_grad,
    grad_qkv_left,
    grad_qkv_right,
    grad_qkv_mags,
    grad_mlp_left,
    grad_mlp_right,
    grad_mlp_mags,
    grad_out_left,
    grad_down_left,
    grad_exit_right,
    grad_out_mags,
    grad_down_mags,
    query,
    keys,
    values,
    att,
    mixed,
    summed,
    act_sem,
    lth,
    gz,
    key_sums,
    value_sums,
    query_turned,
    factors,
    weights,
    mine,
    outer,
    inner_sums,
    outer_down,
    inner_down,
    block_part,
    wide,
    wide_in,
    line_in,
    whole,
    group_in,
    unit_in,
    small,
    small_line,
    small_rows,
    load_sem,
    part_sem,
    sum_send,
    outer_recv,
    inner_recv,
    down_send,
    down_outer_recv,
    down_inner_recv,
    wide_send,
    wide_recv,
    line_send,
    line_recv,
    whole_send,
    whole_recv,
    group_send,
    group_recv,
    unit_send,
    unit_recv,
    small_send,
    small_recv,
    final_send,
    final_recv,
):
    right_down, norms_down = right_exit.at[1], exit_norms.at[1:2]
    total = query.shape[0]
    depth = mine.shape[1]
    size = total // 4
    half = size // PIECES
    team, me = lax.axis_index("rows"), lax.axis_index("heads")
    inward = jnp.where(me < 2, 1, -1)
    is_end = (me == 0) | (me == 3)
    in_middle = jnp.logical_not(is_end)
    ahead, behind = me + inward, me - inward

    def move(source, target, send, recv, peer, peer_team=team):
        return pltpu.make_async_remote_copy(
            src_ref=source,
            dst_ref=target,
            send_sem=send,
            recv_sem=recv,
            device_id=(peer_team, peer),
            device_id_type=MESH,
        )

    def rows_of(block, piece=None):
        if piece is None:
            return pl.ds(pl.multiple_of(block * size, size), size)
        return pl.ds(pl.multiple_of(block * size + piece * half, half), half)

    def piece_of(piece):
        return pl.ds(piece * half, half)

    barrier = pltpu.get_barrier_semaphore()
    for step in range(1, 4):
        pl.semaphore_signal(
            barrier, inc=1, device_id=(team, lax.rem(me + step, 4)), device_id_type=MESH
        )
    for step in range(1, teams):
        pl.semaphore_signal(
            barrier, inc=1, device_id=(lax.rem(team + step, teams), me), device_id_type=MESH
        )
    pl.semaphore_wait(barrier, teams + 2)

    def down_outer(slot, piece, block):
        return move(
            part.at[rows_of(block, piece), :],
            outer_down.at[slot, piece_of(piece), :],
            down_send.at[slot, piece],
            down_outer_recv.at[slot, piece],
            ahead,
        )

    def down_inner(slot, piece, send, peer):
        return move(
            block_part.at[send, piece_of(piece), :],
            inner_down.at[slot, piece_of(piece), :],
            down_send.at[send, piece],
            down_inner_recv.at[slot, piece],
            peer,
        )

    @pl.when(is_end)
    def _():
        for piece in range(PIECES):
            down_outer(1, piece, me + inward * 3).start()
        for piece in range(PIECES):
            down_outer(0, piece, me + inward * 2).start()

    def part_load(slot, block):
        return pltpu.make_async_copy(part.at[rows_of(block), :], block_part.at[slot], part_sem.at[slot])

    @pl.when(in_middle)
    def _():
        part_load(0, ahead).start()
        part_load(1, ahead + inward).start()
        part_load(3, behind).start()

    part_load(2, me).start()

    def unit_copy(step):
        return move(
            unit_in.at[team],
            unit_in.at[team],
            unit_send.at[step],
            unit_recv.at[step],
            me,
            lax.rem(team + step, teams),
        )

    def group_copy(step):
        return move(
            group_in.at[team],
            group_in.at[team],
            group_send.at[step],
            group_recv.at[step],
            me,
            lax.rem(team + step, teams),
        )

    act_loads = [
        pltpu.make_async_copy(source, target, act_sem.at[index])
        for index, (source, target) in enumerate(
            (
                (query_any, query),
                (keys_any, keys),
                (values_any, values),
                (att_any, att),
                (mixed_any, mixed),
                (summed_any, summed),
            )
        )
    ]
    for load in act_loads:
        load.start()
    unit_in[team] = early_rows[...].astype(bf16)
    for step in range(1, teams):
        unit_copy(step).start()

    loads = [
        pltpu.make_async_copy(source, weights.at[index], load_sem.at[index])
        for index, source in enumerate((weights_any_query, weights_any_key, weights_any_value))
    ]
    load_first = pltpu.make_async_copy(first_any, mine, load_sem.at[3])
    for load in loads:
        load.start()
    load_first.start()

    for load in act_loads:
        load.wait()
    lth[...] = lt_triple[...].astype(bf16)
    heads = query.shape[1] // HEAD_DIM
    length = length_ref[0]
    factor = 1.0 / math.sqrt(HEAD_DIM)
    factors[:3, :] = mags[...] / norms_ref[...]

    def finish(index, head, grad):
        place = slice(head * HEAD_DIM, (head + 1) * HEAD_DIM)
        if index < 2:
            cosines, sines = turning(angles[...])
            grad = grad * cosines - pltpu.roll(grad, HEAD_DIM // 2, 1) * sines
        factors[index + 3 : index + 4, place] = jnp.sum(
            grad * summed[index, :, place].astype(f32), axis=0, keepdims=True
        )
        gz[index, :, place] = (grad * factors[index : index + 1, place]).astype(bf16)

    for head in range(heads):
        place = slice(head * HEAD_DIM, (head + 1) * HEAD_DIM)
        turned_keys = keys[:, place].astype(f32).T.astype(bf16)
        key_sums[...] = jnp.zeros_like(key_sums)
        value_sums[...] = jnp.zeros_like(value_sums)
        for block in range(total // 256):
            reach = (block + 1) * 256
            at = slice(block * 256, reach)
            grad_rows = mixed[at, place]
            rows = query[at, place]
            scores = nt(keys[:reach, place], rows)
            spots = lax.broadcasted_iota(jnp.int32, (reach, 256), 0)
            asking = lax.broadcasted_iota(jnp.int32, (reach, 256), 1) + block * 256
            allowed = (spots <= asking) & (spots < length)
            scores = jnp.where(allowed, scores * factor, mask_fill)
            probs = jnp.exp(scores - lse[head : head + 1, at])
            grad_probs = nt(values[:reach, place], grad_rows)
            centre = jnp.sum(
                (grad_rows.astype(f32) * att[at, place].astype(f32)).T, axis=0, keepdims=True
            )
            raw = (probs * (grad_probs - centre) * factor).astype(bf16)
            value_sums[:reach, :] += nn(probs.astype(bf16), grad_rows)
            key_sums[:reach, :] += nn(raw, rows)
            query_turned[:, at] = nn(turned_keys[:, :reach], raw)
        finish(0, head, query_turned[...].T)
        finish(1, head, key_sums[...])
        finish(2, head, value_sums[...])

    gin = jnp.zeros((total, 3 * RANK), f32)
    for index in range(3):
        gin = gin + nt(gz[index], padded_right(right[index], index, 3, SCALE))
    gin_low = gin.astype(bf16)
    load_first.wait()
    left = nn(gin.T.astype(bf16), mine[...])
    inner_turned = inner[...].astype(f32).T.astype(bf16)
    for index in range(3):
        block = slice(index * RANK, (index + 1) * RANK)
        norms = norms_ref[index : index + 1, :]
        factor_grad = factors[index + 3 : index + 4, :]
        shape = -factor_grad * mags[index : index + 1, :] / (norms * norms * norms)
        shaped = right[index] * shape
        loads[index].wait()
        pieces = nt(split_rows(shaped), weights[index])
        lt = lt_triple[block, :]
        extra = pieces[:RANK] + pieces[RANK:] + SCALE * nn_exact(nt_exact(shaped, right[index]), lt)
        wide[block, :] = (left[block, :] + SCALE * extra).astype(bf16)
        group_in[team, block, :] = (
            SCALE * (nn(inner_turned, gz[index])[block] + fulls[index] * shape)
        ).astype(bf16)
    tail = group_in.shape[1] - 3 * RANK
    group_in[team, 3 * RANK :, :] = jnp.concatenate(
        [factors[3:6, :] / norms_ref[...], jnp.zeros((tail - 3, factors.shape[1]), f32)], axis=0
    ).astype(bf16)
    wide[3 * RANK : 6 * RANK, :] = early[...].astype(bf16)
    wide[6 * RANK :, :] = early_out[...].astype(bf16)
    for step in range(1, teams):
        group_copy(step).start()

    tiles = wide.shape[0] // 16
    parts_of_tile = teams // tiles
    stretch = depth // parts_of_tile

    def tile_of(owner):
        return (
            pl.ds(pl.multiple_of(lax.rem(owner, tiles) * 16, 16), 16),
            pl.ds(pl.multiple_of((owner // tiles) * stretch, stretch), stretch),
        )

    def wide_copy(step):
        owner = lax.rem(team + step, teams)
        across, along = tile_of(owner)
        return move(
            wide.at[across, along],
            wide_in.at[team],
            wide_send.at[step],
            wide_recv.at[step],
            me,
            owner,
        )

    for step in range(1, teams):
        wide_copy(step).start()
    across, along = tile_of(team)
    wide_in[team] = wide[across, along]

    def add_down(send, piece, ref):
        at = piece_of(piece)
        block_part[send, at, :] = (
            block_part[send, at, :].astype(f32) + ref[at, :].astype(f32)
        ).astype(bf16)

    @pl.when(in_middle)
    def _():
        part_load(1, me).wait()
        for piece in range(PIECES):
            down_outer(1, piece, me).wait_recv()
            add_down(1, piece, outer_down.at[1])
            down_inner(1, piece, 1, ahead).start()

    def grad_block(block):
        at = rows_of(block)
        mine[at, :] = (
            nt(gz[0, at, :], weights[0])
            + nt(gz[1, at, :], weights[1])
            + nt(gz[2, at, :], weights[2])
            + nn(
                (
                    SCALE
                    * (
                        nt(gz[0, at, :], padded_right(right[0], 0, 3, 1.0))
                        + nt(gz[1, at, :], padded_right(right[1], 1, 3, 1.0))
                        + nt(gz[2, at, :], padded_right(right[2], 2, 3, 1.0))
                    )
                ).astype(bf16),
                lth[...],
            )
        ).astype(bf16)

    def outer_copy(slot, piece, block):
        return move(
            mine.at[rows_of(block, piece), :],
            outer.at[slot, piece_of(piece), :],
            sum_send.at[slot, piece],
            outer_recv.at[slot, piece],
            ahead,
        )

    def inner_copy(slot, piece, block, send, peer):
        return move(
            mine.at[rows_of(block, piece), :],
            inner_sums.at[slot, piece_of(piece), :],
            sum_send.at[send, piece],
            inner_recv.at[slot, piece],
            peer,
        )

    @pl.loop(0, 4)
    def _(step):
        middle_block = jnp.where(
            step == 0, ahead + inward, jnp.where(step == 1, ahead, jnp.where(step == 2, behind, me))
        )
        grad_block(jnp.where(is_end, me + inward * (3 - step), middle_block))

        @pl.when(is_end & (step == 0))
        def _():
            for piece in range(PIECES):
                outer_copy(2, piece, me + inward * 3).start()

    def add_into(block, piece, ref):
        at = rows_of(block, piece)
        mine[at, :] = (
            mine[at, :].astype(f32) + ref[piece_of(piece), :].astype(f32)
        ).astype(bf16)

    for step in range(1, teams):
        wide_copy(step).wait_recv()
    gathered = jnp.zeros((16, stretch), f32)
    for index in range(teams):
        gathered = gathered + wide_in[index].astype(f32)
    line_in[me] = gathered.astype(bf16)

    def line_copy(step):
        return move(
            line_in.at[me],
            line_in.at[me],
            line_send.at[step],
            line_recv.at[step],
            lax.rem(me + step, 4),
        )

    for step in range(1, 4):
        line_copy(step).start()

    @pl.when(is_end)
    def _():
        for piece in range(PIECES):
            outer_copy(1, piece, ahead + inward).start()

    @pl.when(in_middle)
    def _():
        part_load(0, me).wait()
        part_load(3, me).wait()
        for piece in range(PIECES):
            down_outer(0, piece, me).wait_recv()
            add_down(0, piece, outer_down.at[0])
            down_inner(0, piece, 0, ahead).start()
        for piece in range(PIECES):
            down_inner(1, piece, 0, ahead).wait_recv()
            add_down(3, piece, inner_down.at[1])
            down_inner(0, piece, 3, behind).start()
        for piece in range(PIECES):
            outer_copy(2, piece, me).wait_recv()
            add_into(ahead + inward, piece, outer.at[2])
            inner_copy(1, piece, ahead + inward, 1, ahead).start()

    part_load(2, me).wait()

    for piece in range(PIECES):
        down_inner(0, piece, 0, ahead).wait_recv()

    load_own = [
        pltpu.make_async_copy(source, target, load_sem.at[index])
        for index, (source, target) in enumerate(
            ((middle, input_grad), (cot_own.at[rows_of(me), :], outputs))
        )
    ]
    for load in load_own:
        load.start()
    norm_down = norms_down[...]
    done = block_part[2].astype(f32) + inner_down[0].astype(f32)
    for load in load_own:
        load.wait()
    small[0:1, :] = jnp.sum(outputs[...].astype(f32) * done, axis=0, keepdims=True)
    small[1:2, :] = early_mags[...]
    outputs[...] = (input_grad[...] + done * (mags_down[...] / norm_down)).astype(bf16)
    small_line[me] = small[...]

    def small_copy(step):
        return move(
            small_line.at[me],
            small_line.at[me],
            small_send.at[step],
            small_recv.at[step],
            lax.rem(me + step, 4),
        )

    for step in range(1, 4):
        small_copy(step).start()

    @pl.when(is_end)
    def _():
        for piece in range(PIECES):
            outer_copy(0, piece, ahead).start()

    load_wide = [
        pltpu.make_async_copy(
            w_down.at[:, index * 512 : (index + 1) * 512],
            weights.at[index, : w_down.shape[0], :],
            load_sem.at[index],
        )
        for index in range(3)
    ]
    load_wide.append(
        pltpu.make_async_copy(w_down.at[:1024, 1536:], gz.at[0], load_sem.at[3])
    )
    load_wide.append(
        pltpu.make_async_copy(
            w_down.at[1024:, 1536:], gz.at[1, : w_down.shape[0] - 1024, :], load_sem.at[4]
        )
    )
    for load in load_wide:
        load.start()

    for step in range(1, 4):
        line_copy(step).wait_recv()
    whole[team] = (
        line_in[0].astype(f32)
        + line_in[1].astype(f32)
        + line_in[2].astype(f32)
        + line_in[3].astype(f32)
    ).astype(bf16)

    def whole_copy(step):
        return move(
            whole.at[team],
            whole.at[team],
            whole_send.at[step],
            whole_recv.at[step],
            me,
            lax.rem(team + step, teams),
        )

    for step in range(1, teams):
        whole_copy(step).start()
    for step in range(1, 4):
        small_copy(step).wait_recv()
    small_rows[team] = small_line[0] + small_line[1] + small_line[2] + small_line[3]

    def final_copy(step):
        return move(
            small_rows.at[team],
            small_rows.at[team],
            final_send.at[step],
            final_recv.at[step],
            me,
            lax.rem(team + step, teams),
        )

    for step in range(1, teams):
        final_copy(step).start()

    @pl.when(in_middle)
    def _():
        for piece in range(PIECES):
            inner_copy(1, piece, me, 0, ahead).wait_recv()
            add_into(behind, piece, inner_sums.at[1])
            inner_copy(0, piece, behind, 2, behind).start()
            outer_copy(1, piece, me).wait_recv()
            add_into(ahead, piece, outer.at[1])
            inner_copy(0, piece, ahead, 0, ahead).start()

    for step in range(1, teams):
        final_copy(step).wait_recv()
    sums = jnp.zeros((2, depth), f32)
    for index in range(teams):
        sums = sums + small_rows[index]
    grad_down_mags[...] = sums[0:1] / norm_down
    grad_out_mags[...] = sums[1:2]
    shape = -sums[0:1] * mags_down[...] / (norm_down * norm_down * norm_down)
    shaped = right_down[...] * shape
    right_extra = SCALE * full_down[...] * shape
    for load in load_wide:
        load.wait()
    cut = split_rows(shaped)
    units = w_down.shape[0]
    pieces = (
        nt(cut[:, :512], weights[0, :units, :])
        + nt(cut[:, 512:1024], weights[1, :units, :])
        + nt(cut[:, 1024:1536], weights[2, :units, :])
    )
    last = cut[:, 1536:]
    mixing = nt_exact(shaped, right_down[...])
    lt = lt_down[...]
    extra = pieces[:RANK] + pieces[RANK:] + SCALE * nn_exact(mixing, lt)
    ends = [nt(last, gz[0]), nt(last, gz[1, : units - 1024, :])]
    grad_down_left[:, :1024] = SCALE * (extra[:, :1024] + ends[0][:RANK] + ends[0][RANK:])
    grad_down_left[:, 1024:] = SCALE * (extra[:, 1024:] + ends[1][:RANK] + ends[1][RANK:])

    for step in range(1, teams):
        group_copy(step).wait_recv()
        unit_copy(step).wait_recv()
        whole_copy(step).wait_recv()
    group_total = jnp.zeros(group_in.shape[1:], f32)
    unit_total = jnp.zeros(unit_in.shape[1:], f32)
    for index in range(teams):
        group_total = group_total + group_in[index].astype(f32)
        unit_total = unit_total + unit_in[index].astype(f32)
    for index in range(3):
        grad_qkv_right[index] = group_total[index * RANK : (index + 1) * RANK]
    grad_qkv_mags[...] = group_total[3 * RANK : 3 * RANK + 3]
    for index in range(2):
        grad_mlp_right[index] = unit_total[index * RANK : (index + 1) * RANK]
    grad_down_left[...] += unit_total[2 * RANK : 3 * RANK]
    grad_mlp_mags[...] = unit_total[3 * RANK : 3 * RANK + 2]
    for part_index in range(parts_of_tile):
        along = slice(part_index * stretch, (part_index + 1) * stretch)
        tile = [whole[part_index * tiles + index].astype(f32) for index in range(7)]
        for index in range(3):
            grad_qkv_left[index, :, along] = tile[index]
        for index in range(2):
            grad_mlp_left[index, :, along] = tile[3 + index]
        grad_exit_right[1, :, along] = tile[5] + right_extra[:, along]
        grad_exit_right[0, :, along] = tile[6]
    group = query.shape[1]
    within = min(group, stretch)
    for index in range(group // within):
        spot = me * group + index * within
        grad_out_left[:, index * within : (index + 1) * within] = whole[
            (spot // stretch) * tiles + 7,
            :,
            pl.ds(pl.multiple_of(lax.rem(spot, stretch), within), within),
        ].astype(f32)

    load_end = [
        pltpu.make_async_copy(source, target, load_sem.at[index])
        for index, (source, target) in enumerate(
            ((grad_middle, input_grad), (x_own.at[rows_of(me), :], block_part.at[2]))
        )
    ]
    for load in load_end:
        load.start()
    for load in load_end:
        load.wait()
    gain = row_of(gain_ref)

    for piece in range(PIECES):
        at = rows_of(me, piece)
        spot = piece_of(piece)

        @pl.when(in_middle)
        def _():
            outer_copy(0, piece, me).wait_recv()
            add_into(me, piece, outer.at[0])

        inner_copy(0, piece, me, 0, ahead).wait_recv()
        grad = mine[at, :].astype(f32) + inner_sums[0, spot, :].astype(f32)
        rows = block_part[2, spot, :].astype(f32)
        inverse = lax.rsqrt(jnp.mean(rows * rows, axis=-1, keepdims=True) + norm_eps)
        scaled = grad * gain
        input_grad[spot, :] = (
            input_grad[spot, :]
            + inverse * scaled
            - rows
            * (inverse * inverse * inverse)
            * jnp.mean(rows * scaled, axis=-1, keepdims=True)
        )

    @pl.when(in_middle)
    def _():
        for piece in range(PIECES):
            for send in (0, 1, 3):
                down_inner(0, piece, send, ahead).wait_send()
            for send in range(3):
                inner_copy(0, piece, me, send, ahead).wait_send()

    @pl.when(is_end)
    def _():
        for piece in range(PIECES):
            for slot in range(2):
                down_outer(slot, piece, me).wait_send()
            for slot in range(3):
                outer_copy(slot, piece, me).wait_send()

    for step in range(1, 4):
        line_copy(step).wait_send()
        small_copy(step).wait_send()
    for step in range(1, teams):
        unit_copy(step).wait_send()
        group_copy(step).wait_send()
        wide_copy(step).wait_send()
        whole_copy(step).wait_send()
        final_copy(step).wait_send()


def call(kernel, outs, ins, specs=None, out_specs=None, scratch=(), flops=0, moved=0, collective=None):
    extra = {} if collective is None else {"collective_id": collective, "has_side_effects": True}
    return pl.pallas_call(
        kernel,
        out_shape=[jax.ShapeDtypeStruct(shape, kind) for shape, kind in outs],
        in_specs=specs or [VMEM] * len(ins),
        out_specs=out_specs or [VMEM] * len(outs),
        scratch_shapes=list(scratch),
        cost_estimate=pl.CostEstimate(flops=flops, bytes_accessed=moved, transcendentals=0),
        compiler_params=pltpu.CompilerParams(vmem_limit_bytes=LIMIT, **extra),
    )(*ins)


def rope_table(length, width):
    half = width // 2
    freqs = np.float32(rope_base) ** (-(np.arange(half, dtype=np.float32) * 2.0) / width)
    angles = np.arange(length, dtype=np.float32)[:, None] * freqs[None, :].astype(np.float32)
    return np.concatenate([np.cos(angles), np.sin(angles)], axis=1).astype(np.float32)


def local(
    inputs,
    cotangent,
    lengths,
    gain_attn,
    gain_mlp,
    w_query,
    w_key,
    w_value,
    w_out,
    w_gate,
    w_up,
    w_down,
    qkv_left,
    qkv_right,
    qkv_mags,
    mlp_left,
    mlp_right,
    mlp_mags,
    out_left,
    down_left,
    exit_right,
    out_mags,
    down_mags,
):
    count = lax.axis_size("heads")
    teams = lax.axis_size("rows")
    total, depth = inputs.shape
    share = total // count
    group = w_query.shape[1]
    units = w_gate.shape[1]
    heads = group // HEAD_DIM
    deep = group // teams
    lt_qkv = jnp.transpose(qkv_left, (0, 2, 1)).reshape(3 * RANK, depth)
    lt_mlp = jnp.transpose(mlp_left, (0, 2, 1)).reshape(2 * RANK, depth)
    angles = jnp.asarray(rope_table(total, HEAD_DIM))
    out_mag, down_mag = out_mags.reshape(1, depth), down_mags.reshape(1, depth)
    bits = teams.bit_length() - 1
    assert teams == 1 << bits
    slots = 3 * (2 * (2 ** (bits - 1) - 1) + 2 ** (bits - 1))

    (
        first,
        query,
        keys,
        values,
        att,
        qkv_summed,
        w_full,
        lse,
        qkv_inner,
        qkv_norms,
        qkv_full,
        gathered,
        middle,
        second,
        out_summed,
        out_inner,
        full_out,
        lt_out,
        exit_norms,
        full_down,
        mlp_norms,
        mlp_full,
        norm_stats,
    ) = call(
        functools.partial(attention_forward_kernel, count, teams),
        [
            ((total, depth), bf16),
            ((total, group), bf16),
            ((total, group), bf16),
            ((total, group), bf16),
            ((total, group), bf16),
            ((3, total, group), bf16),
            ((depth, depth), bf16),
            ((heads, total), f32),
            ((total, 3 * RANK), bf16),
            ((3, group), f32),
            ((3, RANK, group), f32),
            ((count, share, group), bf16),
            ((share, depth), f32),
            ((share, depth), bf16),
            ((share, depth), bf16),
            ((share, RANK), f32),
            ((RANK, depth), f32),
            ((RANK, depth), f32),
            ((2, depth), f32),
            ((RANK, depth), f32),
            ((2, units), f32),
            ((2, RANK, units), f32),
            ((2, 3 * count * group + 2 * count * units + 2 * depth), f32),
        ],
        (
            lengths,
            gain_attn,
            lt_qkv,
            qkv_right,
            qkv_mags,
            angles,
            out_left.T,
            down_left.T,
            exit_right,
            out_mag,
            down_mag,
            gain_mlp,
            lt_mlp,
            mlp_right,
            mlp_mags,
            inputs,
            w_query,
            w_key,
            w_value,
            w_out,
            w_down,
            w_gate,
            w_up,
        ),
        specs=[SMEM] + [VMEM] * 14 + [ANY] * 8,
        out_specs=[ANY] * 7 + [VMEM] * 16,
        scratch=(
            pltpu.VMEM((total + 2 * RANK, depth), bf16),
            pltpu.VMEM((3, depth, group), bf16),
            pltpu.VMEM((total, group), bf16),
            pltpu.VMEM((total, group), bf16),
            pltpu.VMEM((total, group), bf16),
            pltpu.VMEM((total, group), bf16),
            pltpu.VMEM((3, total, group), bf16),
            pltpu.VMEM((count, teams, deep, depth), bf16),
            pltpu.VMEM((units, depth), bf16),
            pltpu.VMEM((2, depth, units), bf16),
            pltpu.VMEM((share, depth), bf16),
            pltpu.VMEM((share + 2 * RANK, depth), bf16),
            pltpu.VMEM((count, RANK, group), f32),
            pltpu.VMEM((count, 2, depth), f32),
            pltpu.VMEM((count, RANK, depth), bf16),
            pltpu.VMEM((count, 8, depth), f32),
            pltpu.SemaphoreType.DMA((8 + teams,)),
            pltpu.SemaphoreType.DMA((6 + count * teams,)),
            pltpu.SemaphoreType.DMA((heads, count)),
            pltpu.SemaphoreType.DMA((heads, count)),
            pltpu.SemaphoreType.DMA((count,)),
            pltpu.SemaphoreType.DMA((count,)),
            pltpu.SemaphoreType.DMA((slots,)),
            pltpu.SemaphoreType.DMA((slots,)),
            pltpu.SemaphoreType.DMA((4, count)),
            pltpu.SemaphoreType.DMA((4, count)),
        ),
        flops=6 * total * depth * group + 4 * total * total * group,
        moved=2 * (2 * total * depth + 3 * depth * group + 8 * total * group),
        collective=0,
    )
    assert count == 4
    (
        part,
        early,
        early_rows,
        grad_middle,
        mixed,
        early_out,
        early_mags,
    ) = call(
        feed_forward_kernel,
        [
            ((total, depth), bf16),
            ((3 * RANK, depth), f32),
            ((4 * RANK, units), f32),
            ((share, depth), f32),
            ((count, share, group), bf16),
            ((2 * RANK, depth), f32),
            ((1, depth), f32),
        ],
        (
            second,
            cotangent,
            w_gate,
            w_up,
            w_down,
            lt_mlp,
            down_left.T,
            mlp_right,
            mlp_mags,
            exit_right,
            down_mag,
            exit_norms,
            mlp_norms,
            mlp_full,
            out_mag,
            gain_mlp,
            out_inner,
            lt_out,
            full_out,
            middle,
            out_summed,
            gathered,
            w_full,
        ),
        specs=[ANY] * 5 + [VMEM] * 14 + [ANY] * 4,
        out_specs=[ANY] + [VMEM] * 6,
        scratch=(
            pltpu.VMEM((share, depth), f32),
            pltpu.VMEM((share + 2 * RANK, depth), bf16),
            pltpu.VMEM((2 * RANK, depth), f32),
            pltpu.VMEM((2 * RANK, depth), bf16),
            pltpu.VMEM((RANK, units), bf16),
            pltpu.VMEM((2, units), f32),
            pltpu.VMEM((depth, units), bf16),
            pltpu.VMEM((depth, units), bf16),
            pltpu.VMEM((units, depth), bf16),
            pltpu.VMEM((count, share, depth), bf16),
            pltpu.VMEM((2, share, depth), bf16),
            pltpu.VMEM((share, depth), bf16),
            pltpu.VMEM((count, share, depth), bf16),
            pltpu.VMEM((count, share, depth), bf16),
            pltpu.VMEM((3, share, depth), bf16),
            pltpu.VMEM((2, share, depth), bf16),
            pltpu.VMEM((share, depth), bf16),
            pltpu.SemaphoreType.DMA((3,)),
            pltpu.SemaphoreType.DMA((2,)),
            pltpu.SemaphoreType.DMA((4,)),
            pltpu.SemaphoreType.DMA((5, PIECES)),
            pltpu.SemaphoreType.DMA((4, PIECES)),
            pltpu.SemaphoreType.DMA((3, PIECES)),
            pltpu.SemaphoreType.DMA((3, PIECES)),
            pltpu.SemaphoreType.DMA((2, PIECES)),
            pltpu.SemaphoreType.DMA,
            pltpu.SemaphoreType.DMA,
            pltpu.SemaphoreType.DMA((9,)),
            pltpu.SemaphoreType.DMA,
            pltpu.SemaphoreType.DMA((4,)),
            pltpu.SemaphoreType.DMA((4,)),
        ),
        flops=12 * total * depth * units,
        moved=2 * (3 * depth * units + 4 * total * depth),
        collective=1,
    )
    results = call(
        functools.partial(attention_back_kernel, teams),
        [
            ((share, depth), bf16),
            ((share, depth), f32),
            ((3, RANK, depth), f32),
            ((3, RANK, group), f32),
            ((3, group), f32),
            ((2, RANK, depth), f32),
            ((2, RANK, units), f32),
            ((2, units), f32),
            ((RANK, group), f32),
            ((RANK, units), f32),
            ((2, RANK, depth), f32),
            ((1, depth), f32),
            ((1, depth), f32),
        ],
        (
            lengths,
            query,
            keys,
            values,
            att,
            lse,
            mixed.reshape(total, group),
            qkv_summed,
            qkv_norms,
            qkv_mags,
            qkv_full,
            qkv_inner,
            lt_qkv,
            qkv_right,
            angles,
            gain_attn,
            early,
            early_out,
            early_rows,
            early_mags,
            exit_norms,
            down_mag,
            exit_right,
            full_down,
            down_left.T,
            first,
            part,
            w_query,
            w_key,
            w_value,
            w_down,
            inputs,
            grad_middle,
            middle,
            cotangent,
        ),
        specs=[SMEM] + [ANY] * 4 + [VMEM] + [ANY] * 2 + [VMEM] * 17 + [ANY] * 10,
        scratch=(
            pltpu.VMEM((total, group), bf16),
            pltpu.VMEM((total, group), bf16),
            pltpu.VMEM((total, group), bf16),
            pltpu.VMEM((total, group), bf16),
            pltpu.VMEM((total, group), bf16),
            pltpu.VMEM((3, total, group), bf16),
            pltpu.SemaphoreType.DMA((6,)),
            pltpu.VMEM((3 * RANK, depth), bf16),
            pltpu.VMEM((3, total, group), bf16),
            pltpu.VMEM((total, HEAD_DIM), f32),
            pltpu.VMEM((total, HEAD_DIM), f32),
            pltpu.VMEM((HEAD_DIM, total), f32),
            pltpu.VMEM((8, group), f32),
            pltpu.VMEM((3, depth, group), bf16),
            pltpu.VMEM((total, depth), bf16),
            pltpu.VMEM((3, share, depth), bf16),
            pltpu.VMEM((2, share, depth), bf16),
            pltpu.VMEM((2, share, depth), bf16),
            pltpu.VMEM((2, share, depth), bf16),
            pltpu.VMEM((4, share, depth), bf16),
            pltpu.VMEM((8 * RANK, depth), bf16),
            pltpu.VMEM((teams, 16, depth * 8 // teams), bf16),
            pltpu.VMEM((count, 16, depth * 8 // teams), bf16),
            pltpu.VMEM((teams, 16, depth * 8 // teams), bf16),
            pltpu.VMEM((teams, 4 * RANK, group), bf16),
            pltpu.VMEM((teams, 4 * RANK, units), bf16),
            pltpu.VMEM((2, depth), f32),
            pltpu.VMEM((count, 2, depth), f32),
            pltpu.VMEM((teams, 2, depth), f32),
            pltpu.SemaphoreType.DMA((5,)),
            pltpu.SemaphoreType.DMA((4,)),
            pltpu.SemaphoreType.DMA((3, PIECES)),
            pltpu.SemaphoreType.DMA((3, PIECES)),
            pltpu.SemaphoreType.DMA((2, PIECES)),
            pltpu.SemaphoreType.DMA((4, PIECES)),
            pltpu.SemaphoreType.DMA((2, PIECES)),
            pltpu.SemaphoreType.DMA((2, PIECES)),
            pltpu.SemaphoreType.DMA((teams,)),
            pltpu.SemaphoreType.DMA((teams,)),
            pltpu.SemaphoreType.DMA((count,)),
            pltpu.SemaphoreType.DMA((count,)),
            pltpu.SemaphoreType.DMA((teams,)),
            pltpu.SemaphoreType.DMA((teams,)),
            pltpu.SemaphoreType.DMA((teams,)),
            pltpu.SemaphoreType.DMA((teams,)),
            pltpu.SemaphoreType.DMA((teams,)),
            pltpu.SemaphoreType.DMA((teams,)),
            pltpu.SemaphoreType.DMA((count,)),
            pltpu.SemaphoreType.DMA((count,)),
            pltpu.SemaphoreType.DMA((teams,)),
            pltpu.SemaphoreType.DMA((teams,)),
        ),
        flops=6 * total * depth * group + 10 * total * total * group,
        moved=2 * (2 * total * depth + 3 * depth * group + 8 * total * group),
        collective=2,
    )
    (
        outputs,
        input_grad,
        grad_qkv_left,
        grad_qkv_right,
        grad_qkv_mags,
        grad_mlp_left,
        grad_mlp_right,
        grad_mlp_mags,
        grad_out_left,
        grad_down_left,
        grad_exit_right,
        grad_out_mags,
        grad_down_mags,
    ) = results
    results = [*results, norm_stats]

    def hand_over(*refs):
        half = len(results)
        for index in range(half):
            refs[half + index][...] = refs[index][...]

    (
        outputs,
        input_grad,
        grad_qkv_left,
        grad_qkv_right,
        grad_qkv_mags,
        grad_mlp_left,
        grad_mlp_right,
        grad_mlp_mags,
        grad_out_left,
        grad_down_left,
        grad_exit_right,
        grad_out_mags,
        grad_down_mags,
        norm_stats,
    ) = call(
        hand_over,
        [(item.shape, item.dtype) for item in results],
        results,
        moved=2 * share * depth * 6,
    )
    return (
        outputs,
        input_grad,
        jnp.transpose(grad_qkv_left, (0, 2, 1)),
        grad_qkv_right,
        grad_qkv_mags,
        jnp.transpose(grad_mlp_left, (0, 2, 1)),
        grad_mlp_right,
        grad_mlp_mags,
        grad_out_left.T,
        grad_down_left.T,
        grad_exit_right,
        grad_out_mags.reshape(depth),
        grad_down_mags.reshape(depth),
        norm_stats,
    )


def solution(mesh):
    placed = (
        P("rows", None),
        P("rows", None),
        P("rows"),
        P(),
        P(),
        P(None, "heads"),
        P(None, "heads"),
        P(None, "heads"),
        P("heads", None),
        P(None, "heads"),
        P(None, "heads"),
        P("heads", None),
        P(),
        P(None, None, "heads"),
        P(None, "heads"),
        P(),
        P(None, None, "heads"),
        P(None, "heads"),
        P("heads", None),
        P("heads", None),
        P(),
        P(),
        P(),
    )
    return jax.shard_map(
        local,
        mesh=mesh,
        in_specs=placed,
        out_specs=(
            P(("rows", "heads"), None),
            P(("rows", "heads"), None),
            P(),
            P(None, None, "heads"),
            P(None, "heads"),
            P(),
            P(None, None, "heads"),
            P(None, "heads"),
            P("heads", None),
            P("heads", None),
            P(),
            P(),
            P(),
            P(),
        ),
        check_vma=False,
    )
```
